32 devices in a mesh: seq: 2 (over y), rows: 16 (over z, x, core).
Axes of the slice: x: 2, y: 2, z: 4, core: 2. Of those that a mesh axis runs over, the one named last changes fastest.
Arguments:
- hidden: bfloat16 [16, 1024, 384], P('rows', 'seq'), may hold values from -6 to 6
- grad_out: bfloat16 [16, 1024, 384], P('rows', 'seq'), may hold values from -6 to 6
- grad_mask: int32 [16, 1024], P('rows', 'seq'), may hold values from 0 to 1, as said below
- w_query: bfloat16 [384, 384], replicated, may hold values from -0.4375 to 0.4375
- w_key: bfloat16 [384, 384], replicated, may hold values from -0.4375 to 0.4375
- w_value: bfloat16 [384, 384], replicated, may hold values from -0.3125 to 0.3125
- w_output: bfloat16 [384, 384], replicated, may hold values from -1.25 to 1.25
- rel_table: bfloat16 [512, 384], replicated, may hold values from -6 to 6
- w_pos_key: bfloat16 [384, 384], replicated, may hold values from -0.4375 to 0.4375
- w_pos_query: bfloat16 [384, 384], replicated, may hold values from -0.4375 to 0.4375
- attn_biases: bfloat16 [4, 384], replicated, may hold values from -1.796875 to 1.796875
- norm_gains: bfloat16 [2, 384], replicated, may hold values from 0.25 to 1.75
- norm_shifts: bfloat16 [2, 384], replicated, may hold values from -1.796875 to 1.796875
- w_inner: bfloat16 [384, 1536], replicated, may hold values from -0.3125 to 0.3125
- inner_bias: bfloat16 [1536], replicated, may hold values from -1.796875 to 1.796875
- w_outer: bfloat16 [1536, 384], replicated, may hold values from -0.15625 to 0.15625
- outer_bias: bfloat16 [384], replicated, may hold values from -1.796875 to 1.796875
Outputs:
- result: bfloat16 [16, 1024, 384], P('rows', 'seq')
- grad_hidden: bfloat16 [16, 1024, 384], P('rows', 'seq')
- grad_w_query: float32 [384, 384], P('rows')
- grad_w_key: float32 [384, 384], P('rows')
- grad_w_value: float32 [384, 384], P('rows')
- grad_w_output: float32 [384, 384], P('rows')
- grad_rel_table: float32 [512, 384], P(None, 'rows')
- grad_w_pos_key: float32 [384, 384], P('rows')
- grad_w_pos_query: float32 [384, 384], P('rows')
- grad_attn_biases: float32 [4, 384], P(None, 'rows')
- grad_norm_gains: float32 [2, 384], P(None, 'rows')
- grad_norm_shifts: float32 [2, 384], P(None, 'rows')
- grad_w_inner: float32 [384, 1536], P('rows')
- grad_inner_bias: float32 [1536], replicated
- grad_w_outer: float32 [1536, 384], P(None, 'rows')
- grad_outer_bias: float32 [384], P('rows')
The draws below stay inside these ranges and needn't reach their ends.
Inputs may be any that keep to these rules, and one draw needn't show every extreme that they name: `grad_mask`: in every sequence a share of the positions is 1, taken as 1024 * p // 100 positions where the sequences' p run evenly from 5 to 40 over the 16 sequences in an order drawn from the seed; the marked positions are spread at random.
All inputs are finite; a program needn't handle non-finite values.
Results may differ from the reference program's by a relative error of at most 0.02.
Values may be sent and summed in bfloat16 or wider, within the bound.
No kernel may reach another device: no remote copies, remote signals or barrier semaphores. Data moves between devices by JAX's collectives and lax.ppermute only.
A program may use at most 128 MiB of HBM per device.

```python
import jax
import jax.numpy as jnp
from jax import lax

D = 384
HEADS = 6
HEAD = 64
FF = 1536
SPAN = 256
BLOCK = 512
SEQS = 16
LENGTH = 1024
NREL = 512


def draw_grad_mask(key, part):
    order_key = jax.random.fold_in(key, 11)
    place_key = jax.random.fold_in(key, 23)
    ranks = jax.random.permutation(order_key, SEQS)
    share = 5 + 35 * ranks // max(SEQS - 1, 1)
    marked = LENGTH * share // 100
    place_keys = jax.random.split(place_key, SEQS)

    def one_order(single):
        return jax.random.permutation(single, LENGTH)
    places = jax.vmap(one_order)(place_keys)
    return (places < marked[:, None]).astype(jnp.int32)


def strengthened(entries, key, source, target, shards_of, factor):
    def block_of(axis_at):
        return (jnp.arange(entries.shape[axis_at]) // (entries.shape[axis_at] // shards_of)).reshape((-1,) + (1,) * (entries.ndim - 1 - axis_at))

    first = jax.random.permutation(key, shards_of)[block_of(target)]
    second = (block_of(target) + shards_of // 2) % shards_of
    return jnp.where((block_of(source) == first) | (block_of(source) == second), factor * entries, entries)


def shard_levels(rng, extent, shards, smallest, high):
    def one(dim, blocks):
        draws = jax.random.uniform(jax.random.fold_in(jax.random.fold_in(rng, 6), dim), (blocks,), jnp.float32, smallest / len(shards), high / len(shards))
        return jnp.repeat(jnp.exp(draws), extent[dim] // blocks).reshape((-1,) + (1,) * (len(extent) - dim - 1))

    factor_of = one(*shards[0])
    for cut in shards[1:]:
        factor_of = factor_of * one(*cut)
    return factor_of


def centred(stream_key, shape, width, bound, cuts=(), held_as=jnp.bfloat16):
    factor_of = shard_levels(stream_key, shape, cuts, -0.22, 0.18) if cuts else 1.0
    entries = jax.random.normal(stream_key, shape, jnp.float32) * width * factor_of
    return jnp.minimum(jnp.maximum(entries, -bound), bound).astype(held_as)


def noise_with(own_key, extent, scale, most, shards, heavy, held_as=jnp.bfloat16):
    values = scale * jax.random.normal(own_key, extent, jnp.float32)
    if shards:
        values = values * shard_levels(own_key, extent, shards, -0.22, 0.18)
    return jnp.clip(strengthened(values, jax.random.fold_in(own_key, 3), *heavy), -most, most).astype(held_as)


def setup_inputs(seed: int = 0) -> dict:
    key_list = jax.random.split(jax.random.key(seed), 18)
    return {
        "hidden": centred(key_list[0], (SEQS, LENGTH, D), 1.0, 6.0, ((0, 16), (1, 2))),
        "grad_out": noise_with(key_list[1], (SEQS, LENGTH, D), 1.0, 6.0, ((0, 16), (1, 2)), (0, 2, 16, 2.0)),
        "grad_mask": draw_grad_mask(jax.random.fold_in(key_list[17], 71), 0),
        "w_query": centred(key_list[3], (D, D), (D // 2) ** -0.5, 0.4375),
        "w_key": centred(key_list[4], (D, D), (D // 2) ** -0.5, 0.4375),
        "w_value": centred(key_list[5], (D, D), D ** -0.5, 0.3125),
        "w_output": centred(key_list[6], (D, D), (D // 16) ** -0.5, 1.25),
        "rel_table": centred(key_list[7], (NREL, D), 1.0, 6.0),
        "w_pos_key": centred(key_list[8], (D, D), (D // 2) ** -0.5, 0.4375),
        "w_pos_query": centred(key_list[9], (D, D), (D // 2) ** -0.5, 0.4375),
        "attn_biases": centred(key_list[10], (4, D), 0.3, 1.796875),
        "norm_gains": jnp.clip(1.0 + 0.15 * jax.random.normal(key_list[11], (2, D), jnp.float32), 0.25, 1.75).astype(jnp.bfloat16),
        "norm_shifts": centred(key_list[12], (2, D), 0.3, 1.796875),
        "w_inner": centred(key_list[13], (D, FF), D ** -0.5, 0.3125),
        "inner_bias": centred(key_list[14], (FF,), 0.3, 1.796875),
        "w_outer": centred(key_list[15], (FF, D), FF ** -0.5, 0.15625),
        "outer_bias": centred(key_list[16], (D,), 0.3, 1.796875),
    }


@jax.custom_vjp
def low(v):
    return lax.optimization_barrier(v.astype(jnp.bfloat16)).astype(jnp.float32)

@jax.custom_vjp
def low_back(v):
    return v

def low_keep(v):
    return (low(v), None)

def low_pass(kept, grad):
    return (grad,)

def back_keep(v):
    return (v, None)

def back_low(kept, grad):
    return (low(grad),)
low.defvjp(low_keep, low_pass)
low_back.defvjp(back_keep, back_low)
norm_eps = 1e-07
masked_score = -1e+30
highest = lax.Precision.HIGHEST

def product(left, right):
    return jnp.dot(left, right, precision=highest, preferred_element_type=jnp.float32)

def layer_norm(values, gain, shift):
    centre = values - lax.optimization_barrier(jnp.mean(values, axis=-1, keepdims=True))
    spread = lax.optimization_barrier(jnp.mean(centre * centre, axis=-1, keepdims=True))
    return centre * lax.rsqrt(spread + norm_eps) * gain + shift

def attention(query, keys, values, pos_keys, pos_queries):
    length = query.shape[0]
    blocks = length // BLOCK
    window = BLOCK + 2 * SPAN
    scale = (3.0 * HEAD) ** (-0.5)
    head_query = query.reshape(length, HEADS, HEAD).transpose(1, 0, 2)
    pad_keys = jnp.pad(keys.reshape(length, HEADS, HEAD).transpose(1, 0, 2), ((0, 0), (SPAN, SPAN), (0, 0)))
    pad_values = jnp.pad(values.reshape(length, HEADS, HEAD).transpose(1, 0, 2), ((0, 0), (SPAN, SPAN), (0, 0)))
    table_keys = pos_keys.reshape(2 * SPAN, HEADS, HEAD).transpose(1, 0, 2)
    table_queries = pos_queries.reshape(2 * SPAN, HEADS, HEAD).transpose(1, 0, 2)
    offsets = jnp.arange(window, dtype=jnp.int32)[None, :] - jnp.arange(BLOCK, dtype=jnp.int32)[:, None]
    to_index = jnp.broadcast_to(jnp.clip(2 * SPAN - offsets, 0, 2 * SPAN - 1)[None], (HEADS, BLOCK, window))
    from_index = jnp.broadcast_to(jnp.clip(offsets, 0, 2 * SPAN - 1).T[None], (HEADS, window, BLOCK))

    def one_block(number):
        first = number * BLOCK
        block_query = lax.dynamic_slice_in_dim(head_query, first, BLOCK, 1)
        block_keys = lax.dynamic_slice_in_dim(pad_keys, first, window, 1)
        block_values = lax.dynamic_slice_in_dim(pad_values, first, window, 1)
        direct = jnp.einsum('hid,hjd->hij', block_query, block_keys, precision=highest)
        to_all = jnp.einsum('hid,hrd->hir', block_query, table_keys, precision=highest)
        from_all = jnp.einsum('hjd,hrd->hjr', block_keys, table_queries, precision=highest)
        to_pos = jnp.take_along_axis(to_all, to_index, axis=2)
        from_pos = jnp.take_along_axis(from_all, from_index, axis=2).transpose(0, 2, 1)
        raw = low_back(direct + to_pos + from_pos)
        target = first - SPAN + jnp.arange(window, dtype=jnp.int32)[None, :]
        valid = (offsets >= 1) & (offsets <= 2 * SPAN) & (target >= 0) & (target < length)
        scores = jnp.where(valid[None], raw * scale, masked_score)
        largest = lax.optimization_barrier(jnp.max(scores, axis=2, keepdims=True))
        weights = jnp.exp(scores - largest)
        probs = weights / lax.optimization_barrier(jnp.sum(weights, axis=2, keepdims=True))
        return jnp.einsum('hij,hjd->hid', low(probs), block_values, precision=highest)
    context = lax.map(jax.checkpoint(one_block), jnp.arange(blocks, dtype=jnp.int32))
    return context.transpose(0, 2, 1, 3).reshape(length, HEADS * HEAD)

def layer(x, w_query, w_key, w_value, w_output, rel_table, w_pos_key, w_pos_query, attn_biases, norm_gains, norm_shifts, w_inner, inner_bias, w_outer, outer_bias):
    query = low(low_back(product(x, w_query) + attn_biases[0]))
    keys = low(low_back(product(x, w_key)))
    values = low(low_back(product(x, w_value) + attn_biases[1]))
    pos_keys = low(product(rel_table, w_pos_key))
    pos_queries = low(product(rel_table, w_pos_query) + attn_biases[2])
    context = low(low_back(attention(query, keys, values, pos_keys, pos_queries)))
    attended = low_back(product(context, w_output) + attn_biases[3])
    normed = layer_norm(x + attended, norm_gains[0], norm_shifts[0])
    inner = low_back(product(low(normed), w_inner) + inner_bias)
    active = low(jax.nn.gelu(inner, approximate=False))
    outer = low_back(product(active, w_outer) + outer_bias)
    return layer_norm(normed + outer, norm_gains[1], norm_shifts[1])

def reference(hidden, grad_out, grad_mask, w_query, w_key, w_value, w_output, rel_table, w_pos_key, w_pos_query, attn_biases, norm_gains, norm_shifts, w_inner, inner_bias, w_outer, outer_bias):
    weights = tuple((item.astype(jnp.float32) for item in (w_query, w_key, w_value, w_output, rel_table, w_pos_key, w_pos_query, attn_biases, norm_gains, norm_shifts, w_inner, inner_bias, w_outer, outer_bias)))

    def one_sequence(totals, pieces):
        sequence, cotangent, marks = pieces
        output, pullback = jax.vjp(layer, sequence.astype(jnp.float32), *weights)
        grads = pullback(cotangent.astype(jnp.float32) * marks.astype(jnp.float32)[:, None])
        totals = tuple((total + grad for total, grad in zip(totals, grads[1:])))
        return (totals, (output.astype(jnp.bfloat16), grads[0].astype(jnp.bfloat16)))
    start = tuple((jnp.zeros(item.shape, jnp.float32) for item in weights))
    totals, outputs = lax.scan(one_sequence, start, (hidden, grad_out, grad_mask))
    return (outputs[0], outputs[1], totals[0], totals[1], totals[2], totals[3], totals[4], totals[5], totals[6], totals[7], totals[8], totals[9], totals[10], totals[11], totals[12], totals[13])
```

```python
from functools import partial
import math

import jax
import jax.numpy as jnp
import numpy as np
from jax import lax
from jax.experimental import pallas as pl
from jax.experimental.pallas import tpu as pltpu
from jax.sharding import PartitionSpec as P

HEADS = 6
PAIRS = HEADS // 2
TILE = 128
norm_eps = 1e-07
masked_score = -1e30
f32 = jnp.float32
bf16 = jnp.bfloat16
MiB = 1 << 20


def nn(left, right):
    return lax.dot_general(left, right, (((1,), (0,)), ((), ())), preferred_element_type=f32)


def nt(left, right):
    return lax.dot_general(left, right, (((1,), (1,)), ((), ())), preferred_element_type=f32)


def iota(shape, axis):
    return lax.broadcasted_iota(jnp.int32, shape, axis)


def where_bf16(mask, value):
    return jnp.where(mask, value.astype(f32), 0.0).astype(bf16)


def skew(block, first):
    return pltpu.roll(block, first, 1, stride=1, stride_axis=0)


def exchange(value, axis, bit):
    count = lax.axis_size(axis)
    return lax.ppermute(value, axis, [(i, i ^ bit) for i in range(count)])


def project_kernel(
    info,
    x,
    x_low,
    x_high,
    w_query,
    w_key,
    w_value,
    rel,
    w_pos_key,
    w_pos_query,
    biases,
    places,
    q_out,
    k_out,
    v_out,
    pk_out,
    pk_rev_out,
    pq_rev_out,
    order_out,
):
    def split(out, first, value):
        rows = value.shape[0]
        for p in range(PAIRS):
            out[p, first : first + rows, :] = value[:, p * TILE : (p + 1) * TILE].astype(bf16)

    bias = biases[...].astype(f32)
    block = x.shape[0]
    span = x_low.shape[0]
    split(q_out, 0, nn(x[...], w_query[...]) + bias[0:1])
    for first, source in ((0, x_low), (span, x), (span + block, x_high)):
        split(k_out, first, nn(source[...], w_key[...]))
        split(v_out, first, nn(source[...], w_value[...]) + bias[1:2])
    count = rel.shape[0]
    pos_keys = nn(rel[...], w_pos_key[...]).astype(bf16)
    pos_queries = (nn(rel[...], w_pos_query[...]) + bias[2:3]).astype(bf16)
    row, col = iota((count, count), 0), iota((count, count), 1)
    flip = jnp.where(col == count - 1 - row, 1.0, 0.0).astype(bf16)
    pick = jnp.where(col == jnp.minimum(count - row, count - 1), 1.0, 0.0).astype(bf16)
    split(pk_out, 0, pos_keys)
    split(pk_rev_out, 0, nn(flip, pos_keys))
    split(pq_rev_out, 0, nn(pick, pos_queries))
    width = order_out.shape[0]
    shard = jnp.bitwise_xor(places[:, 0:1], info[2])
    target = shard * places[0, 2] + places[:, 1:2]
    order_out[...] = jnp.where(iota((width, width), 1) == target, 1.0, 0.0).astype(bf16)


def key_block_range(wb, blocks, tiles):
    low, high = max(0, blocks - 1 - wb), min(blocks - 1, tiles + blocks - 2 - wb)
    return low, high, max(low - 1, 0), min(high, blocks - 2)


def attend_kernel(info, q, k, v, pk_rev, pq_rev, context, probs, from_scr, *, scale):
    row, lane = iota((TILE, TILE), 0), iota((TILE, TILE), 1)
    eye = jnp.where(row == lane, 1.0, 0.0).astype(bf16)
    halves = (lane < TILE // 2, lane >= TILE // 2)
    tiles = q.shape[1] // TILE
    blocks = pk_rev.shape[1] // TILE + 1
    side = blocks // 2
    tables = []
    for h in range(2):
        table = pq_rev[0].astype(f32)
        half = iota((table.shape[0], TILE), 1) // (TILE // 2) == h
        tables.append(jnp.where(half, table, 0.0).astype(bf16))
    for wb in range(tiles + blocks - 1):
        low, high, first, last = key_block_range(wb, blocks, tiles)
        kb = k[0, wb * TILE : (wb + 1) * TILE, :]
        for h in range(2):
            product = nt(kb, tables[h][first * TILE : (last + 1) * TILE])
            turned = {}
            for a in range(first, last + 1):
                turned[a] = skew(product[:, (a - first) * TILE : (a - first + 1) * TILE], 0)
            for e in range(low, high + 1):
                if e == 0:
                    term = turned[0]
                elif e == blocks - 1:
                    term = turned[blocks - 2]
                else:
                    term = jnp.where(lane >= row, turned[e], turned[e - 1])
                it, b = wb - (blocks - 1) + e, blocks - 1 - e
                from_scr[h, it, b] = term.astype(bf16)
    before = jnp.where(info[0] == 0, masked_score, 0.0)
    after = jnp.where(info[0] == info[1] - 1, masked_score, 0.0)
    rate = scale * math.log2(math.e)
    for it in range(tiles):
        qt = q[0, it * TILE : (it + 1) * TILE, :]
        parts = []
        for h in range(2):
            qh = where_bf16(halves[h], qt)
            product = nt(qh, pk_rev[0])
            turned = [
                skew(product[:, b * TILE : (b + 1) * TILE], 1) for b in range(blocks - 1)
            ]
            left = jnp.concatenate([qh, eye], axis=1)
            scores = []
            for b in range(blocks):
                wb = it + b
                right = jnp.concatenate(
                    [k[0, wb * TILE : (wb + 1) * TILE, :], from_scr[h, it, b]], axis=1
                )
                score = nt(left, right)
                if b == 0:
                    score = jnp.where(lane > row, score + turned[0], masked_score)
                elif b == blocks - 1:
                    score = jnp.where(lane <= row, score + turned[b - 1], masked_score)
                else:
                    score = score + jnp.where(lane > row, turned[b], turned[b - 1])
                if wb < side:
                    score = score + before
                if wb >= side + tiles:
                    score = score + after
                scores.append(score)
            largest = scores[0]
            for score in scores[1:]:
                largest = jnp.maximum(largest, score)
            largest = jnp.max(largest, axis=1, keepdims=True)
            weights = [jnp.exp2((score - largest) * rate) for score in scores]
            total = weights[0]
            for weight in weights[1:]:
                total = total + weight
            inverse = 1.0 / jnp.sum(total, axis=1, keepdims=True)
            low_probs = jnp.concatenate([(w * inverse).astype(bf16) for w in weights], axis=1)
            probs[0, h, it] = low_probs
            parts.append(nn(low_probs, v[0, it * TILE : (it + blocks) * TILE, :]))
        context[it * TILE : (it + 1) * TILE, :] = jnp.where(halves[0], parts[0], parts[1]).astype(
            bf16
        )


def attend_back_kernel(
    q,
    k,
    v,
    pk,
    pq_rev,
    d_context,
    context,
    probs,
    dq_out,
    dk_out,
    dv_out,
    dpk_out,
    dpq_out,
    turn_scr,
    dk_scr,
    dv_scr,
    dpk_scr,
    dpq_scr,
    *,
    scale,
):
    row, lane = iota((TILE, TILE), 0), iota((TILE, TILE), 1)
    flip = jnp.where(row + lane == TILE - 1, 1.0, 0.0).astype(bf16)
    row2, lane2 = iota((2 * TILE, 2 * TILE), 0), iota((2 * TILE, 2 * TILE), 1)
    same = (row2 // TILE) == (lane2 // TILE)
    flip2 = jnp.where(
        same & (row2 % TILE + lane2 % TILE == TILE - 1), 1.0, 0.0
    ).astype(bf16)
    halves = (lane < TILE // 2, lane >= TILE // 2)
    row_halves = (row < TILE // 2, row >= TILE // 2)
    tiles = q.shape[1] // TILE
    blocks = pk.shape[1] // TILE + 1
    tables = []
    for h in range(2):
        table = pq_rev[0].astype(f32)
        half = iota((table.shape[0], TILE), 1) // (TILE // 2) == h
        tables.append(jnp.where(half, table, 0.0).astype(bf16))

    def turned_pair(value):
        flat = value.astype(f32).T
        return jnp.concatenate(
            [jnp.where(row_halves[h], flat, 0.0).astype(bf16) for h in range(2)], axis=1
        )

    dk_scr[...] = jnp.zeros_like(dk_scr)
    dv_scr[...] = jnp.zeros_like(dv_scr)
    dpk_scr[...] = jnp.zeros_like(dpk_scr)
    dpq_scr[...] = jnp.zeros_like(dpq_scr)
    for it in range(tiles):
        rows = slice(it * TILE, (it + 1) * TILE)
        window = slice(it * TILE, (it + blocks) * TILE)
        qt, dct = q[0, rows, :], d_context[rows, :]
        overlap = dct.astype(f32) * context[rows, :].astype(f32)
        d_raw, bands, parts, heads_q = [], [], [], []
        for h in range(2):
            d_probs = nt(where_bf16(halves[h], dct), v[0, window, :])
            delta = jnp.sum(jnp.where(halves[h], overlap, 0.0), axis=1, keepdims=True)
            p = probs[0, h, it].astype(f32)
            ds = p * (d_probs - delta) * scale
            ds_low = ds.astype(bf16)
            part = nn(ds_low, k[0, window, :])
            merged = [
                jnp.where(
                    lane > row,
                    ds[:, b * TILE : (b + 1) * TILE],
                    ds[:, (b + 1) * TILE : (b + 2) * TILE],
                ).astype(bf16)
                for b in range(blocks - 1)
            ]
            band = [None] * (blocks - 1)
            for b in range(0, blocks - 1, 2):
                flipped = nn(jnp.concatenate(merged[b : b + 2], axis=1), flip2)
                for c in range(2):
                    band[blocks - 2 - b - c] = skew(
                        flipped[:, c * TILE : (c + 1) * TILE], 1
                    ).astype(bf16)
            band = jnp.concatenate(band, axis=1)
            part = part + nn(band, pk[0])
            d_raw.append(ds_low)
            bands.append(band)
            parts.append(part)
            heads_q.append(where_bf16(halves[h], qt))
        dq_out[rows, :] = jnp.where(halves[0], parts[0], parts[1]).astype(bf16)
        q_turned, dc_turned = turned_pair(qt), turned_pair(dct)
        dpk_scr[...] += nn(q_turned, jnp.concatenate(bands, axis=0))
        dv_scr[:, window] += nn(
            dc_turned, jnp.concatenate([probs[0, 0, it], probs[0, 1, it]], axis=0)
        )
        stacked_q = jnp.concatenate(heads_q, axis=0)
        both = jnp.concatenate(d_raw, axis=0)
        for b in range(blocks):
            wb = it + b
            turned = nt(flip, both[:, b * TILE : (b + 1) * TILE]).astype(bf16)
            turn_scr[it, b] = turned
            dk_scr[wb * TILE : (wb + 1) * TILE, :] += nn(turned, stacked_q)
    for wb in range(tiles + blocks - 1):
        low, high, first, last = key_block_range(wb, blocks, tiles)
        rows = slice(wb * TILE, (wb + 1) * TILE)

        def source(e, h):
            if e < low or e > high:
                return jnp.zeros((TILE, TILE), f32)
            it, b = wb - (blocks - 1) + e, blocks - 1 - e
            return turn_scr[it, b, :, h * TILE : (h + 1) * TILE].astype(f32)

        bands, total = [], None
        for h in range(2):
            pieces = []
            for a in range(first, last + 1):
                merged = jnp.where(lane + row >= TILE - 1, source(a, h), source(a + 1, h))
                pieces.append(skew(merged, 1).astype(bf16))
            band = jnp.concatenate(pieces, axis=1)
            bands.append(band)
            part = nn(band, tables[h][first * TILE : (last + 1) * TILE])
            total = part if total is None else total + part
        dk_low = (dk_scr[rows, :] + total).astype(bf16)
        dk_out[rows, :] = nn(flip, dk_low).astype(bf16)
        k_turned = nn(k[0, rows, :].astype(f32).T.astype(bf16), flip)
        k_turned = jnp.concatenate(
            [jnp.where(row_halves[h], k_turned, 0.0).astype(bf16) for h in range(2)], axis=1
        )
        dpq_scr[:, first * TILE : (last + 1) * TILE] += nn(
            k_turned, jnp.concatenate(bands, axis=0)
        )
        dv_out[rows, :] = dv_scr[:, rows].T.astype(bf16)
    dpk_out[...] = dpk_scr[...].astype(bf16)
    dpq_out[...] = dpq_scr[...].astype(bf16)


def norm_parts(value):
    centre = value - jnp.mean(value, axis=1, keepdims=True)
    rate = lax.rsqrt(jnp.mean(centre * centre, axis=1, keepdims=True) + norm_eps)
    return centre * rate, rate


def norm_back(cotangent, normal, rate):
    return rate * (
        cotangent
        - jnp.mean(cotangent, axis=1, keepdims=True)
        - normal * jnp.mean(cotangent * normal, axis=1, keepdims=True)
    )


def middle_kernel(
    x,
    context,
    grad_out,
    mask,
    w_output,
    biases,
    gains,
    shifts,
    w_inner,
    inner_bias,
    w_outer,
    outer_bias,
    order,
    result,
    d_first_out,
    d_context,
    keep,
    send,
    inner_out,
    rows_out,
    low_scr,
    active_scr,
    d_inner_scr,
    d_outer_scr,
    d_att_scr,
    *,
    step,
):
    tokens, width = x.shape
    units = w_inner.shape[1]
    bias = biases[3:4, :].astype(f32)
    gain_one, gain_two = gains[0:1, :].astype(f32), gains[1:2, :].astype(f32)
    shift_one, shift_two = shifts[0:1, :].astype(f32), shifts[1:2, :].astype(f32)
    in_bias, out_bias = inner_bias[...].astype(f32), outer_bias[...].astype(f32)
    diagonal = iota((TILE, TILE), 0) == iota((TILE, TILE), 1)
    sums = [jnp.zeros((1, width), f32) for _ in range(6)]

    def add(index, value):
        sums[index] = sums[index] + jnp.sum(value, axis=0, keepdims=True)

    for first in range(0, tokens, step):
        rows = slice(first, first + step)
        attended = nn(context[rows, :], w_output[...]) + bias
        n_one, r_one = norm_parts(x[rows, :].astype(f32) + attended)
        normed = n_one * gain_one + shift_one
        low = normed.astype(bf16)
        low_scr[rows, :] = low
        inner = nn(low, w_inner[...]) + in_bias
        cumulative = 0.5 + 0.5 * lax.erf(inner * math.sqrt(0.5))
        active = (inner * cumulative).astype(bf16)
        active_scr[rows, :] = active
        slope = cumulative + inner * jnp.exp(-0.5 * inner * inner) * (1.0 / math.sqrt(2 * math.pi))
        outer = nn(active, w_outer[...]) + out_bias
        n_two, r_two = norm_parts(normed + outer)
        result[rows, :] = (n_two * gain_two + shift_two).astype(bf16)
        columns = []
        for part in range(first, first + step, TILE):
            line = mask[0:1, part : part + TILE].astype(f32)
            columns.append(jnp.sum(jnp.where(diagonal, line, 0.0), axis=1, keepdims=True))
        cotangent = grad_out[rows, :].astype(f32) * jnp.concatenate(columns, axis=0)
        add(0, cotangent * n_two)
        add(1, cotangent)
        d_second = norm_back(cotangent * gain_two, n_two, r_two)
        d_outer = d_second.astype(bf16)
        d_outer_scr[rows, :] = d_outer
        add(2, d_outer.astype(f32))
        d_inner = (nt(d_outer, w_outer[...]) * slope).astype(bf16)
        d_inner_scr[rows, :] = d_inner
        d_normed = d_second + nt(d_inner, w_inner[...])
        add(3, d_normed * n_one)
        add(4, d_normed)
        d_first = norm_back(d_normed * gain_one, n_one, r_one)
        d_first_out[rows, :] = d_first
        d_att = d_first.astype(bf16)
        d_att_scr[rows, :] = d_att
        add(5, d_att.astype(f32))
        d_context[rows, :] = nt(d_att, w_output[...]).astype(bf16)

    half = width // 2

    def put(first, left, right):
        turned = nt(order[...], left).astype(bf16)
        for c in range(0, right.shape[1], width):
            value = nn(turned, right[:, c : c + width]).astype(bf16)
            keep[:, first + c : first + c + width] = value[:half]
            send[:, first + c : first + c + width] = value[half:]

    put(0, low_scr[...], d_inner_scr)
    put(units, d_outer_scr[...], active_scr)
    put(2 * units, context[...], d_att_scr)
    inner_out[...] = nn(jnp.ones((8, tokens), bf16), d_inner_scr[...])
    zero = jnp.zeros((1, width), f32)
    table = [zero, zero, zero, sums[5], sums[3], sums[0], sums[4], sums[1], sums[2]]
    rows_out[...] = jnp.concatenate(table + [zero] * (16 - len(table)), axis=0)


def weight_grad_kernel(
    x, x_low, x_high, rel, w_pos_key, w_pos_query, order, dq, dk, dv, dpk, dpq, rows, keep, send
):
    width = x.shape[1]
    half = width // 2
    span = x_low.shape[0]
    block = x.shape[0]
    count = rel.shape[0]

    def put(first, value):
        value = value.astype(bf16)
        keep[:, first : first + value.shape[1]] = value[:half]
        send[:, first : first + value.shape[1]] = value[half:]

    ord_ = order[...]
    x_low_t = nt(ord_, x_low[...]).astype(bf16)
    x_t = nt(ord_, x[...]).astype(bf16)
    x_high_t = nt(ord_, x_high[...]).astype(bf16)
    put(0, nn(x_t, dq[...]))
    x_all = jnp.concatenate([x_low_t, x_t, x_high_t], axis=1)
    put(width, nn(x_all, dk[...]))
    put(2 * width, nn(x_all, dv[...]))
    rel_t = nt(ord_, rel[...]).astype(bf16)
    put(3 * width, nt(rel_t, dpk[...]))
    row, col = iota((count, count), 0), iota((count, count), 1)
    pick = jnp.where(col == jnp.minimum(count - row, count - 1), 1.0, 0.0).astype(bf16)
    dpq_nat = nn(dpq[...], pick).astype(bf16)
    put(4 * width, nt(rel_t, dpq_nat))
    rel_grad = nn(nn(ord_, w_pos_key[...]).astype(bf16), dpk[...])
    rel_grad = rel_grad + nn(nn(ord_, w_pos_query[...]).astype(bf16), dpq_nat)
    put(5 * width, rel_grad)
    known = rows[...]
    sum_q = nn(jnp.ones((8, block), bf16), dq[...])[0:1]
    sum_v = nn(jnp.ones((8, dv.shape[0]), bf16), dv[...])[0:1]
    sum_p = nt(jnp.ones((8, count), bf16), dpq_nat)[0:1]
    place = iota(known.shape, 0)
    known = jnp.where(place == 0, sum_q, known)
    known = jnp.where(place == 1, sum_v, known)
    known = jnp.where(place == 2, sum_p, known)
    padded = jnp.concatenate([known, jnp.zeros((TILE - known.shape[0], width), f32)], axis=0)
    put(5 * width + count, nt(ord_, padded.astype(bf16)))


def input_grad_kernel(dq, dk, dv, d_first, w_query, w_key, w_value, own, low, high):
    span = low.shape[0]
    block = own.shape[0]

    def halo(rows):
        return nt(dk[rows, :], w_key[...]) + nt(dv[rows, :], w_value[...])

    low[...] = halo(slice(0, span)).astype(bf16)
    high[...] = halo(slice(span + block, 2 * span + block)).astype(bf16)
    own[...] = halo(slice(span, span + block)) + d_first[...] + nt(dq[...], w_query[...])


def final_kernel(mid, mid_other, rest, rest_other, *outs, width, units, count):
    def whole(own, other, first, size):
        cols = slice(first, first + size)
        return own[:, cols].astype(f32) + other[:, cols].astype(f32)

    (g_q, g_k, g_v, g_o, g_rel, g_pk, g_pq, g_bias, g_gain, g_shift, g_in, g_out, g_ob) = outs
    g_in[...] = whole(mid, mid_other, 0, units)
    g_out[...] = whole(mid, mid_other, units, units).T
    g_o[...] = whole(mid, mid_other, 2 * units, width)
    for i, out in enumerate((g_q, g_k, g_v, g_pk, g_pq)):
        out[...] = whole(rest, rest_other, i * width, width)
    g_rel[...] = whole(rest, rest_other, 5 * width, count).T
    lines = whole(rest, rest_other, 5 * width + count, TILE).T
    g_bias[...] = lines[0:4]
    g_gain[...] = lines[4:6]
    g_shift[...] = lines[6:8]
    g_ob[...] = lines[8:9]


def bit_reversed(value, bits):
    out = 0
    for _ in range(bits):
        out = out * 2 + value % 2
        value //= 2
    return out


def whole_spec(array):
    rank = len(array.shape)
    return pl.BlockSpec(array.shape, lambda *_: (0,) * rank)


smem = pl.BlockSpec(memory_space=pltpu.SMEM)


def local(
    hidden,
    grad_out,
    grad_mask,
    w_query,
    w_key,
    w_value,
    w_output,
    rel_table,
    w_pos_key,
    w_pos_query,
    attn_biases,
    norm_gains,
    norm_shifts,
    w_inner,
    inner_bias,
    w_outer,
    outer_bias,
):
    count, block, width = hidden.shape
    tokens = count * block
    table = rel_table.shape[0]
    span = table // 2
    window = block + 2 * span
    units = w_inner.shape[1]
    head = width // HEADS
    scale = 1.0 / math.sqrt(3.0 * head)
    n_rows, n_seq = lax.axis_size("rows"), lax.axis_size("seq")
    row_bits, seq_bits = n_rows.bit_length() - 1, n_seq.bit_length() - 1
    share = width // n_rows
    tiles, blocks = block // TILE, table // TILE + 1
    me_seq, me_rows = lax.axis_index("seq"), lax.axis_index("rows")
    info = jnp.stack([me_seq, jnp.int32(n_seq), me_rows]).astype(jnp.int32)
    x = hidden.reshape(tokens, width)
    shape = jax.ShapeDtypeStruct

    forward = [(i, i + 1) for i in range(n_seq - 1)]
    backward = [(i + 1, i) for i in range(n_seq - 1)]
    x_low = lax.ppermute(x[block - span :], "seq", forward)
    x_high = lax.ppermute(x[:span], "seq", backward)

    places = np.zeros((width, 4), np.int32)
    for i in range(width):
        places[i] = (bit_reversed(i // share, row_bits), i % share, share, 0)

    q3, k3, v3, pk3, pk_rev3, pq_rev3, order = pl.pallas_call(
        project_kernel,
        out_shape=(
            shape((PAIRS, block, TILE), bf16),
            shape((PAIRS, window, TILE), bf16),
            shape((PAIRS, window, TILE), bf16),
            shape((PAIRS, table, TILE), bf16),
            shape((PAIRS, table, TILE), bf16),
            shape((PAIRS, table, TILE), bf16),
            shape((width, width), bf16),
        ),
        in_specs=[smem] + [pl.BlockSpec()] * 11,
        compiler_params=pltpu.CompilerParams(vmem_limit_bytes=40 * MiB),
        name="project",
    )(
        info,
        x,
        x_low,
        x_high,
        w_query,
        w_key,
        w_value,
        rel_table,
        w_pos_key,
        w_pos_query,
        attn_biases,
        jnp.asarray(places),
    )

    def pair(rows):
        return pl.BlockSpec((1, rows, TILE), lambda p: (p, 0, 0))

    def flat(rows):
        return pl.BlockSpec((rows, TILE), lambda p: (0, p))

    def turned(cols):
        return pl.BlockSpec((TILE, cols), lambda p: (p, 0))

    probs_spec = pl.BlockSpec(
        (1, 2, tiles, TILE, blocks * TILE), lambda p: (p, 0, 0, 0, 0)
    )
    context, probs = pl.pallas_call(
        partial(attend_kernel, scale=scale),
        grid=(PAIRS,),
        out_shape=(
            shape((tokens, width), bf16),
            shape((PAIRS, 2, tiles, TILE, blocks * TILE), bf16),
        ),
        in_specs=[smem, pair(block), pair(window), pair(window), pair(table), pair(table)],
        out_specs=(flat(block), probs_spec),
        scratch_shapes=[pltpu.VMEM((2, tiles, blocks, TILE, TILE), bf16)],
        compiler_params=pltpu.CompilerParams(vmem_limit_bytes=40 * MiB),
        name="attend",
    )(info, q3, k3, v3, pk_rev3, pq_rev3)

    mid_cols = 2 * units + width
    result, d_first, d_context, mid_keep, mid_send, inner_sum, rows = pl.pallas_call(
        partial(middle_kernel, step=256),
        out_shape=(
            shape((tokens, width), bf16),
            shape((tokens, width), f32),
            shape((tokens, width), bf16),
            shape((width // 2, mid_cols), bf16),
            shape((width // 2, mid_cols), bf16),
            shape((8, units), f32),
            shape((16, width), f32),
        ),
        scratch_shapes=[
            pltpu.VMEM((tokens, width), bf16),
            pltpu.VMEM((tokens, units), bf16),
            pltpu.VMEM((tokens, units), bf16),
            pltpu.VMEM((tokens, width), bf16),
            pltpu.VMEM((tokens, width), bf16),
        ],
        compiler_params=pltpu.CompilerParams(vmem_limit_bytes=56 * MiB),
        name="middle",
    )(
        x,
        context,
        grad_out.reshape(tokens, width),
        grad_mask,
        w_output,
        attn_biases,
        norm_gains,
        norm_shifts,
        w_inner,
        inner_bias.reshape(1, units),
        w_outer,
        outer_bias.reshape(1, width),
        order,
    )

    dq, dk, dv, dpk, dpq = pl.pallas_call(
        partial(attend_back_kernel, scale=scale),
        grid=(PAIRS,),
        out_shape=(
            shape((block, width), bf16),
            shape((window, width), bf16),
            shape((window, width), bf16),
            shape((width, table), bf16),
            shape((width, table), bf16),
        ),
        in_specs=[
            pair(block),
            pair(window),
            pair(window),
            pair(table),
            pair(table),
            flat(block),
            flat(block),
            probs_spec,
        ],
        out_specs=(flat(block), flat(window), flat(window), turned(table), turned(table)),
        scratch_shapes=[
            pltpu.VMEM((tiles, blocks, TILE, 2 * TILE), bf16),
            pltpu.VMEM((window, TILE), f32),
            pltpu.VMEM((TILE, window), f32),
            pltpu.VMEM((TILE, table), f32),
            pltpu.VMEM((TILE, table), f32),
        ],
        compiler_params=pltpu.CompilerParams(vmem_limit_bytes=40 * MiB),
        name="attend_back",
    )(q3, k3, v3, pk3, pq_rev3, d_context, context, probs)

    rest_cols = 5 * width + table + TILE
    rest_keep, rest_send = pl.pallas_call(
        weight_grad_kernel,
        out_shape=(
            shape((width // 2, rest_cols), bf16),
            shape((width // 2, rest_cols), bf16),
        ),
        compiler_params=pltpu.CompilerParams(vmem_limit_bytes=40 * MiB),
        name="weight_grad",
    )(x, x_low, x_high, rel_table, w_pos_key, w_pos_query, order, dq, dk, dv, dpk, dpq, rows)

    own, to_prev, to_next = pl.pallas_call(
        input_grad_kernel,
        out_shape=(
            shape((tokens, width), f32),
            shape((span, width), bf16),
            shape((span, width), bf16),
        ),
        compiler_params=pltpu.CompilerParams(vmem_limit_bytes=40 * MiB),
        name="input_grad",
    )(dq, dk, dv, d_first, w_query, w_key, w_value)
    from_next = lax.ppermute(to_prev, "seq", backward)
    from_prev = lax.ppermute(to_next, "seq", forward)
    grad_hidden = jnp.concatenate(
        [
            own[:span] + from_prev.astype(f32),
            own[span : block - span],
            own[block - span :] + from_next.astype(f32),
        ],
        axis=0,
    ) if block > 2 * span else jnp.concatenate(
        [own[:span] + from_prev.astype(f32), own[span:] + from_next.astype(f32)], axis=0
    )

    def scattered(keep, send):
        for step in range(row_bits):
            total = keep + exchange(send, "rows", 1 << step)
            half = total.shape[0] // 2
            if step < row_bits - 1:
                keep, send = total[:half], total[half:]
        for step in range(seq_bits - 1):
            total = total + exchange(total, "seq", 1 << step)
        return total, exchange(total, "seq", 1 << (seq_bits - 1))

    inner_total = inner_sum[0:1]
    for step in range(row_bits):
        inner_total = inner_total + exchange(inner_total, "rows", 1 << step)
    for step in range(seq_bits):
        inner_total = inner_total + exchange(inner_total, "seq", 1 << step)

    mid, mid_other = scattered(mid_keep, mid_send)
    rest, rest_other = scattered(rest_keep, rest_send)
    square = shape((share, width), f32)
    grads = pl.pallas_call(
        partial(final_kernel, width=width, units=units, count=table),
        out_shape=(
            square,
            square,
            square,
            square,
            shape((table, share), f32),
            square,
            square,
            shape((4, share), f32),
            shape((2, share), f32),
            shape((2, share), f32),
            shape((share, units), f32),
            shape((units, share), f32),
            shape((1, share), f32),
        ),
        name="final",
    )(mid, mid_other, rest, rest_other)
    return (
        result.reshape(count, block, width),
        grad_hidden.astype(bf16).reshape(count, block, width),
        *grads[:11],
        inner_total.reshape(units),
        grads[11],
        grads[12].reshape(share),
    )


def solution(mesh):
    in_specs = (
        P("rows", "seq", None),
        P("rows", "seq", None),
        P("rows", "seq"),
    ) + (P(),) * 14
    out_specs = (
        P("rows", "seq", None),
        P("rows", "seq", None),
        P("rows", None),
        P("rows", None),
        P("rows", None),
        P("rows", None),
        P(None, "rows"),
        P("rows", None),
        P("rows", None),
        P(None, "rows"),
        P(None, "rows"),
        P(None, "rows"),
        P("rows", None),
        P(),
        P(None, "rows"),
        P("rows"),
    )
    return jax.shard_map(local, mesh=mesh, in_specs=in_specs, out_specs=out_specs, check_vma=False)
```

```python
from functools import partial
import math

import jax
import jax.numpy as jnp
import numpy as np
from jax import lax
from jax.experimental import pallas as pl
from jax.experimental.pallas import tpu as pltpu
from jax.sharding import PartitionSpec as P

HEADS = 6
PAIRS = HEADS // 2
TILE = 128
norm_eps = 1e-07
masked_score = -1e30
f32 = jnp.float32
bf16 = jnp.bfloat16
MiB = 1 << 20


def nn(left, right):
    return lax.dot_general(left, right, (((1,), (0,)), ((), ())), preferred_element_type=f32)


def nt(left, right):
    return lax.dot_general(left, right, (((1,), (1,)), ((), ())), preferred_element_type=f32)


def iota(shape, axis):
    return lax.broadcasted_iota(jnp.int32, shape, axis)


def where_bf16(mask, value):
    return jnp.where(mask, value.astype(f32), 0.0).astype(bf16)


def skew(block, first):
    return pltpu.roll(block, first, 1, stride=1, stride_axis=0)


def exchange(value, axis, bit):
    count = lax.axis_size(axis)
    return lax.ppermute(value, axis, [(i, i ^ bit) for i in range(count)])


def project_kernel(*refs):
    sources, outs, held, arrived = refs[:9], refs[9:16], refs[16:25], refs[25]
    q_out, k_out, v_out, pk_out, pk_rev_out, pq_rev_out, order_out = outs
    places, x, w_query, w_key, w_value, rel, w_pos_key, w_pos_query, biases = held
    copies = [
        pltpu.make_async_copy(source, target, arrived.at[i])
        for i, (source, target) in enumerate(zip(sources, held))
    ]
    for copy in copies:
        copy.start()

    def split(out, value):
        for p in range(PAIRS):
            out[p] = value[:, p * TILE : (p + 1) * TILE].astype(bf16)

    width = order_out.shape[0]
    copies[0].wait()
    shard = jnp.bitwise_xor(places[:, 0:1], lax.axis_index("rows"))
    target = shard * places[0, 2] + places[:, 1:2]
    order_out[...] = jnp.where(iota((width, width), 1) == target, 1.0, 0.0).astype(bf16)
    for copy in copies[1:]:
        copy.wait()
    bias = biases[...].astype(f32)
    split(q_out, nn(x[...], w_query[...]) + bias[0:1])
    split(k_out, nn(x[...], w_key[...]))
    split(v_out, nn(x[...], w_value[...]) + bias[1:2])
    count = rel.shape[0]
    pos_keys = nn(rel[...], w_pos_key[...]).astype(bf16)
    pos_queries = (nn(rel[...], w_pos_query[...]) + bias[2:3]).astype(bf16)
    row, col = iota((count, count), 0), iota((count, count), 1)
    flip = jnp.where(col == count - 1 - row, 1.0, 0.0).astype(bf16)
    pick = jnp.where(col == jnp.minimum(count - row, count - 1), 1.0, 0.0).astype(bf16)
    split(pk_out, pos_keys)
    split(pk_rev_out, nn(flip, pos_keys))
    split(pq_rev_out, nn(pick, pos_queries))


def key_block_range(wb, blocks, tiles):
    low, high = max(0, blocks - 1 - wb), min(blocks - 1, tiles + blocks - 2 - wb)
    return low, high, max(low - 1, 0), min(high, blocks - 2)


def attend_kernel(
    q,
    k_own,
    v_own,
    pk_rev,
    pq_rev,
    x_low,
    x_high,
    w_key,
    w_value,
    biases,
    context,
    probs,
    k,
    v,
    from_scr,
    *,
    scale,
    n_seq,
):
    def one_pair(p, carry):
        attend_pair(
            p,
            q,
            k_own,
            v_own,
            pk_rev,
            pq_rev,
            x_low,
            x_high,
            w_key,
            w_value,
            biases,
            context,
            probs,
            k,
            v,
            from_scr,
            scale=scale,
            n_seq=n_seq,
        )
        return carry

    lax.fori_loop(0, PAIRS, one_pair, 0)


def attend_pair(
    p,
    q,
    k_own,
    v_own,
    pk_rev,
    pq_rev,
    x_low,
    x_high,
    w_key,
    w_value,
    biases,
    context,
    probs,
    k,
    v,
    from_scr,
    *,
    scale,
    n_seq,
):
    me_seq = lax.axis_index("seq")
    cols = pl.ds(pl.multiple_of(p * TILE, TILE), TILE)
    span, block = x_low.shape[0], k_own.shape[1]
    k[p, span : span + block, :] = k_own[p]
    v[p, span : span + block, :] = v_own[p]
    bias = biases[1:2, cols].astype(f32)
    for first, source in ((0, x_low), (span + block, x_high)):
        k[p, first : first + span, :] = nn(source[...], w_key[:, cols]).astype(bf16)
        v[p, first : first + span, :] = (nn(source[...], w_value[:, cols]) + bias).astype(bf16)
    row, lane = iota((TILE, TILE), 0), iota((TILE, TILE), 1)
    eye = jnp.where(row == lane, 1.0, 0.0).astype(bf16)
    halves = (lane < TILE // 2, lane >= TILE // 2)
    tiles = q.shape[1] // TILE
    blocks = pk_rev.shape[1] // TILE + 1
    side = blocks // 2
    tables = []
    for h in range(2):
        table = pq_rev[p].astype(f32)
        half = iota((table.shape[0], TILE), 1) // (TILE // 2) == h
        tables.append(jnp.where(half, table, 0.0).astype(bf16))
    for wb in range(tiles + blocks - 1):
        low, high, first, last = key_block_range(wb, blocks, tiles)
        kb = k[p, wb * TILE : (wb + 1) * TILE, :]
        for h in range(2):
            product = nt(kb, tables[h][first * TILE : (last + 1) * TILE])
            turned = {}
            for a in range(first, last + 1):
                turned[a] = skew(product[:, (a - first) * TILE : (a - first + 1) * TILE], 0)
            for e in range(low, high + 1):
                if e == 0:
                    term = turned[0]
                elif e == blocks - 1:
                    term = turned[blocks - 2]
                else:
                    term = jnp.where(lane >= row, turned[e], turned[e - 1])
                it, b = wb - (blocks - 1) + e, blocks - 1 - e
                from_scr[h, it, b] = term.astype(bf16)
    before = jnp.where(me_seq == 0, masked_score, 0.0)
    after = jnp.where(me_seq == n_seq - 1, masked_score, 0.0)
    rate = scale * math.log2(math.e)
    for it in range(tiles):
        qt = q[p, it * TILE : (it + 1) * TILE, :]
        parts = []
        for h in range(2):
            qh = where_bf16(halves[h], qt)
            product = nt(qh, pk_rev[p])
            turned = [
                skew(product[:, b * TILE : (b + 1) * TILE], 1) for b in range(blocks - 1)
            ]
            left = jnp.concatenate([qh, eye], axis=1)
            scores = []
            for b in range(blocks):
                wb = it + b
                right = jnp.concatenate(
                    [k[p, wb * TILE : (wb + 1) * TILE, :], from_scr[h, it, b]], axis=1
                )
                score = nt(left, right)
                if b == 0:
                    score = jnp.where(lane > row, score + turned[0], masked_score)
                elif b == blocks - 1:
                    score = jnp.where(lane <= row, score + turned[b - 1], masked_score)
                else:
                    score = score + jnp.where(lane > row, turned[b], turned[b - 1])
                if wb < side:
                    score = score + before
                if wb >= side + tiles:
                    score = score + after
                scores.append(score)
            largest = scores[0]
            for score in scores[1:]:
                largest = jnp.maximum(largest, score)
            largest = jnp.max(largest, axis=1, keepdims=True)
            weights = [jnp.exp2((score - largest) * rate) for score in scores]
            total = weights[0]
            for weight in weights[1:]:
                total = total + weight
            inverse = 1.0 / jnp.sum(total, axis=1, keepdims=True)
            low_probs = jnp.concatenate([(w * inverse).astype(bf16) for w in weights], axis=1)
            probs[p, h, it] = low_probs
            parts.append(nn(low_probs, v[p, it * TILE : (it + blocks) * TILE, :]))
        context[it * TILE : (it + 1) * TILE, cols] = jnp.where(halves[0], parts[0], parts[1]).astype(
            bf16
        )


def attend_back_kernel(
    q,
    k,
    v,
    pk,
    pq_rev,
    d_context,
    context,
    probs,
    dq_out,
    dk_out,
    dv_out,
    dpk_out,
    dpq_out,
    turn_scr,
    dk_scr,
    dv_scr,
    dpk_scr,
    dpq_scr,
    *,
    scale,
    p,
):
    row, lane = iota((TILE, TILE), 0), iota((TILE, TILE), 1)
    flip = jnp.where(row + lane == TILE - 1, 1.0, 0.0).astype(bf16)
    row2, lane2 = iota((2 * TILE, 2 * TILE), 0), iota((2 * TILE, 2 * TILE), 1)
    same = (row2 // TILE) == (lane2 // TILE)
    flip2 = jnp.where(
        same & (row2 % TILE + lane2 % TILE == TILE - 1), 1.0, 0.0
    ).astype(bf16)
    halves = (lane < TILE // 2, lane >= TILE // 2)
    row_halves = (row < TILE // 2, row >= TILE // 2)
    cols = slice(p * TILE, (p + 1) * TILE)
    tiles = q.shape[1] // TILE
    blocks = pk.shape[1] // TILE + 1
    tables = []
    for h in range(2):
        table = pq_rev[p].astype(f32)
        half = iota((table.shape[0], TILE), 1) // (TILE // 2) == h
        tables.append(jnp.where(half, table, 0.0).astype(bf16))

    def turned_pair(value):
        flat = value.astype(f32).T
        return jnp.concatenate(
            [jnp.where(row_halves[h], flat, 0.0).astype(bf16) for h in range(2)], axis=1
        )

    dk_scr[...] = jnp.zeros_like(dk_scr)
    dv_scr[...] = jnp.zeros_like(dv_scr)
    dpk_scr[...] = jnp.zeros_like(dpk_scr)
    dpq_scr[...] = jnp.zeros_like(dpq_scr)
    for it in range(tiles):
        rows = slice(it * TILE, (it + 1) * TILE)
        window = slice(it * TILE, (it + blocks) * TILE)
        qt, dct = q[p, rows, :], d_context[rows, cols]
        overlap = dct.astype(f32) * context[rows, cols].astype(f32)
        d_raw, bands, parts, heads_q = [], [], [], []
        for h in range(2):
            d_probs = nt(where_bf16(halves[h], dct), v[p, window, :])
            delta = jnp.sum(jnp.where(halves[h], overlap, 0.0), axis=1, keepdims=True)
            ds = probs[p, h, it].astype(f32) * (d_probs - delta) * scale
            ds_low = ds.astype(bf16)
            part = nn(ds_low, k[p, window, :])
            merged = [
                jnp.where(
                    lane > row,
                    ds[:, b * TILE : (b + 1) * TILE],
                    ds[:, (b + 1) * TILE : (b + 2) * TILE],
                ).astype(bf16)
                for b in range(blocks - 1)
            ]
            band = [None] * (blocks - 1)
            for b in range(0, blocks - 1, 2):
                flipped = nn(jnp.concatenate(merged[b : b + 2], axis=1), flip2)
                for c in range(2):
                    band[blocks - 2 - b - c] = skew(
                        flipped[:, c * TILE : (c + 1) * TILE], 1
                    ).astype(bf16)
            band = jnp.concatenate(band, axis=1)
            part = part + nn(band, pk[p])
            d_raw.append(ds_low)
            bands.append(band)
            parts.append(part)
            heads_q.append(where_bf16(halves[h], qt))
        dq_out[rows, :] = jnp.where(halves[0], parts[0], parts[1]).astype(bf16)
        q_turned, dc_turned = turned_pair(qt), turned_pair(dct)
        dpk_scr[...] += nn(q_turned, jnp.concatenate(bands, axis=0))
        dv_scr[:, window] += nn(
            dc_turned, jnp.concatenate([probs[p, 0, it], probs[p, 1, it]], axis=0)
        )
        stacked_q = jnp.concatenate(heads_q, axis=0)
        both = jnp.concatenate(d_raw, axis=0)
        for b in range(blocks):
            wb = it + b
            turned = nt(flip, both[:, b * TILE : (b + 1) * TILE]).astype(bf16)
            turn_scr[it, b] = turned
            dk_scr[wb * TILE : (wb + 1) * TILE, :] += nn(turned, stacked_q)
    for wb in range(tiles + blocks - 1):
        low, high, first, last = key_block_range(wb, blocks, tiles)
        rows = slice(wb * TILE, (wb + 1) * TILE)

        def source(e, h):
            if e < low or e > high:
                return jnp.zeros((TILE, TILE), f32)
            it, b = wb - (blocks - 1) + e, blocks - 1 - e
            return turn_scr[it, b, :, h * TILE : (h + 1) * TILE].astype(f32)

        bands, total = [], None
        for h in range(2):
            pieces = []
            for a in range(first, last + 1):
                merged = jnp.where(lane + row >= TILE - 1, source(a, h), source(a + 1, h))
                pieces.append(skew(merged, 1).astype(bf16))
            band = jnp.concatenate(pieces, axis=1)
            bands.append(band)
            part = nn(band, tables[h][first * TILE : (last + 1) * TILE])
            total = part if total is None else total + part
        dk_low = (dk_scr[rows, :] + total).astype(bf16)
        dk_out[rows, :] = nn(flip, dk_low).astype(bf16)
        k_turned = nn(k[p, rows, :].astype(f32).T.astype(bf16), flip)
        k_turned = jnp.concatenate(
            [jnp.where(row_halves[h], k_turned, 0.0).astype(bf16) for h in range(2)], axis=1
        )
        dpq_scr[:, first * TILE : (last + 1) * TILE] += nn(
            k_turned, jnp.concatenate(bands, axis=0)
        )
        dv_out[rows, :] = dv_scr[:, rows].T.astype(bf16)
    dpk_out[...] = dpk_scr[...].astype(bf16)
    dpq_out[...] = dpq_scr[...].astype(bf16)


def norm_parts(value):
    centre = value - jnp.mean(value, axis=1, keepdims=True)
    rate = lax.rsqrt(jnp.mean(centre * centre, axis=1, keepdims=True) + norm_eps)
    return centre * rate, rate


def norm_back(cotangent, normal, rate):
    return rate * (
        cotangent
        - jnp.mean(cotangent, axis=1, keepdims=True)
        - normal * jnp.mean(cotangent * normal, axis=1, keepdims=True)
    )


def middle_kernel(
    x,
    context,
    grad_out,
    mask,
    w_output,
    biases,
    gains,
    shifts,
    w_inner,
    inner_bias,
    w_outer,
    outer_bias,
    order,
    result,
    d_first_out,
    d_context,
    keep,
    send,
    rows_out,
    low_scr,
    active_scr,
    d_inner_scr,
    d_outer_scr,
    d_att_scr,
    *,
    step,
    share,
):
    tokens, width = x.shape
    units = w_inner.shape[1]
    bias = biases[3:4, :].astype(f32)
    gain_one, gain_two = gains[0:1, :].astype(f32), gains[1:2, :].astype(f32)
    shift_one, shift_two = shifts[0:1, :].astype(f32), shifts[1:2, :].astype(f32)
    in_bias = inner_bias[...].astype(f32).reshape(1, units)
    out_bias = outer_bias[...].astype(f32).reshape(1, width)
    diagonal = iota((TILE, TILE), 0) == iota((TILE, TILE), 1)
    sums = [jnp.zeros((1, width), f32) for _ in range(6)]

    def add(index, value):
        sums[index] = sums[index] + jnp.sum(value, axis=0, keepdims=True)

    for first in range(0, tokens, step):
        rows = slice(first, first + step)
        attended = nn(context[rows, :], w_output[...]) + bias
        n_one, r_one = norm_parts(x[rows, :].astype(f32) + attended)
        normed = n_one * gain_one + shift_one
        low = normed.astype(bf16)
        low_scr[rows, :] = low
        inner = nn(low, w_inner[...]) + in_bias
        cumulative = 0.5 + 0.5 * lax.erf(inner * math.sqrt(0.5))
        active = (inner * cumulative).astype(bf16)
        active_scr[rows, :] = active
        slope = cumulative + inner * jnp.exp(-0.5 * inner * inner) * (1.0 / math.sqrt(2 * math.pi))
        outer = nn(active, w_outer[...]) + out_bias
        n_two, r_two = norm_parts(normed + outer)
        result[rows, :] = (n_two * gain_two + shift_two).astype(bf16)
        columns = []
        for part in range(first, first + step, TILE):
            line = mask[0:1, part : part + TILE].astype(f32)
            columns.append(jnp.sum(jnp.where(diagonal, line, 0.0), axis=1, keepdims=True))
        cotangent = grad_out[rows, :].astype(f32) * jnp.concatenate(columns, axis=0)
        add(0, cotangent * n_two)
        add(1, cotangent)
        d_second = norm_back(cotangent * gain_two, n_two, r_two)
        d_outer = d_second.astype(bf16)
        d_outer_scr[rows, :] = d_outer
        add(2, d_outer.astype(f32))
        d_inner = (nt(d_outer, w_outer[...]) * slope).astype(bf16)
        d_inner_scr[rows, :] = d_inner
        d_normed = d_second + nt(d_inner, w_inner[...])
        add(3, d_normed * n_one)
        add(4, d_normed)
        d_first = norm_back(d_normed * gain_one, n_one, r_one)
        d_first_out[rows, :] = d_first
        d_att = d_first.astype(bf16)
        d_att_scr[rows, :] = d_att
        add(5, d_att.astype(f32))
        d_context[rows, :] = nt(d_att, w_output[...]).astype(bf16)

    half = width // 2

    def put(first, left, right):
        turned = nt(order[...], left).astype(bf16)
        for c in range(0, right.shape[1], width):
            value = nn(turned, right[:, c : c + width]).astype(bf16)
            keep[:, first + c : first + c + width] = value[:half]
            send[:, first + c : first + c + width] = value[half:]

    put(0, low_scr[...], d_inner_scr)
    put(units, d_outer_scr[...], active_scr)
    put(2 * units, context[...], d_att_scr)
    line = nn(jnp.ones((8, tokens), bf16), d_inner_scr[...])[0:1]
    lines = [line[:, c : c + TILE] for c in range(0, units, TILE)]
    lines = jnp.concatenate(lines + [jnp.zeros((share - len(lines), TILE), f32)] * (share > len(lines)), axis=0)
    lines = jnp.concatenate([lines] * (half // share), axis=0).astype(bf16)
    keep[:, 2 * units + width :] = lines
    send[:, 2 * units + width :] = lines
    zero = jnp.zeros((1, width), f32)
    table = [zero, zero, zero, sums[5], sums[3], sums[0], sums[4], sums[1], sums[2]]
    rows_out[...] = jnp.concatenate(table + [zero] * (16 - len(table)), axis=0)


def weight_grad_kernel(
    x,
    x_low,
    x_high,
    rel,
    w_pos_key,
    w_pos_query,
    order,
    rows,
    *refs,
):
    backs, (keep, send) = refs[:-2], refs[-2:]
    width = x.shape[1]
    half = width // 2
    block = x.shape[0]
    count = rel.shape[0]

    def put(first, value):
        value = value.astype(bf16)
        keep[:, first : first + value.shape[1]] = value[:half]
        send[:, first : first + value.shape[1]] = value[half:]

    ord_ = order[...]
    x_low_t = nt(ord_, x_low[...]).astype(bf16)
    x_t = nt(ord_, x[...]).astype(bf16)
    x_high_t = nt(ord_, x_high[...]).astype(bf16)
    dq, dk, dv = (
        jnp.concatenate([ref[...] for ref in backs[PAIRS * i : PAIRS * (i + 1)]], axis=1)
        for i in range(3)
    )
    dpk, dpq = (
        jnp.concatenate([ref[...] for ref in backs[PAIRS * i : PAIRS * (i + 1)]], axis=0)
        for i in (3, 4)
    )
    put(0, nn(x_t, dq))
    x_all = jnp.concatenate([x_low_t, x_t, x_high_t], axis=1)
    put(width, nn(x_all, dk))
    put(2 * width, nn(x_all, dv))
    rel_t = nt(ord_, rel[...]).astype(bf16)
    put(3 * width, nt(rel_t, dpk))
    row, col = iota((count, count), 0), iota((count, count), 1)
    pick = jnp.where(col == jnp.minimum(count - row, count - 1), 1.0, 0.0).astype(bf16)
    dpq_nat = nn(dpq, pick).astype(bf16)
    put(4 * width, nt(rel_t, dpq_nat))
    rel_grad = nn(nn(ord_, w_pos_key[...]).astype(bf16), dpk)
    rel_grad = rel_grad + nn(nn(ord_, w_pos_query[...]).astype(bf16), dpq_nat)
    put(5 * width, rel_grad)
    known = rows[...]
    sum_q = nn(jnp.ones((8, block), bf16), dq)[0:1]
    sum_v = nn(jnp.ones((8, dv.shape[0]), bf16), dv)[0:1]
    sum_p = nt(jnp.ones((8, count), bf16), dpq_nat)[0:1]
    place = iota(known.shape, 0)
    known = jnp.where(place == 0, sum_q, known)
    known = jnp.where(place == 1, sum_v, known)
    known = jnp.where(place == 2, sum_p, known)
    padded = jnp.concatenate([known, jnp.zeros((TILE - known.shape[0], width), f32)], axis=0)
    put(5 * width + count, nt(ord_, padded.astype(bf16)))


def input_grad_kernel(
    dq0, dq1, dq2, dk0, dk1, dk2, dv0, dv1, dv2, d_first, w_query, w_key, w_value, own, *outs
):
    span = outs[0].shape[0]
    block = own.shape[0]

    def joined(refs, rows):
        return jnp.concatenate([ref[rows, :] for ref in refs], axis=1)

    def halo(rows):
        return nt(joined((dk0, dk1, dk2), rows), w_key[...]) + nt(
            joined((dv0, dv1, dv2), rows), w_value[...]
        )

    if len(outs) == 1:
        first = pl.multiple_of((1 - lax.axis_index("seq")) * (span + block), TILE)
        outs[0][...] = halo(pl.ds(first, span)).astype(bf16)
    else:
        outs[0][...] = halo(slice(0, span)).astype(bf16)
        outs[1][...] = halo(slice(span + block, 2 * span + block)).astype(bf16)
    dq = jnp.concatenate([dq0[...], dq1[...], dq2[...]], axis=1)
    own[...] = halo(slice(span, span + block)) + d_first[...] + nt(dq, w_query[...])


def final_kernel(
    mid, mid_other, one, one_other, two, two_other, *outs, width, units, count
):
    (g_q, g_k, g_v, g_o, g_rel, g_pk, g_pq, g_bias, g_gain, g_shift, g_in, g_out, g_ob, g_ib) = outs

    def middle(first, size):
        cols = slice(first, first + size)
        return mid[:, cols].astype(f32) + mid_other[:, cols].astype(f32)

    g_in[...] = middle(0, units)
    g_out[...] = middle(units, units)
    g_o[...] = middle(2 * units, width)
    g_ib[...] = middle(2 * units + width, TILE)[: units // TILE]
    low = lax.axis_index("seq") % 2 == 0
    mine, other = two[...].astype(f32), two_other[...].astype(f32)
    rest = jnp.concatenate(
        [
            one[...].astype(f32) + one_other[...].astype(f32),
            jnp.where(low, mine, other),
            jnp.where(low, other, mine),
        ],
        axis=1,
    )
    for i, out in enumerate((g_q, g_k, g_v, g_pk, g_pq)):
        out[...] = rest[:, i * width : (i + 1) * width]
    g_rel[...] = rest[:, 5 * width : 5 * width + count]
    lines = rest[:, 5 * width + count :].T
    g_bias[...] = lines[0:4]
    g_gain[...] = lines[4:6]
    g_shift[...] = lines[6:8]
    g_ob[...] = lines[8:9]


def bit_reversed(value, bits):
    out = 0
    for _ in range(bits):
        out = out * 2 + value % 2
        value //= 2
    return out


def local(
    hidden,
    grad_out,
    grad_mask,
    w_query,
    w_key,
    w_value,
    w_output,
    rel_table,
    w_pos_key,
    w_pos_query,
    attn_biases,
    norm_gains,
    norm_shifts,
    w_inner,
    inner_bias,
    w_outer,
    outer_bias,
):
    count, block, width = hidden.shape
    tokens = count * block
    table = rel_table.shape[0]
    span = table // 2
    window = block + 2 * span
    units = w_inner.shape[1]
    head = width // HEADS
    scale = 1.0 / math.sqrt(3.0 * head)
    n_rows, n_seq = lax.axis_size("rows"), lax.axis_size("seq")
    row_bits, seq_bits = n_rows.bit_length() - 1, n_seq.bit_length() - 1
    share = width // n_rows
    tiles, blocks = block // TILE, table // TILE + 1
    me_seq = lax.axis_index("seq")
    x = hidden.reshape(tokens, width)
    shape = jax.ShapeDtypeStruct

    forward = [(i, i + 1) for i in range(n_seq - 1)]
    backward = [(i + 1, i) for i in range(n_seq - 1)]
    if n_seq == 2:
        start = (1 - me_seq) * (block - span)
        x_low = exchange(lax.dynamic_slice_in_dim(x, start, span, axis=0), "seq", 1)
        x_high = x_low
    else:
        x_low = lax.ppermute(x[block - span :], "seq", forward)
        x_high = lax.ppermute(x[:span], "seq", backward)

    places = np.zeros((width, 4), np.int32)
    for i in range(width):
        places[i] = (bit_reversed(i // share, row_bits), i % share, share, 0)

    loaded = (
        jnp.asarray(places),
        x,
        w_query,
        w_key,
        w_value,
        rel_table,
        w_pos_key,
        w_pos_query,
        attn_biases,
    )
    q3, k3, v3, pk3, pk_rev3, pq_rev3, order = pl.pallas_call(
        project_kernel,
        out_shape=(
            shape((PAIRS, block, TILE), bf16),
            shape((PAIRS, block, TILE), bf16),
            shape((PAIRS, block, TILE), bf16),
            shape((PAIRS, table, TILE), bf16),
            shape((PAIRS, table, TILE), bf16),
            shape((PAIRS, table, TILE), bf16),
            shape((width, width), bf16),
        ),
        in_specs=[pl.BlockSpec(memory_space=pltpu.HBM)] * len(loaded),
        scratch_shapes=[pltpu.VMEM(a.shape, a.dtype) for a in loaded]
        + [pltpu.SemaphoreType.DMA((len(loaded),))],
        compiler_params=pltpu.CompilerParams(vmem_limit_bytes=24 * MiB),
        name="project",
    )(*(pltpu.with_memory_space_constraint(a, pltpu.HBM) for a in loaded))
    probs_shape = (PAIRS, 2, tiles, TILE, blocks * TILE)
    context, probs, k3, v3 = pl.pallas_call(
        partial(attend_kernel, scale=scale, n_seq=n_seq),
        out_shape=(
            shape((tokens, width), bf16),
            shape(probs_shape, bf16),
            shape((PAIRS, window, TILE), bf16),
            shape((PAIRS, window, TILE), bf16),
        ),
        scratch_shapes=[pltpu.VMEM((2, tiles, blocks, TILE, TILE), bf16)],
        compiler_params=pltpu.CompilerParams(vmem_limit_bytes=24 * MiB),
        name="attend",
    )(q3, k3, v3, pk_rev3, pq_rev3, x_low, x_high, w_key, w_value, attn_biases)

    mid_cols = 2 * units + width + TILE
    result, d_first, d_context, mid_keep, mid_send, rows = pl.pallas_call(
        partial(middle_kernel, step=256, share=share),
        out_shape=(
            shape((tokens, width), bf16),
            shape((tokens, width), f32),
            shape((tokens, width), bf16),
            shape((width // 2, mid_cols), bf16),
            shape((width // 2, mid_cols), bf16),
            shape((16, width), f32),
        ),
        scratch_shapes=[
            pltpu.VMEM((tokens, width), bf16),
            pltpu.VMEM((tokens, units), bf16),
            pltpu.VMEM((tokens, units), bf16),
            pltpu.VMEM((tokens, width), bf16),
            pltpu.VMEM((tokens, width), bf16),
        ],
        compiler_params=pltpu.CompilerParams(vmem_limit_bytes=32 * MiB),
        name="middle",
    )(
        x,
        context,
        grad_out.reshape(tokens, width),
        grad_mask,
        w_output,
        attn_biases,
        norm_gains,
        norm_shifts,
        w_inner,
        inner_bias,
        w_outer,
        outer_bias,
        order,
    )

    def back(p, d_context):
        return pl.pallas_call(
            partial(attend_back_kernel, scale=scale, p=p),
            out_shape=(
                shape((block, TILE), bf16),
                shape((window, TILE), bf16),
                shape((window, TILE), bf16),
                shape((TILE, table), bf16),
                shape((TILE, table), bf16),
            ),
            scratch_shapes=[
                pltpu.VMEM((tiles, blocks, TILE, 2 * TILE), bf16),
                pltpu.VMEM((window, TILE), f32),
                pltpu.VMEM((TILE, window), f32),
                pltpu.VMEM((TILE, table), f32),
                pltpu.VMEM((TILE, table), f32),
            ],
            compiler_params=pltpu.CompilerParams(vmem_limit_bytes=20 * MiB),
            cost_estimate=pl.CostEstimate(
                flops=7 * 10**9, bytes_accessed=2 * 10**6, transcendentals=0
            ),
            name="attend_back",
        )(q3, k3, v3, pk3, pq_rev3, d_context, context, probs)

    def tied(first, second):
        return lax.optimization_barrier((first, second))

    def halves(total):
        return total[: total.shape[0] // 2], total[total.shape[0] // 2 :]

    received = exchange(mid_send, "rows", 1)
    back0 = back(0, d_context)
    mid_keep, dq0 = tied(mid_keep, back0[0])
    mid = mid_keep + received
    mid, d_context = tied(mid, d_context)
    mid_keep, mid_send = halves(mid)
    received = exchange(mid_send, "rows", 2)
    back1 = back(1, d_context)
    dq1, d_context = tied(back1[0], d_context)
    back2 = back(2, d_context)
    mid_keep, dq2 = tied(mid_keep, back2[0])
    mid = mid_keep + received
    mid, rows = tied(mid, rows)
    dq = (dq0, dq1, dq2)
    dk, dv, dpk, dpq = ((back0[i], back1[i], back2[i]) for i in range(1, 5))

    rest_cols = 5 * width + table + TILE
    rest_keep, rest_send = pl.pallas_call(
        weight_grad_kernel,
        out_shape=(
            shape((width // 2, rest_cols), bf16),
            shape((width // 2, rest_cols), bf16),
        ),
        compiler_params=pltpu.CompilerParams(vmem_limit_bytes=24 * MiB),
        name="weight_grad",
    )(x, x_low, x_high, rel_table, w_pos_key, w_pos_query, order, rows, *dq, *dk, *dv, *dpk, *dpq)

    edge = shape((span, width), bf16)
    own, *edges = pl.pallas_call(
        input_grad_kernel,
        out_shape=(shape((tokens, width), f32),) + (edge,) * (1 if n_seq == 2 else 2),
        compiler_params=pltpu.CompilerParams(vmem_limit_bytes=24 * MiB),
        name="input_grad",
    )(*dq, *dk, *dv, d_first, w_query, w_key, w_value)
    nothing = jnp.zeros((block - span, width), f32)
    if n_seq == 2:
        arrived = exchange(edges[0], "seq", 1).astype(f32)
        own = own + jnp.where(
            me_seq == 0,
            jnp.concatenate([nothing, arrived], axis=0),
            jnp.concatenate([arrived, nothing], axis=0),
        )
    else:
        from_next = lax.ppermute(edges[0], "seq", backward).astype(f32)
        from_prev = lax.ppermute(edges[1], "seq", forward).astype(f32)
        own = (
            own
            + jnp.concatenate([nothing, from_next], axis=0)
            + jnp.concatenate([from_prev, nothing], axis=0)
        )
    grad_hidden = own.astype(bf16)

    def row_steps(total, first):
        for step in range(first, row_bits):
            keep, send = halves(total)
            total = keep + exchange(send, "rows", 1 << step)
        return total

    def seq_sum(total, steps):
        for step in steps:
            total = total + exchange(total, "seq", 1 << step)
        return total

    mid = seq_sum(row_steps(mid, 2), range(seq_bits - 1))
    mid_other = exchange(mid, "seq", 1 << (seq_bits - 1))

    total = rest_keep + exchange(rest_send, "rows", 1)
    cut = rest_cols // 2 // (2 * TILE) * (2 * TILE)
    part = (rest_cols - cut) // 2
    one = seq_sum(row_steps(total[:, :cut], 1), range(seq_bits - 1))
    one_other = exchange(one, "seq", 1 << (seq_bits - 1))
    bit = me_seq % 2
    two = lax.dynamic_slice_in_dim(total, cut + bit * part, part, axis=1) + exchange(
        lax.dynamic_slice_in_dim(total, cut + (1 - bit) * part, part, axis=1), "seq", 1
    )
    two = seq_sum(row_steps(two, 1), range(1, seq_bits))
    two_other = exchange(two, "seq", 1)

    square = shape((share, width), f32)
    grads = pl.pallas_call(
        partial(final_kernel, width=width, units=units, count=table),
        out_shape=(
            square,
            square,
            square,
            square,
            shape((share, table), f32),
            square,
            square,
            shape((4, share), f32),
            shape((2, share), f32),
            shape((2, share), f32),
            shape((share, units), f32),
            shape((share, units), f32),
            shape((1, share), f32),
            shape((units // TILE, TILE), f32),
        ),
        name="final",
    )(mid, mid_other, one, one_other, two, two_other)
    return (
        result.reshape(count, block, width),
        grad_hidden.reshape(count, block, width),
        *grads[:4],
        grads[4].T,
        *grads[5:11],
        grads[13].reshape(units),
        grads[11].T,
        grads[12].reshape(share),
    )


def solution(mesh):
    in_specs = (
        P("rows", "seq", None),
        P("rows", "seq", None),
        P("rows", "seq"),
    ) + (P(),) * 14
    out_specs = (
        P("rows", "seq", None),
        P("rows", "seq", None),
        P("rows", None),
        P("rows", None),
        P("rows", None),
        P("rows", None),
        P(None, "rows"),
        P("rows", None),
        P("rows", None),
        P(None, "rows"),
        P(None, "rows"),
        P(None, "rows"),
        P("rows", None),
        P(),
        P(None, "rows"),
        P("rows"),
    )
    return jax.shard_map(local, mesh=mesh, in_specs=in_specs, out_specs=out_specs, check_vma=False)
```

```python
from functools import partial
import math

import jax
import jax.numpy as jnp
import numpy as np
from jax import lax
from jax.experimental import pallas as pl
from jax.experimental.pallas import tpu as pltpu
from jax.sharding import PartitionSpec as P

HEADS = 6
PAIRS = HEADS // 2
TILE = 128
norm_eps = 1e-07
masked_score = -1e30
f32 = jnp.float32
bf16 = jnp.bfloat16
MiB = 1 << 20


def nn(left, right):
    return lax.dot_general(left, right, (((1,), (0,)), ((), ())), preferred_element_type=f32)


def nt(left, right):
    return lax.dot_general(left, right, (((1,), (1,)), ((), ())), preferred_element_type=f32)


def iota(shape, axis):
    return lax.broadcasted_iota(jnp.int32, shape, axis)


def where_bf16(mask, value):
    return jnp.where(mask, value.astype(f32), 0.0).astype(bf16)


def skew(block, first):
    return pltpu.roll(block, first, 1, stride=1, stride_axis=0)


def column_cut(columns):
    cut = columns // (4 * TILE) * (2 * TILE) + columns % (2 * TILE)
    return cut, (columns - cut) // 2


def store_halves(keep, send, first, value):
    value = value.astype(bf16)
    half = value.shape[0] // 2
    keep[:, first : first + value.shape[1]] = value[:half]
    send[:, first : first + value.shape[1]] = value[half:]


def store_parts(keep, send, first, value):
    cut, part = column_cut(keep.shape[1])
    bit = lax.axis_index("seq") % 2
    value = value.astype(bf16)
    half = value.shape[0] // 2
    ahead = min(max(cut - first, 0), value.shape[1])
    if ahead:
        keep[:, first : first + ahead] = value[:half, :ahead]
        send[:, first : first + ahead] = value[half:, :ahead]
    for c in range(ahead, value.shape[1], TILE):
        which, offset = divmod(first + c - cut, part)
        place = cut + jnp.bitwise_xor(which, bit) * part + offset
        cols = pl.ds(pl.multiple_of(place, TILE), TILE)
        keep[:, cols] = value[:half, c : c + TILE]
        send[:, cols] = value[half:, c : c + TILE]


def exchange(value, axis, bit):
    count = lax.axis_size(axis)
    return lax.ppermute(value, axis, [(i, i ^ bit) for i in range(count)])


def project_kernel(*refs):
    sources, outs, held, arrived = refs[:9], refs[9:20], refs[20:29], refs[29]
    q_out, k_out, v_out, pk_out, pk_rev_out, pq_rev_out, order_out = outs[:7]
    x_turned, rel_turned, w_pk_ordered, w_pq_ordered = outs[7:]
    places, x, w_query, w_key, w_value, rel, w_pos_key, w_pos_query, biases = held
    copies = [
        pltpu.make_async_copy(source, target, arrived.at[i])
        for i, (source, target) in enumerate(zip(sources, held))
    ]
    for copy in copies:
        copy.start()

    def split(out, value):
        for p in range(PAIRS):
            out[p] = value[:, p * TILE : (p + 1) * TILE].astype(bf16)

    width = order_out.shape[0]
    copies[0].wait()
    shard = jnp.bitwise_xor(places[:, 0:1], lax.axis_index("rows"))
    target = shard * places[0, 2] + places[:, 1:2]
    order_out[...] = jnp.where(iota((width, width), 1) == target, 1.0, 0.0).astype(bf16)
    for copy in copies[1:]:
        copy.wait()
    bias = biases[...].astype(f32)
    split(q_out, nn(x[...], w_query[...]) + bias[0:1])
    split(k_out, nn(x[...], w_key[...]))
    split(v_out, nn(x[...], w_value[...]) + bias[1:2])
    count = rel.shape[0]
    pos_keys = nn(rel[...], w_pos_key[...]).astype(bf16)
    pos_queries = (nn(rel[...], w_pos_query[...]) + bias[2:3]).astype(bf16)
    row, col = iota((count, count), 0), iota((count, count), 1)
    flip = jnp.where(col == count - 1 - row, 1.0, 0.0).astype(bf16)
    pick = jnp.where(col == jnp.minimum(count - row, count - 1), 1.0, 0.0).astype(bf16)
    split(pk_out, pos_keys)
    split(pk_rev_out, nn(flip, pos_keys))
    split(pq_rev_out, nn(pick, pos_queries))
    x_turned[...] = nt(order_out[...], x[...]).astype(bf16)
    rel_turned[...] = nt(order_out[...], rel[...]).astype(bf16)
    w_pk_ordered[...] = nn(order_out[...], w_pos_key[...]).astype(bf16)
    w_pq_ordered[...] = nn(order_out[...], w_pos_query[...]).astype(bf16)


def key_block_range(wb, blocks, tiles):
    low, high = max(0, blocks - 1 - wb), min(blocks - 1, tiles + blocks - 2 - wb)
    return low, high, max(low - 1, 0), min(high, blocks - 2)


def attend_kernel(q, k_own, v_own, pk_rev, pq_rev, w_key, w_value, biases, *refs, scale, n_seq):
    edges, refs = refs[:-6], refs[-6:]

    def one_pair(p, carry):
        attend_pair(
            p, q, k_own, v_own, pk_rev, pq_rev, w_key, w_value, biases, edges, *refs, scale, n_seq
        )
        return carry

    lax.fori_loop(0, PAIRS, one_pair, 0)


def attend_pair(
    p,
    q,
    k_own,
    v_own,
    pk_rev,
    pq_rev,
    w_key,
    w_value,
    biases,
    edges,
    context,
    probs,
    k,
    v,
    from_scr,
    score_scr,
    scale,
    n_seq,
):
    me_seq = lax.axis_index("seq")
    cols = pl.ds(pl.multiple_of(p * TILE, TILE), TILE)
    span, block = edges[0].shape[0], k_own.shape[1]
    k[p, span : span + block, :] = k_own[p]
    v[p, span : span + block, :] = v_own[p]
    bias = biases[1:2, cols].astype(f32)
    both = jnp.concatenate([w_key[:, cols], w_value[:, cols]], axis=1)
    sides = ((0, span + block),) if len(edges) == 1 else ((0,), (span + block,))
    for firsts, source in zip(sides, edges):
        product = nn(source[...], both)
        for first in firsts:
            k[p, first : first + span, :] = product[:, :TILE].astype(bf16)
            v[p, first : first + span, :] = (product[:, TILE:] + bias).astype(bf16)
    row, lane = iota((TILE, TILE), 0), iota((TILE, TILE), 1)
    eye = jnp.where(row == lane, 1.0, 0.0).astype(bf16)
    halves = (lane < TILE // 2, lane >= TILE // 2)
    tiles = q.shape[1] // TILE
    blocks = pk_rev.shape[1] // TILE + 1
    side = blocks // 2
    tables = []
    for h in range(2):
        table = pq_rev[p].astype(f32)
        half = iota((table.shape[0], TILE), 1) // (TILE // 2) == h
        tables.append(jnp.where(half, table, 0.0).astype(bf16))
    for wb in range(tiles + blocks - 1):
        low, high, first, last = key_block_range(wb, blocks, tiles)
        kb = k[p, wb * TILE : (wb + 1) * TILE, :]
        span = slice(first * TILE, (last + 1) * TILE)
        product = nt(kb, jnp.concatenate([tables[0][span], tables[1][span]], axis=0))
        for h in range(2):
            turned = {}
            for a in range(first, last + 1):
                at = (h * (last + 1 - first) + a - first) * TILE
                turned[a] = skew(product[:, at : at + TILE], 0)
            for e in range(low, high + 1):
                if e == 0:
                    term = turned[0]
                elif e == blocks - 1:
                    term = turned[blocks - 2]
                else:
                    term = jnp.where(lane >= row, turned[e], turned[e - 1])
                it, b = wb - (blocks - 1) + e, blocks - 1 - e
                from_scr[h, it, b * TILE : (b + 1) * TILE, :] = term.astype(bf16)
    before = jnp.where(me_seq == 0, masked_score, 0.0)
    after = jnp.where(me_seq == n_seq - 1, masked_score, 0.0)
    rate = scale * math.log2(math.e)
    chains = [(it, h) for it in range(tiles) for h in range(2)]
    stacked = jnp.concatenate(
        [where_bf16(halves[h], q[p, it * TILE : (it + 1) * TILE, :]) for it, h in chains], axis=0
    )
    product = nt(stacked, pk_rev[p])
    tops = []
    for n, (it, h) in enumerate(chains):
        rows = slice(n * TILE, (n + 1) * TILE)
        turned = [
            skew(product[rows, b * TILE : (b + 1) * TILE], 1) for b in range(blocks - 1)
        ]
        left = jnp.concatenate([stacked[rows], eye], axis=1)
        right = jnp.concatenate(
            [k[p, it * TILE : (it + blocks) * TILE, :], from_scr[h, it]], axis=1
        )
        content = nt(left, right)
        largest = None
        for b in range(blocks):
            score = content[:, b * TILE : (b + 1) * TILE]
            if b == 0:
                score = jnp.where(lane > row, score + turned[0], masked_score)
            elif b == blocks - 1:
                score = jnp.where(lane <= row, score + turned[b - 1], masked_score)
            else:
                score = score + jnp.where(lane > row, turned[b], turned[b - 1])
            if it + b < side:
                score = score + before
            if it + b >= side + tiles:
                score = score + after
            score_scr[n, :, b * TILE : (b + 1) * TILE] = score
            largest = score if largest is None else jnp.maximum(largest, score)
        tops.append(largest)
    tops = [jnp.max(top, axis=1, keepdims=True) for top in tops]
    totals = []
    for n in range(len(chains)):
        weight = jnp.exp2((score_scr[n] - tops[n]) * rate)
        score_scr[n] = weight
        total = weight[:, :TILE]
        for b in range(1, blocks):
            total = total + weight[:, b * TILE : (b + 1) * TILE]
        totals.append(total)
    inverses = [1.0 / jnp.sum(total, axis=1, keepdims=True) for total in totals]
    for n, (it, h) in enumerate(chains):
        probs[p, h, it] = (score_scr[n] * inverses[n]).astype(bf16)
    for it in range(tiles):
        both = jnp.concatenate([probs[p, 0, it], probs[p, 1, it]], axis=0)
        part = nn(both, v[p, it * TILE : (it + blocks) * TILE, :])
        context[it * TILE : (it + 1) * TILE, cols] = jnp.where(
            halves[0], part[:TILE], part[TILE:]
        ).astype(bf16)


def attend_back_kernel(
    q,
    k,
    v,
    pk,
    pq_rev,
    d_context,
    context,
    probs,
    dq_out,
    dk_out,
    dv_out,
    dpk_out,
    dpq_out,
    ds_scr,
    merged_scr,
    band_scr,
    turn_scr,
    shifted_scr,
    dv_scr,
    *,
    scale,
    p,
):
    row, lane = iota((TILE, TILE), 0), iota((TILE, TILE), 1)
    flip = jnp.where(row + lane == TILE - 1, 1.0, 0.0).astype(bf16)
    row2, lane2 = iota((2 * TILE, 2 * TILE), 0), iota((2 * TILE, 2 * TILE), 1)
    same = (row2 // TILE) == (lane2 // TILE)
    flip2 = jnp.where(
        same & (row2 % TILE + lane2 % TILE == TILE - 1), 1.0, 0.0
    ).astype(bf16)
    halves = (lane < TILE // 2, lane >= TILE // 2)
    row_halves = (row < TILE // 2, row >= TILE // 2)
    cols = slice(p * TILE, (p + 1) * TILE)
    tiles = q.shape[1] // TILE
    blocks = pk.shape[1] // TILE + 1
    keys = tiles + blocks - 1
    pairs = (blocks - 1) // 2

    def part(index):
        return slice(index * TILE, (index + 1) * TILE)

    def window(it):
        return slice(it * TILE, (it + blocks) * TILE)

    def split_rows(value):
        return jnp.concatenate([where_bf16(halves[h], value) for h in range(2)], axis=0)

    def split_turned(value):
        flat = value.astype(f32).T
        return [jnp.where(row_halves[h], flat, 0.0).astype(bf16) for h in range(2)]

    stacked_q = [split_rows(q[p, part(it), :]) for it in range(tiles)]
    for it in range(tiles):
        dct = d_context[part(it), cols]
        overlap = dct.astype(f32) * context[part(it), cols].astype(f32)
        delta = jnp.concatenate(
            [
                jnp.sum(jnp.where(halves[h], overlap, 0.0), axis=1, keepdims=True)
                for h in range(2)
            ],
            axis=0,
        )
        d_probs = nt(split_rows(dct), v[p, window(it), :])
        weights = jnp.concatenate([probs[p, 0, it], probs[p, 1, it]], axis=0)
        ds = weights.astype(f32) * (d_probs - delta) * scale
        ds_scr[it] = ds.astype(bf16)
        for h in range(2):
            for b in range(blocks - 1):
                merged = jnp.where(lane > row, ds[part(h), part(b)], ds[part(h), part(b + 1)])
                at = (it * 2 + h) * pairs + b // 2
                merged_scr[part(at), part(b % 2)] = merged.astype(bf16)
    flipped = nn(merged_scr[...], flip2)
    for it in range(tiles):
        for h in range(2):
            for b in range(blocks - 1):
                at = (it * 2 + h) * pairs + b // 2
                band_scr[part(it * 2 + h), part(blocks - 2 - b)] = skew(
                    flipped[part(at), part(b % 2)], 1
                ).astype(bf16)
    for it in range(tiles):
        for b in range(blocks):
            turn_scr[it, b] = nt(flip, ds_scr[it, :, part(b)]).astype(bf16)
    for it in range(tiles):
        both = slice(2 * it * TILE, 2 * (it + 1) * TILE)
        total = nn(
            jnp.concatenate([ds_scr[it], band_scr[both, :]], axis=1),
            jnp.concatenate([k[p, window(it), :], pk[p]], axis=0),
        )
        dq_out[part(it), :] = jnp.where(halves[0], total[:TILE], total[TILE:]).astype(bf16)
    turned = [split_turned(q[p, part(it), :]) for it in range(tiles)]
    dpk_out[...] = nn(jnp.concatenate(sum(turned, []), axis=1), band_scr[...]).astype(bf16)
    dv_scr[...] = jnp.zeros_like(dv_scr)
    for it in range(tiles):
        dv_scr[:, window(it)] += nn(
            jnp.concatenate(split_turned(d_context[part(it), cols]), axis=1),
            jnp.concatenate([probs[p, 0, it], probs[p, 1, it]], axis=0),
        )

    tables = []
    for h in range(2):
        table = pq_rev[p].astype(f32)
        half = iota((table.shape[0], TILE), 1) // (TILE // 2) == h
        tables.append(jnp.where(half, table, 0.0).astype(bf16))
    for wb in range(keys):
        low, high, first, last = key_block_range(wb, blocks, tiles)

        def source(e, h):
            if e < low or e > high:
                return jnp.zeros((TILE, TILE), f32)
            it, b = wb - (blocks - 1) + e, blocks - 1 - e
            return turn_scr[it, b, :, part(h)].astype(f32)

        for h in range(2):
            for a in range(blocks - 1):
                if first <= a <= last:
                    merged = jnp.where(lane + row >= TILE - 1, source(a, h), source(a + 1, h))
                    shifted_scr[part(2 * wb + h), part(a)] = skew(merged, 1).astype(bf16)
                else:
                    shifted_scr[part(2 * wb + h), part(a)] = jnp.zeros((TILE, TILE), bf16)
    lows = []
    for wb in range(keys):
        low, high, first, last = key_block_range(wb, blocks, tiles)
        left, right = [], []
        for e in range(low, high + 1):
            it, b = wb - (blocks - 1) + e, blocks - 1 - e
            left.append(turn_scr[it, b])
            right.append(stacked_q[it])
        span = slice(first * TILE, (last + 1) * TILE)
        for h in range(2):
            left.append(shifted_scr[part(2 * wb + h), span])
            right.append(tables[h][span])
        total = nn(jnp.concatenate(left, axis=1), jnp.concatenate(right, axis=0))
        lows.append(total.astype(bf16))
    natural = nn(flip, jnp.concatenate(lows, axis=1)).astype(bf16)
    for wb in range(keys):
        dk_out[part(wb), :] = natural[:, part(wb)]
    reverse = nn(flip, jnp.concatenate([k[p, part(wb), :] for wb in range(keys)], axis=1))
    turned = sum([split_turned(reverse[:, part(wb)]) for wb in range(keys)], [])
    dpq_out[...] = nn(jnp.concatenate(turned, axis=1), shifted_scr[...]).astype(bf16)
    for wb in range(keys):
        dv_out[part(wb), :] = dv_scr[:, part(wb)].T.astype(bf16)


def norm_parts(value):
    centre = value - jnp.mean(value, axis=1, keepdims=True)
    rate = lax.rsqrt(jnp.mean(centre * centre, axis=1, keepdims=True) + norm_eps)
    return centre * rate, rate


def norm_back(cotangent, normal, rate):
    return rate * (
        cotangent
        - jnp.mean(cotangent, axis=1, keepdims=True)
        - normal * jnp.mean(cotangent * normal, axis=1, keepdims=True)
    )


def middle_kernel(
    x,
    context,
    grad_out,
    mask,
    w_output,
    biases,
    gains,
    shifts,
    w_inner,
    inner_bias,
    w_outer,
    outer_bias,
    order,
    result,
    d_first_out,
    d_context,
    keep,
    send,
    rows_out,
    low_scr,
    active_scr,
    d_inner_scr,
    d_outer_scr,
    d_att_scr,
    *,
    step,
    share,
):
    tokens, width = x.shape
    units = w_inner.shape[1]
    bias = biases[3:4, :].astype(f32)
    gain_one, gain_two = gains[0:1, :].astype(f32), gains[1:2, :].astype(f32)
    shift_one, shift_two = shifts[0:1, :].astype(f32), shifts[1:2, :].astype(f32)
    in_bias = inner_bias[...].astype(f32).reshape(1, units)
    out_bias = outer_bias[...].astype(f32).reshape(1, width)
    diagonal = iota((TILE, TILE), 0) == iota((TILE, TILE), 1)
    sums = [jnp.zeros((1, width), f32) for _ in range(6)]

    def add(index, value):
        sums[index] = sums[index] + jnp.sum(value, axis=0, keepdims=True)

    parts = [slice(first, first + step) for first in range(0, tokens, step)]
    first_norm, slopes, second = [], [], []
    for rows in parts:
        attended = nn(context[rows, :], w_output[...]) + bias
        n_one, r_one = norm_parts(x[rows, :].astype(f32) + attended)
        normed = n_one * gain_one + shift_one
        low_scr[rows, :] = normed.astype(bf16)
        first_norm.append((n_one, r_one, normed))
    for rows in parts:
        inner = nn(low_scr[rows, :], w_inner[...]) + in_bias
        cumulative = 0.5 + 0.5 * lax.erf(inner * math.sqrt(0.5))
        active_scr[rows, :] = (inner * cumulative).astype(bf16)
        slopes.append(
            cumulative + inner * jnp.exp(-0.5 * inner * inner) * (1.0 / math.sqrt(2 * math.pi))
        )
    for rows, (_, _, normed) in zip(parts, first_norm):
        outer = nn(active_scr[rows, :], w_outer[...]) + out_bias
        n_two, r_two = norm_parts(normed + outer)
        result[rows, :] = (n_two * gain_two + shift_two).astype(bf16)
        columns = []
        for part in range(rows.start, rows.stop, TILE):
            line = mask[0:1, part : part + TILE].astype(f32)
            columns.append(jnp.sum(jnp.where(diagonal, line, 0.0), axis=1, keepdims=True))
        cotangent = grad_out[rows, :].astype(f32) * jnp.concatenate(columns, axis=0)
        add(0, cotangent * n_two)
        add(1, cotangent)
        d_second = norm_back(cotangent * gain_two, n_two, r_two)
        d_outer = d_second.astype(bf16)
        d_outer_scr[rows, :] = d_outer
        add(2, d_outer.astype(f32))
        second.append(d_second)
    for rows, slope in zip(parts, slopes):
        d_inner_scr[rows, :] = (nt(d_outer_scr[rows, :], w_outer[...]) * slope).astype(bf16)
    for rows, d_second, (n_one, r_one, _) in zip(parts, second, first_norm):
        d_normed = d_second + nt(d_inner_scr[rows, :], w_inner[...])
        add(3, d_normed * n_one)
        add(4, d_normed)
        d_first = norm_back(d_normed * gain_one, n_one, r_one)
        d_first_out[rows, :] = d_first
        d_att = d_first.astype(bf16)
        d_att_scr[rows, :] = d_att
        add(5, d_att.astype(f32))
    for rows in parts:
        d_context[rows, :] = nt(d_att_scr[rows, :], w_output[...]).astype(bf16)

    def put(first, left, right):
        turned = nt(order[...], left).astype(bf16)
        for c in range(0, right.shape[1], width):
            store_halves(keep, send, first + c, nn(turned, right[:, c : c + width]))

    put(0, low_scr[...], d_inner_scr)
    put(units, d_outer_scr[...], active_scr)
    line = nn(jnp.ones((8, tokens), bf16), d_inner_scr[...])[0:1]
    lines = [line[:, c : c + TILE] for c in range(0, units, TILE)]
    lines = jnp.concatenate(lines + [jnp.zeros((share - len(lines), TILE), f32)] * (share > len(lines)), axis=0)
    lines = jnp.concatenate([lines] * (width // share), axis=0)
    store_halves(keep, send, 2 * units, lines)
    zero = jnp.zeros((1, width), f32)
    table = [zero, zero, zero, sums[5], sums[3], sums[0], sums[4], sums[1], sums[2]]
    rows_out[...] = jnp.concatenate(table + [zero] * (16 - len(table)), axis=0)


def weight_grad_kernel(
    x_t, rel_t, w_pk_t, w_pq_t, order, rows, context, d_first, *refs, n_seq
):
    edges = refs[: 1 if n_seq == 2 else 2]
    backs, (keep, send) = refs[len(edges) : -2], refs[-2:]
    width, block = x_t.shape
    count = rel_t.shape[1]
    span = count // 2
    put = partial(store_parts, keep, send)

    def joined(index, rows=slice(None), axis=1):
        some = backs[PAIRS * index : PAIRS * (index + 1)]
        return jnp.concatenate([ref[rows, :] for ref in some], axis=axis)

    ord_ = order[...]
    dq = joined(0)
    put(0, nn(x_t[...], dq))
    turned = [nt(ord_, edge[...]).astype(bf16) for edge in edges] + [x_t[...]]
    if n_seq == 2:
        first = pl.multiple_of((1 - lax.axis_index("seq")) * (span + block), TILE)
        places = [pl.ds(first, span)]
    else:
        places = [slice(0, span), slice(span + block, 2 * span + block)]
    places.append(slice(span, span + block))
    left = jnp.concatenate(turned, axis=1)
    dk, dv = (jnp.concatenate([joined(i, r) for r in places], axis=0) for i in (1, 2))
    put(width, nn(left, dk))
    put(2 * width, nn(left, dv))
    context_t = nt(ord_, context[...]).astype(bf16)
    put(5 * width, nn(context_t, d_first[...].astype(bf16)))
    dpk, dpq = joined(3, axis=0), joined(4, axis=0)
    put(3 * width, nt(rel_t[...], dpk))
    row, col = iota((count, count), 0), iota((count, count), 1)
    pick = jnp.where(col == jnp.minimum(count - row, count - 1), 1.0, 0.0).astype(bf16)
    dpq_nat = nn(dpq, pick).astype(bf16)
    put(4 * width, nt(rel_t[...], dpq_nat))
    rel_grad = nn(w_pk_t[...], dpk)
    rel_grad = rel_grad + nn(w_pq_t[...], dpq_nat)
    put(6 * width, rel_grad)
    known = rows[...]
    sum_q = nn(jnp.ones((8, block), bf16), dq)[0:1]
    sum_v = nn(jnp.ones((8, dv.shape[0]), bf16), dv)[0:1]
    sum_p = nt(jnp.ones((8, count), bf16), dpq_nat)[0:1]
    place = iota(known.shape, 0)
    known = jnp.where(place == 0, sum_q, known)
    known = jnp.where(place == 1, sum_v, known)
    known = jnp.where(place == 2, sum_p, known)
    padded = jnp.concatenate([known, jnp.zeros((TILE - known.shape[0], width), f32)], axis=0)
    put(6 * width + count, nt(ord_, padded.astype(bf16)))


def input_grad_kernel(
    dq0, dq1, dq2, dk0, dk1, dk2, dv0, dv1, dv2, d_first, w_query, w_key, w_value, own, *outs
):
    span = outs[0].shape[0]
    block = own.shape[0]

    def joined(refs, rows):
        return jnp.concatenate([ref[rows, :] for ref in refs], axis=1)

    def halo(rows):
        return nt(joined((dk0, dk1, dk2), rows), w_key[...]) + nt(
            joined((dv0, dv1, dv2), rows), w_value[...]
        )

    if len(outs) == 1:
        first = pl.multiple_of((1 - lax.axis_index("seq")) * (span + block), TILE)
        outs[0][...] = halo(pl.ds(first, span)).astype(bf16)
    else:
        outs[0][...] = halo(slice(0, span)).astype(bf16)
        outs[1][...] = halo(slice(span + block, 2 * span + block)).astype(bf16)
    dq = jnp.concatenate([dq0[...], dq1[...], dq2[...]], axis=1)
    own[...] = halo(slice(span, span + block)) + d_first[...] + nt(dq, w_query[...])


def final_kernel(*refs, width, units, count):
    (g_q, g_k, g_v, g_o, g_rel, g_pk, g_pq, g_bias, g_gain, g_shift, g_in, g_out, g_ob, g_ib) = (
        refs[6:]
    )
    low = lax.axis_index("seq") % 2 == 0

    def joined(one, one_other, two, two_other):
        mine, other = two[...].astype(f32), two_other[...].astype(f32)
        return jnp.concatenate(
            [
                one[...].astype(f32) + one_other[...].astype(f32),
                jnp.where(low, mine, other),
                jnp.where(low, other, mine),
            ],
            axis=1,
        )

    mid = refs[0][...].astype(f32) + refs[1][...].astype(f32)
    rest = joined(*refs[2:6])
    g_in[...] = mid[:, :units]
    g_out[...] = mid[:, units : 2 * units]
    g_ib[...] = mid[: units // TILE, 2 * units :]
    for i, out in enumerate((g_q, g_k, g_v, g_pk, g_pq, g_o)):
        out[...] = rest[:, i * width : (i + 1) * width]
    g_rel[...] = rest[:, 6 * width : 6 * width + count]
    lines = rest[:, 6 * width + count :].T
    g_bias[...] = lines[0:4]
    g_gain[...] = lines[4:6]
    g_shift[...] = lines[6:8]
    g_ob[...] = lines[8:9]


def bit_reversed(value, bits):
    out = 0
    for _ in range(bits):
        out = out * 2 + value % 2
        value //= 2
    return out


def local(
    hidden,
    grad_out,
    grad_mask,
    w_query,
    w_key,
    w_value,
    w_output,
    rel_table,
    w_pos_key,
    w_pos_query,
    attn_biases,
    norm_gains,
    norm_shifts,
    w_inner,
    inner_bias,
    w_outer,
    outer_bias,
):
    count, block, width = hidden.shape
    tokens = count * block
    table = rel_table.shape[0]
    span = table // 2
    window = block + 2 * span
    units = w_inner.shape[1]
    head = width // HEADS
    scale = 1.0 / math.sqrt(3.0 * head)
    n_rows, n_seq = lax.axis_size("rows"), lax.axis_size("seq")
    row_bits, seq_bits = n_rows.bit_length() - 1, n_seq.bit_length() - 1
    share = width // n_rows
    tiles, blocks = block // TILE, table // TILE + 1
    me_seq = lax.axis_index("seq")
    x = hidden.reshape(tokens, width)
    shape = jax.ShapeDtypeStruct

    forward = [(i, i + 1) for i in range(n_seq - 1)]
    backward = [(i + 1, i) for i in range(n_seq - 1)]
    if n_seq == 2:
        start = (1 - me_seq) * (block - span)
        x_low = exchange(lax.dynamic_slice_in_dim(x, start, span, axis=0), "seq", 1)
        x_high = x_low
    else:
        x_low = lax.ppermute(x[block - span :], "seq", forward)
        x_high = lax.ppermute(x[:span], "seq", backward)

    outside = (x_low,) if n_seq == 2 else (x_low, x_high)
    places = np.zeros((width, 4), np.int32)
    for i in range(width):
        places[i] = (bit_reversed(i // share, row_bits), i % share, share, 0)

    loaded = (
        jnp.asarray(places),
        x,
        w_query,
        w_key,
        w_value,
        rel_table,
        w_pos_key,
        w_pos_query,
        attn_biases,
    )
    q3, k3, v3, pk3, pk_rev3, pq_rev3, order, x_t, rel_t, w_pk_t, w_pq_t = pl.pallas_call(
        project_kernel,
        out_shape=(
            shape((PAIRS, block, TILE), bf16),
            shape((PAIRS, block, TILE), bf16),
            shape((PAIRS, block, TILE), bf16),
            shape((PAIRS, table, TILE), bf16),
            shape((PAIRS, table, TILE), bf16),
            shape((PAIRS, table, TILE), bf16),
            shape((width, width), bf16),
            shape((width, tokens), bf16),
            shape((width, table), bf16),
            shape((width, width), bf16),
            shape((width, width), bf16),
        ),
        in_specs=[pl.BlockSpec(memory_space=pltpu.HBM)] * len(loaded),
        scratch_shapes=[pltpu.VMEM(a.shape, a.dtype) for a in loaded]
        + [pltpu.SemaphoreType.DMA((len(loaded),))],
        compiler_params=pltpu.CompilerParams(vmem_limit_bytes=12 * MiB),
        name="project",
    )(*(pltpu.with_memory_space_constraint(a, pltpu.HBM) for a in loaded))
    probs_shape = (PAIRS, 2, tiles, TILE, blocks * TILE)
    context, probs, k3, v3 = pl.pallas_call(
        partial(attend_kernel, scale=scale, n_seq=n_seq),
        out_shape=(
            shape((tokens, width), bf16),
            shape(probs_shape, bf16),
            shape((PAIRS, window, TILE), bf16),
            shape((PAIRS, window, TILE), bf16),
        ),
        scratch_shapes=[
            pltpu.VMEM((2, tiles, blocks * TILE, TILE), bf16),
            pltpu.VMEM((2 * tiles, TILE, blocks * TILE), f32),
        ],
        compiler_params=pltpu.CompilerParams(vmem_limit_bytes=20 * MiB),
        name="attend",
    )(q3, k3, v3, pk_rev3, pq_rev3, w_key, w_value, attn_biases, *outside)

    mid_cols = 2 * units + TILE
    result, d_first, d_context, mid_keep, mid_send, rows = pl.pallas_call(
        partial(middle_kernel, step=512, share=share),
        out_shape=(
            shape((tokens, width), bf16),
            shape((tokens, width), f32),
            shape((tokens, width), bf16),
            shape((width // 2, mid_cols), bf16),
            shape((width // 2, mid_cols), bf16),
            shape((16, width), f32),
        ),
        scratch_shapes=[
            pltpu.VMEM((tokens, width), bf16),
            pltpu.VMEM((tokens, units), bf16),
            pltpu.VMEM((tokens, units), bf16),
            pltpu.VMEM((tokens, width), bf16),
            pltpu.VMEM((tokens, width), bf16),
        ],
        compiler_params=pltpu.CompilerParams(vmem_limit_bytes=22 * MiB),
        name="middle",
    )(
        x,
        context,
        grad_out.reshape(tokens, width),
        grad_mask,
        w_output,
        attn_biases,
        norm_gains,
        norm_shifts,
        w_inner,
        inner_bias,
        w_outer,
        outer_bias,
        order,
    )

    def back(p, d_context):
        return pl.pallas_call(
            partial(attend_back_kernel, scale=scale, p=p),
            out_shape=(
                shape((block, TILE), bf16),
                shape((window, TILE), bf16),
                shape((window, TILE), bf16),
                shape((TILE, table), bf16),
                shape((TILE, table), bf16),
            ),
            scratch_shapes=[
                pltpu.VMEM((tiles, 2 * TILE, blocks * TILE), bf16),
                pltpu.VMEM((tiles * (blocks - 1) * TILE, 2 * TILE), bf16),
                pltpu.VMEM((2 * tiles * TILE, table), bf16),
                pltpu.VMEM((tiles, blocks, TILE, 2 * TILE), bf16),
                pltpu.VMEM((2 * window, table), bf16),
                pltpu.VMEM((TILE, window), f32),
            ],
            compiler_params=pltpu.CompilerParams(vmem_limit_bytes=20 * MiB),
            cost_estimate=pl.CostEstimate(
                flops=1000, bytes_accessed=1000, transcendentals=0
            ),
            name="attend_back",
        )(q3, k3, v3, pk3, pq_rev3, d_context, context, probs)

    def tied(first, second):
        return lax.optimization_barrier((first, second))

    def halves(total):
        return total[: total.shape[0] // 2], total[total.shape[0] // 2 :]

    def row_begin(total, step):
        keep, send = halves(total)
        return keep, exchange(send, "rows", 1 << step)

    def row_step(total, step):
        keep, received = row_begin(total, step)
        return keep + received

    def seq_step(total, step):
        return total + exchange(total, "seq", 1 << step)

    def opened(total):
        cut, part = column_cut(total.shape[1])
        one = row_step(total[:, :cut], 1)
        two = total[:, cut : cut + part] + exchange(total[:, cut + part :], "seq", 1)
        return one, two

    def finished(one, two, first=2):
        for step in range(first, row_bits + 1):
            if step < row_bits:
                one = row_step(one, step)
            two = row_step(two, step - 1)
        for step in range(seq_bits - 1):
            one = seq_step(one, step)
            two = seq_step(two, step + 1)
        return one, exchange(one, "seq", 1 << (seq_bits - 1)), two, exchange(two, "seq", 1)

    received = exchange(mid_send, "rows", 1)
    back0 = back(0, d_context)
    mid_keep, dq0 = tied(mid_keep, back0[0])
    mid = mid_keep + received
    mid, d_context = tied(mid, d_context)
    keep, send = halves(mid)
    back1 = back(1, d_context)
    received = exchange(send, "rows", 2)
    back2 = back(2, d_context)
    dq1, dq2 = back1[0], back2[0]
    mid = keep + received
    dq = (dq0, dq1, dq2)
    dk, dv, dpk, dpq = ((back0[i], back1[i], back2[i]) for i in range(1, 5))

    rest_cols = 6 * width + table + TILE
    rest_keep, rest_send = pl.pallas_call(
        partial(weight_grad_kernel, n_seq=n_seq),
        out_shape=(
            shape((width // 2, rest_cols), bf16),
            shape((width // 2, rest_cols), bf16),
        ),
        compiler_params=pltpu.CompilerParams(vmem_limit_bytes=20 * MiB),
        cost_estimate=pl.CostEstimate(flops=1000, bytes_accessed=1000, transcendentals=0),
        name="weight_grad",
    )(x_t, rel_t, w_pk_t, w_pq_t, order, rows, context, d_first, *outside, *dq, *dk, *dv, *dpk, *dpq)

    rest_send, d_first = tied(rest_send, d_first)
    edge = shape((span, width), bf16)
    loaded = (d_first, w_query, w_key, w_value)
    own, *edges = pl.pallas_call(
        input_grad_kernel,
        out_shape=(shape((tokens, width), f32),) + (edge,) * (1 if n_seq == 2 else 2),
        compiler_params=pltpu.CompilerParams(vmem_limit_bytes=12 * MiB),
        cost_estimate=pl.CostEstimate(flops=1000, bytes_accessed=1000, transcendentals=0),
        name="input_grad",
    )(*dq, *dk, *dv, *(pltpu.with_memory_space_constraint(a, pltpu.HBM) for a in loaded))
    rest_keep, own = tied(rest_keep, own)
    rest = rest_keep + exchange(rest_send, "rows", 1)
    rest, mid = tied(rest, mid)
    rest_one, rest_two = opened(rest)
    rest_one, rest_two, edges = lax.optimization_barrier((rest_one, rest_two, edges))
    nothing = jnp.zeros((block - span, width), f32)
    if n_seq == 2:
        arrived = exchange(edges[0], "seq", 1).astype(f32)
        own = own + jnp.where(
            me_seq == 0,
            jnp.concatenate([nothing, arrived], axis=0),
            jnp.concatenate([arrived, nothing], axis=0),
        )
    else:
        from_next = lax.ppermute(edges[0], "seq", backward).astype(f32)
        from_prev = lax.ppermute(edges[1], "seq", forward).astype(f32)
        own = (
            own
            + jnp.concatenate([nothing, from_next], axis=0)
            + jnp.concatenate([from_prev, nothing], axis=0)
        )
    grad_hidden = own.astype(bf16)

    rest = finished(rest_one, rest_two)
    for step in range(2, row_bits):
        mid = row_step(mid, step)
    for step in range(seq_bits - 1):
        mid = seq_step(mid, step)
    mid = (mid, exchange(mid, "seq", 1 << (seq_bits - 1)))

    square = shape((share, width), f32)
    grads = pl.pallas_call(
        partial(final_kernel, width=width, units=units, count=table),
        out_shape=(
            square,
            square,
            square,
            square,
            shape((share, table), f32),
            square,
            square,
            shape((4, share), f32),
            shape((2, share), f32),
            shape((2, share), f32),
            shape((share, units), f32),
            shape((share, units), f32),
            shape((1, share), f32),
            shape((units // TILE, TILE), f32),
        ),
        compiler_params=pltpu.CompilerParams(vmem_limit_bytes=12 * MiB),
        name="final",
    )(*mid, *rest)
    return (
        result.reshape(count, block, width),
        grad_hidden.reshape(count, block, width),
        *grads[:4],
        grads[4].T,
        *grads[5:11],
        grads[13].reshape(units),
        grads[11].T,
        grads[12].reshape(share),
    )


def solution(mesh):
    in_specs = (
        P("rows", "seq", None),
        P("rows", "seq", None),
        P("rows", "seq"),
    ) + (P(),) * 14
    out_specs = (
        P("rows", "seq", None),
        P("rows", "seq", None),
        P("rows", None),
        P("rows", None),
        P("rows", None),
        P("rows", None),
        P(None, "rows"),
        P("rows", None),
        P("rows", None),
        P(None, "rows"),
        P(None, "rows"),
        P(None, "rows"),
        P("rows", None),
        P(),
        P(None, "rows"),
        P("rows"),
    )
    return jax.shard_map(local, mesh=mesh, in_specs=in_specs, out_specs=out_specs, check_vma=False)
```

```python
from functools import partial
import math

import jax
import jax.numpy as jnp
import numpy as np
from jax import lax
from jax.experimental import pallas as pl
from jax.experimental.pallas import tpu as pltpu
from jax.sharding import PartitionSpec as P

HEADS = 6
PAIRS = HEADS // 2
TILE = 128
norm_eps = 1e-07
masked_score = -1e30
f32 = jnp.float32
bf16 = jnp.bfloat16
MiB = 1 << 20


def nn(left, right):
    return lax.dot_general(left, right, (((1,), (0,)), ((), ())), preferred_element_type=f32)


def nt(left, right):
    return lax.dot_general(left, right, (((1,), (1,)), ((), ())), preferred_element_type=f32)


def iota(shape, axis):
    return lax.broadcasted_iota(jnp.int32, shape, axis)


def where_bf16(mask, value):
    return jnp.where(mask, value.astype(f32), 0.0).astype(bf16)


def skew(block, first):
    return pltpu.roll(block, first, 1, stride=1, stride_axis=0)


def column_cut(columns):
    cut = columns // (4 * TILE) * (2 * TILE) + columns % (2 * TILE)
    return cut, (columns - cut) // 2


def store_halves(keep, send, first, value):
    value = value.astype(bf16)
    half = value.shape[0] // 2
    keep[:, first : first + value.shape[1]] = value[:half]
    send[:, first : first + value.shape[1]] = value[half:]


def store_parts(keep, send, first, value):
    cut, part = column_cut(keep.shape[1])
    bit = lax.axis_index("seq") % 2
    value = value.astype(bf16)
    half = value.shape[0] // 2
    ahead = min(max(cut - first, 0), value.shape[1])
    if ahead:
        keep[:, first : first + ahead] = value[:half, :ahead]
        send[:, first : first + ahead] = value[half:, :ahead]
    for c in range(ahead, value.shape[1], TILE):
        which, offset = divmod(first + c - cut, part)
        place = cut + jnp.bitwise_xor(which, bit) * part + offset
        cols = pl.ds(pl.multiple_of(place, TILE), TILE)
        keep[:, cols] = value[:half, c : c + TILE]
        send[:, cols] = value[half:, c : c + TILE]


def exchange(value, axis, bit):
    count = lax.axis_size(axis)
    return lax.ppermute(value, axis, [(i, i ^ bit) for i in range(count)])


def project_kernel(*refs):
    sources, outs, held, arrived = refs[:9], refs[9:20], refs[20:29], refs[29]
    q_out, k_out, v_out, pk_out, pk_rev_out, pq_rev_out, order_out = outs[:7]
    x_turned, rel_turned, w_pk_ordered, w_pq_ordered = outs[7:]
    places, x, w_query, w_key, w_value, rel, w_pos_key, w_pos_query, biases = held
    copies = [
        pltpu.make_async_copy(source, target, arrived.at[i])
        for i, (source, target) in enumerate(zip(sources, held))
    ]
    for copy in copies:
        copy.start()

    def split(out, value):
        for p in range(PAIRS):
            out[p] = value[:, p * TILE : (p + 1) * TILE].astype(bf16)

    width = order_out.shape[0]
    copies[0].wait()
    shard = jnp.bitwise_xor(places[:, 0:1], lax.axis_index("rows"))
    target = shard * places[0, 2] + places[:, 1:2]
    order_out[...] = jnp.where(iota((width, width), 1) == target, 1.0, 0.0).astype(bf16)
    for copy in copies[1:]:
        copy.wait()
    bias = biases[...].astype(f32)
    split(q_out, nn(x[...], w_query[...]) + bias[0:1])
    split(k_out, nn(x[...], w_key[...]))
    split(v_out, nn(x[...], w_value[...]) + bias[1:2])
    count = rel.shape[0]
    pos_keys = nn(rel[...], w_pos_key[...]).astype(bf16)
    pos_queries = (nn(rel[...], w_pos_query[...]) + bias[2:3]).astype(bf16)
    row, col = iota((count, count), 0), iota((count, count), 1)
    flip = jnp.where(col == count - 1 - row, 1.0, 0.0).astype(bf16)
    pick = jnp.where(col == jnp.minimum(count - row, count - 1), 1.0, 0.0).astype(bf16)
    split(pk_out, pos_keys)
    split(pk_rev_out, nn(flip, pos_keys))
    split(pq_rev_out, nn(pick, pos_queries))
    x_turned[...] = nt(order_out[...], x[...]).astype(bf16)
    rel_turned[...] = nt(order_out[...], rel[...]).astype(bf16)
    w_pk_ordered[...] = nn(order_out[...], w_pos_key[...]).astype(bf16)
    w_pq_ordered[...] = nn(order_out[...], w_pos_query[...]).astype(bf16)


def key_block_range(wb, blocks, tiles):
    low, high = max(0, blocks - 1 - wb), min(blocks - 1, tiles + blocks - 2 - wb)
    return low, high, max(low - 1, 0), min(high, blocks - 2)


def attend_kernel(q, k_own, v_own, pk_rev, pq_rev, w_key, w_value, biases, *refs, scale, n_seq):
    edges, refs = refs[:-6], refs[-6:]

    def one_pair(p, carry):
        attend_pair(
            p, q, k_own, v_own, pk_rev, pq_rev, w_key, w_value, biases, edges, *refs, scale, n_seq
        )
        return carry

    lax.fori_loop(0, PAIRS, one_pair, 0)


def attend_pair(
    p,
    q,
    k_own,
    v_own,
    pk_rev,
    pq_rev,
    w_key,
    w_value,
    biases,
    edges,
    context,
    probs,
    k,
    v,
    from_scr,
    score_scr,
    scale,
    n_seq,
):
    me_seq = lax.axis_index("seq")
    cols = pl.ds(pl.multiple_of(p * TILE, TILE), TILE)
    span, block = edges[0].shape[0], k_own.shape[1]
    k[p, span : span + block, :] = k_own[p]
    v[p, span : span + block, :] = v_own[p]
    bias = biases[1:2, cols].astype(f32)
    both = jnp.concatenate([w_key[:, cols], w_value[:, cols]], axis=1)
    sides = ((0, span + block),) if len(edges) == 1 else ((0,), (span + block,))
    for firsts, source in zip(sides, edges):
        product = nn(source[...], both)
        for first in firsts:
            k[p, first : first + span, :] = product[:, :TILE].astype(bf16)
            v[p, first : first + span, :] = (product[:, TILE:] + bias).astype(bf16)
    row, lane = iota((TILE, TILE), 0), iota((TILE, TILE), 1)
    eye = jnp.where(row == lane, 1.0, 0.0).astype(bf16)
    halves = (lane < TILE // 2, lane >= TILE // 2)
    tiles = q.shape[1] // TILE
    blocks = pk_rev.shape[1] // TILE + 1
    side = blocks // 2
    tables = []
    for h in range(2):
        table = pq_rev[p].astype(f32)
        half = iota((table.shape[0], TILE), 1) // (TILE // 2) == h
        tables.append(jnp.where(half, table, 0.0).astype(bf16))
    for wb in range(tiles + blocks - 1):
        low, high, first, last = key_block_range(wb, blocks, tiles)
        kb = k[p, wb * TILE : (wb + 1) * TILE, :]
        span = slice(first * TILE, (last + 1) * TILE)
        product = nt(kb, jnp.concatenate([tables[0][span], tables[1][span]], axis=0))
        for h in range(2):
            turned = {}
            for a in range(first, last + 1):
                at = (h * (last + 1 - first) + a - first) * TILE
                turned[a] = skew(product[:, at : at + TILE], 0)
            for e in range(low, high + 1):
                if e == 0:
                    term = turned[0]
                elif e == blocks - 1:
                    term = turned[blocks - 2]
                else:
                    term = jnp.where(lane >= row, turned[e], turned[e - 1])
                it, b = wb - (blocks - 1) + e, blocks - 1 - e
                from_scr[h, it, b * TILE : (b + 1) * TILE, :] = term.astype(bf16)
    before = jnp.where(me_seq == 0, masked_score, 0.0)
    after = jnp.where(me_seq == n_seq - 1, masked_score, 0.0)
    rate = scale * math.log2(math.e)
    chains = [(it, h) for it in range(tiles) for h in range(2)]
    stacked = jnp.concatenate(
        [where_bf16(halves[h], q[p, it * TILE : (it + 1) * TILE, :]) for it, h in chains], axis=0
    )
    product = nt(stacked, pk_rev[p])
    tops = []
    for n, (it, h) in enumerate(chains):
        rows = slice(n * TILE, (n + 1) * TILE)
        turned = [
            skew(product[rows, b * TILE : (b + 1) * TILE], 1) for b in range(blocks - 1)
        ]
        left = jnp.concatenate([stacked[rows], eye], axis=1)
        right = jnp.concatenate(
            [k[p, it * TILE : (it + blocks) * TILE, :], from_scr[h, it]], axis=1
        )
        content = nt(left, right)
        largest = None
        for b in range(blocks):
            score = content[:, b * TILE : (b + 1) * TILE]
            if b == 0:
                score = jnp.where(lane > row, score + turned[0], masked_score)
            elif b == blocks - 1:
                score = jnp.where(lane <= row, score + turned[b - 1], masked_score)
            else:
                score = score + jnp.where(lane > row, turned[b], turned[b - 1])
            if it + b < side:
                score = score + before
            if it + b >= side + tiles:
                score = score + after
            score_scr[n, :, b * TILE : (b + 1) * TILE] = score
            largest = score if largest is None else jnp.maximum(largest, score)
        tops.append(largest)
    tops = [jnp.max(top, axis=1, keepdims=True) for top in tops]
    totals = []
    for n in range(len(chains)):
        weight = jnp.exp2((score_scr[n] - tops[n]) * rate)
        score_scr[n] = weight
        total = weight[:, :TILE]
        for b in range(1, blocks):
            total = total + weight[:, b * TILE : (b + 1) * TILE]
        totals.append(total)
    inverses = [1.0 / jnp.sum(total, axis=1, keepdims=True) for total in totals]
    for n, (it, h) in enumerate(chains):
        probs[p, h, it] = (score_scr[n] * inverses[n]).astype(bf16)
    for it in range(tiles):
        both = jnp.concatenate([probs[p, 0, it], probs[p, 1, it]], axis=0)
        part = nn(both, v[p, it * TILE : (it + blocks) * TILE, :])
        context[it * TILE : (it + 1) * TILE, cols] = jnp.where(
            halves[0], part[:TILE], part[TILE:]
        ).astype(bf16)


def attend_back_kernel(
    q,
    k,
    v,
    pk,
    pq_rev,
    d_context,
    context,
    probs,
    dq_out,
    dk_out,
    dv_out,
    dpk_out,
    dpq_out,
    ds_scr,
    merged_scr,
    band_scr,
    turn_scr,
    shifted_scr,
    dv_scr,
    *,
    scale,
    p,
):
    row, lane = iota((TILE, TILE), 0), iota((TILE, TILE), 1)
    flip = jnp.where(row + lane == TILE - 1, 1.0, 0.0).astype(bf16)
    row2, lane2 = iota((2 * TILE, 2 * TILE), 0), iota((2 * TILE, 2 * TILE), 1)
    same = (row2 // TILE) == (lane2 // TILE)
    flip2 = jnp.where(
        same & (row2 % TILE + lane2 % TILE == TILE - 1), 1.0, 0.0
    ).astype(bf16)
    halves = (lane < TILE // 2, lane >= TILE // 2)
    row_halves = (row < TILE // 2, row >= TILE // 2)
    cols = slice(p * TILE, (p + 1) * TILE)
    tiles = q.shape[1] // TILE
    blocks = pk.shape[1] // TILE + 1
    keys = tiles + blocks - 1
    pairs = (blocks - 1) // 2

    def part(index):
        return slice(index * TILE, (index + 1) * TILE)

    def window(it):
        return slice(it * TILE, (it + blocks) * TILE)

    def split_rows(value):
        return jnp.concatenate([where_bf16(halves[h], value) for h in range(2)], axis=0)

    def split_turned(value):
        flat = value.astype(f32).T
        return [jnp.where(row_halves[h], flat, 0.0).astype(bf16) for h in range(2)]

    stacked_q = [split_rows(q[p, part(it), :]) for it in range(tiles)]
    for it in range(tiles):
        dct = d_context[part(it), cols]
        overlap = dct.astype(f32) * context[part(it), cols].astype(f32)
        delta = jnp.concatenate(
            [
                jnp.sum(jnp.where(halves[h], overlap, 0.0), axis=1, keepdims=True)
                for h in range(2)
            ],
            axis=0,
        )
        d_probs = nt(split_rows(dct), v[p, window(it), :])
        weights = jnp.concatenate([probs[p, 0, it], probs[p, 1, it]], axis=0)
        ds = weights.astype(f32) * (d_probs - delta) * scale
        ds_scr[it] = ds.astype(bf16)
        for h in range(2):
            for b in range(blocks - 1):
                merged = jnp.where(lane > row, ds[part(h), part(b)], ds[part(h), part(b + 1)])
                at = (it * 2 + h) * pairs + b // 2
                merged_scr[part(at), part(b % 2)] = merged.astype(bf16)
    flipped = nn(merged_scr[...], flip2)
    for it in range(tiles):
        for h in range(2):
            for b in range(blocks - 1):
                at = (it * 2 + h) * pairs + b // 2
                band_scr[part(it * 2 + h), part(blocks - 2 - b)] = skew(
                    flipped[part(at), part(b % 2)], 1
                ).astype(bf16)
    for it in range(tiles):
        for b in range(blocks):
            turn_scr[it, b] = nt(flip, ds_scr[it, :, part(b)]).astype(bf16)
    for it in range(tiles):
        both = slice(2 * it * TILE, 2 * (it + 1) * TILE)
        total = nn(
            jnp.concatenate([ds_scr[it], band_scr[both, :]], axis=1),
            jnp.concatenate([k[p, window(it), :], pk[p]], axis=0),
        )
        dq_out[part(it), :] = jnp.where(halves[0], total[:TILE], total[TILE:]).astype(bf16)
    turned = [split_turned(q[p, part(it), :]) for it in range(tiles)]
    dpk_out[...] = nn(jnp.concatenate(sum(turned, []), axis=1), band_scr[...]).astype(bf16)
    dv_scr[...] = jnp.zeros_like(dv_scr)
    for it in range(tiles):
        dv_scr[:, window(it)] += nn(
            jnp.concatenate(split_turned(d_context[part(it), cols]), axis=1),
            jnp.concatenate([probs[p, 0, it], probs[p, 1, it]], axis=0),
        )

    tables = []
    for h in range(2):
        table = pq_rev[p].astype(f32)
        half = iota((table.shape[0], TILE), 1) // (TILE // 2) == h
        tables.append(jnp.where(half, table, 0.0).astype(bf16))
    for wb in range(keys):
        low, high, first, last = key_block_range(wb, blocks, tiles)

        def source(e, h):
            if e < low or e > high:
                return jnp.zeros((TILE, TILE), f32)
            it, b = wb - (blocks - 1) + e, blocks - 1 - e
            return turn_scr[it, b, :, part(h)].astype(f32)

        for h in range(2):
            for a in range(blocks - 1):
                if first <= a <= last:
                    merged = jnp.where(lane + row >= TILE - 1, source(a, h), source(a + 1, h))
                    shifted_scr[part(2 * wb + h), part(a)] = skew(merged, 1).astype(bf16)
                else:
                    shifted_scr[part(2 * wb + h), part(a)] = jnp.zeros((TILE, TILE), bf16)
    lows = []
    for wb in range(keys):
        low, high, first, last = key_block_range(wb, blocks, tiles)
        left, right = [], []
        for e in range(low, high + 1):
            it, b = wb - (blocks - 1) + e, blocks - 1 - e
            left.append(turn_scr[it, b])
            right.append(stacked_q[it])
        span = slice(first * TILE, (last + 1) * TILE)
        for h in range(2):
            left.append(shifted_scr[part(2 * wb + h), span])
            right.append(tables[h][span])
        total = nn(jnp.concatenate(left, axis=1), jnp.concatenate(right, axis=0))
        lows.append(total.astype(bf16))
    natural = nn(flip, jnp.concatenate(lows, axis=1)).astype(bf16)
    for wb in range(keys):
        dk_out[part(wb), :] = natural[:, part(wb)]
    reverse = nn(flip, jnp.concatenate([k[p, part(wb), :] for wb in range(keys)], axis=1))
    turned = sum([split_turned(reverse[:, part(wb)]) for wb in range(keys)], [])
    dpq_out[...] = nn(jnp.concatenate(turned, axis=1), shifted_scr[...]).astype(bf16)
    for wb in range(keys):
        dv_out[part(wb), :] = dv_scr[:, part(wb)].T.astype(bf16)


def norm_parts(value):
    centre = value - jnp.mean(value, axis=1, keepdims=True)
    rate = lax.rsqrt(jnp.mean(centre * centre, axis=1, keepdims=True) + norm_eps)
    return centre * rate, rate


def norm_back(cotangent, normal, rate):
    return rate * (
        cotangent
        - jnp.mean(cotangent, axis=1, keepdims=True)
        - normal * jnp.mean(cotangent * normal, axis=1, keepdims=True)
    )


def middle_kernel(
    x,
    context,
    grad_out,
    mask,
    w_output,
    biases,
    gains,
    shifts,
    w_inner,
    inner_bias,
    w_outer,
    outer_bias,
    order,
    result,
    d_first_out,
    d_context,
    keep,
    send,
    rows_out,
    low_scr,
    active_scr,
    d_inner_scr,
    d_outer_scr,
    d_att_scr,
    *,
    step,
    share,
):
    tokens, width = x.shape
    units = w_inner.shape[1]
    bias = biases[3:4, :].astype(f32)
    gain_one, gain_two = gains[0:1, :].astype(f32), gains[1:2, :].astype(f32)
    shift_one, shift_two = shifts[0:1, :].astype(f32), shifts[1:2, :].astype(f32)
    in_bias = inner_bias[...].astype(f32).reshape(1, units)
    out_bias = outer_bias[...].astype(f32).reshape(1, width)
    diagonal = iota((TILE, TILE), 0) == iota((TILE, TILE), 1)
    sums = [jnp.zeros((1, width), f32) for _ in range(6)]

    def add(index, value):
        sums[index] = sums[index] + jnp.sum(value, axis=0, keepdims=True)

    parts = [slice(first, first + step) for first in range(0, tokens, step)]
    first_norm, slopes, second = [], [], []
    for rows in parts:
        attended = nn(context[rows, :], w_output[...]) + bias
        n_one, r_one = norm_parts(x[rows, :].astype(f32) + attended)
        normed = n_one * gain_one + shift_one
        low_scr[rows, :] = normed.astype(bf16)
        first_norm.append((n_one, r_one, normed))
    for rows in parts:
        inner = nn(low_scr[rows, :], w_inner[...]) + in_bias
        cumulative = 0.5 + 0.5 * lax.erf(inner * math.sqrt(0.5))
        active_scr[rows, :] = (inner * cumulative).astype(bf16)
        slopes.append(
            cumulative + inner * jnp.exp(-0.5 * inner * inner) * (1.0 / math.sqrt(2 * math.pi))
        )
    for rows, (_, _, normed) in zip(parts, first_norm):
        outer = nn(active_scr[rows, :], w_outer[...]) + out_bias
        n_two, r_two = norm_parts(normed + outer)
        result[rows, :] = (n_two * gain_two + shift_two).astype(bf16)
        columns = []
        for part in range(rows.start, rows.stop, TILE):
            line = mask[0:1, part : part + TILE].astype(f32)
            columns.append(jnp.sum(jnp.where(diagonal, line, 0.0), axis=1, keepdims=True))
        cotangent = grad_out[rows, :].astype(f32) * jnp.concatenate(columns, axis=0)
        add(0, cotangent * n_two)
        add(1, cotangent)
        d_second = norm_back(cotangent * gain_two, n_two, r_two)
        d_outer = d_second.astype(bf16)
        d_outer_scr[rows, :] = d_outer
        add(2, d_outer.astype(f32))
        second.append(d_second)
    for rows, slope in zip(parts, slopes):
        d_inner_scr[rows, :] = (nt(d_outer_scr[rows, :], w_outer[...]) * slope).astype(bf16)
    for rows, d_second, (n_one, r_one, _) in zip(parts, second, first_norm):
        d_normed = d_second + nt(d_inner_scr[rows, :], w_inner[...])
        add(3, d_normed * n_one)
        add(4, d_normed)
        d_first = norm_back(d_normed * gain_one, n_one, r_one)
        d_first_out[rows, :] = d_first
        d_att = d_first.astype(bf16)
        d_att_scr[rows, :] = d_att
        add(5, d_att.astype(f32))
    for rows in parts:
        d_context[rows, :] = nt(d_att_scr[rows, :], w_output[...]).astype(bf16)

    def put(first, left, right):
        turned = nt(order[...], left).astype(bf16)
        for c in range(0, right.shape[1], width):
            store_halves(keep, send, first + c, nn(turned, right[:, c : c + width]))

    put(0, low_scr[...], d_inner_scr)
    put(units, d_outer_scr[...], active_scr)
    line = nn(jnp.ones((8, tokens), bf16), d_inner_scr[...])[0:1]
    lines = [line[:, c : c + TILE] for c in range(0, units, TILE)]
    lines = jnp.concatenate(lines + [jnp.zeros((share - len(lines), TILE), f32)] * (share > len(lines)), axis=0)
    lines = jnp.concatenate([lines] * (width // share), axis=0)
    store_halves(keep, send, 2 * units, lines)
    zero = jnp.zeros((1, width), f32)
    table = [zero, zero, zero, sums[5], sums[3], sums[0], sums[4], sums[1], sums[2]]
    rows_out[...] = jnp.concatenate(table + [zero] * (16 - len(table)), axis=0)


def weight_grad_kernel(
    x_t, rel_t, w_pk_t, w_pq_t, order, rows, context, d_first, *refs, n_seq
):
    edges = refs[: 1 if n_seq == 2 else 2]
    backs, (keep, send) = refs[len(edges) : -2], refs[-2:]
    width, block = x_t.shape
    count = rel_t.shape[1]
    span = count // 2
    put = partial(store_parts, keep, send)

    def joined(index, rows=slice(None), axis=1):
        some = backs[PAIRS * index : PAIRS * (index + 1)]
        return jnp.concatenate([ref[rows, :] for ref in some], axis=axis)

    ord_ = order[...]
    dq = joined(0)
    put(0, nn(x_t[...], dq))
    turned = [nt(ord_, edge[...]).astype(bf16) for edge in edges] + [x_t[...]]
    if n_seq == 2:
        first = pl.multiple_of((1 - lax.axis_index("seq")) * (span + block), TILE)
        places = [pl.ds(first, span)]
    else:
        places = [slice(0, span), slice(span + block, 2 * span + block)]
    places.append(slice(span, span + block))
    left = jnp.concatenate(turned, axis=1)
    dk, dv = (jnp.concatenate([joined(i, r) for r in places], axis=0) for i in (1, 2))
    put(width, nn(left, dk))
    put(2 * width, nn(left, dv))
    context_t = nt(ord_, context[...]).astype(bf16)
    put(5 * width, nn(context_t, d_first[...].astype(bf16)))
    dpk, dpq = joined(3, axis=0), joined(4, axis=0)
    put(3 * width, nt(rel_t[...], dpk))
    row, col = iota((count, count), 0), iota((count, count), 1)
    pick = jnp.where(col == jnp.minimum(count - row, count - 1), 1.0, 0.0).astype(bf16)
    dpq_nat = nn(dpq, pick).astype(bf16)
    put(4 * width, nt(rel_t[...], dpq_nat))
    rel_grad = nn(w_pk_t[...], dpk)
    rel_grad = rel_grad + nn(w_pq_t[...], dpq_nat)
    put(6 * width, rel_grad)
    known = rows[...]
    sum_q = nn(jnp.ones((8, block), bf16), dq)[0:1]
    sum_v = nn(jnp.ones((8, dv.shape[0]), bf16), dv)[0:1]
    sum_p = nt(jnp.ones((8, count), bf16), dpq_nat)[0:1]
    place = iota(known.shape, 0)
    known = jnp.where(place == 0, sum_q, known)
    known = jnp.where(place == 1, sum_v, known)
    known = jnp.where(place == 2, sum_p, known)
    padded = jnp.concatenate([known, jnp.zeros((TILE - known.shape[0], width), f32)], axis=0)
    put(6 * width + count, nt(ord_, padded.astype(bf16)))


def input_grad_kernel(
    dq0, dq1, dq2, dk0, dk1, dk2, dv0, dv1, dv2, d_first, w_query, w_key, w_value, own, *outs
):
    span = outs[0].shape[0]
    block = own.shape[0]

    def joined(refs, rows):
        return jnp.concatenate([ref[rows, :] for ref in refs], axis=1)

    def halo(rows):
        return nt(joined((dk0, dk1, dk2), rows), w_key[...]) + nt(
            joined((dv0, dv1, dv2), rows), w_value[...]
        )

    if len(outs) == 1:
        first = pl.multiple_of((1 - lax.axis_index("seq")) * (span + block), TILE)
        outs[0][...] = halo(pl.ds(first, span)).astype(bf16)
    else:
        outs[0][...] = halo(slice(0, span)).astype(bf16)
        outs[1][...] = halo(slice(span + block, 2 * span + block)).astype(bf16)
    dq = jnp.concatenate([dq0[...], dq1[...], dq2[...]], axis=1)
    own[...] = halo(slice(span, span + block)) + d_first[...] + nt(dq, w_query[...])


def final_kernel(*refs, width, units, count):
    (g_q, g_k, g_v, g_o, g_rel, g_pk, g_pq, g_bias, g_gain, g_shift, g_in, g_out, g_ob, g_ib) = (
        refs[4:]
    )
    low = lax.axis_index("seq") % 2 == 0

    mid = refs[0][...].astype(f32) + refs[1][...].astype(f32)
    cut, _ = column_cut(6 * width + count + TILE)
    mine, other = refs[2][...].astype(f32), refs[3][...].astype(f32)
    rest = jnp.concatenate(
        [
            mine[:, :cut] + other[:, :cut],
            jnp.where(low, mine[:, cut:], other[:, cut:]),
            jnp.where(low, other[:, cut:], mine[:, cut:]),
        ],
        axis=1,
    )
    g_in[...] = mid[:, :units]
    g_out[...] = mid[:, units : 2 * units]
    g_ib[...] = mid[: units // TILE, 2 * units :]
    for i, out in enumerate((g_q, g_k, g_v, g_pk, g_pq, g_o)):
        out[...] = rest[:, i * width : (i + 1) * width]
    g_rel[...] = rest[:, 6 * width : 6 * width + count]
    lines = rest[:, 6 * width + count :].T
    g_bias[...] = lines[0:4]
    g_gain[...] = lines[4:6]
    g_shift[...] = lines[6:8]
    g_ob[...] = lines[8:9]


def bit_reversed(value, bits):
    out = 0
    for _ in range(bits):
        out = out * 2 + value % 2
        value //= 2
    return out


def local(
    hidden,
    grad_out,
    grad_mask,
    w_query,
    w_key,
    w_value,
    w_output,
    rel_table,
    w_pos_key,
    w_pos_query,
    attn_biases,
    norm_gains,
    norm_shifts,
    w_inner,
    inner_bias,
    w_outer,
    outer_bias,
):
    count, block, width = hidden.shape
    tokens = count * block
    table = rel_table.shape[0]
    span = table // 2
    window = block + 2 * span
    units = w_inner.shape[1]
    head = width // HEADS
    scale = 1.0 / math.sqrt(3.0 * head)
    n_rows, n_seq = lax.axis_size("rows"), lax.axis_size("seq")
    row_bits, seq_bits = n_rows.bit_length() - 1, n_seq.bit_length() - 1
    share = width // n_rows
    tiles, blocks = block // TILE, table // TILE + 1
    me_seq = lax.axis_index("seq")
    x = hidden.reshape(tokens, width)
    shape = jax.ShapeDtypeStruct

    forward = [(i, i + 1) for i in range(n_seq - 1)]
    backward = [(i + 1, i) for i in range(n_seq - 1)]
    if n_seq == 2:
        start = (1 - me_seq) * (block - span)
        x_low = exchange(lax.dynamic_slice_in_dim(x, start, span, axis=0), "seq", 1)
        x_high = x_low
    else:
        x_low = lax.ppermute(x[block - span :], "seq", forward)
        x_high = lax.ppermute(x[:span], "seq", backward)

    outside = (x_low,) if n_seq == 2 else (x_low, x_high)
    places = np.zeros((width, 4), np.int32)
    for i in range(width):
        places[i] = (bit_reversed(i // share, row_bits), i % share, share, 0)

    loaded = (
        jnp.asarray(places),
        x,
        w_query,
        w_key,
        w_value,
        rel_table,
        w_pos_key,
        w_pos_query,
        attn_biases,
    )
    q3, k3, v3, pk3, pk_rev3, pq_rev3, order, x_t, rel_t, w_pk_t, w_pq_t = pl.pallas_call(
        project_kernel,
        out_shape=(
            shape((PAIRS, block, TILE), bf16),
            shape((PAIRS, block, TILE), bf16),
            shape((PAIRS, block, TILE), bf16),
            shape((PAIRS, table, TILE), bf16),
            shape((PAIRS, table, TILE), bf16),
            shape((PAIRS, table, TILE), bf16),
            shape((width, width), bf16),
            shape((width, tokens), bf16),
            shape((width, table), bf16),
            shape((width, width), bf16),
            shape((width, width), bf16),
        ),
        in_specs=[pl.BlockSpec(memory_space=pltpu.HBM)] * len(loaded),
        scratch_shapes=[pltpu.VMEM(a.shape, a.dtype) for a in loaded]
        + [pltpu.SemaphoreType.DMA((len(loaded),))],
        compiler_params=pltpu.CompilerParams(vmem_limit_bytes=12 * MiB),
        name="project",
    )(*(pltpu.with_memory_space_constraint(a, pltpu.HBM) for a in loaded))
    probs_shape = (PAIRS, 2, tiles, TILE, blocks * TILE)
    context, probs, k3, v3 = pl.pallas_call(
        partial(attend_kernel, scale=scale, n_seq=n_seq),
        out_shape=(
            shape((tokens, width), bf16),
            shape(probs_shape, bf16),
            shape((PAIRS, window, TILE), bf16),
            shape((PAIRS, window, TILE), bf16),
        ),
        scratch_shapes=[
            pltpu.VMEM((2, tiles, blocks * TILE, TILE), bf16),
            pltpu.VMEM((2 * tiles, TILE, blocks * TILE), f32),
        ],
        compiler_params=pltpu.CompilerParams(vmem_limit_bytes=20 * MiB),
        name="attend",
    )(q3, k3, v3, pk_rev3, pq_rev3, w_key, w_value, attn_biases, *outside)

    mid_cols = 2 * units + TILE
    result, d_first, d_context, mid_keep, mid_send, rows = pl.pallas_call(
        partial(middle_kernel, step=512, share=share),
        out_shape=(
            shape((tokens, width), bf16),
            shape((tokens, width), f32),
            shape((tokens, width), bf16),
            shape((width // 2, mid_cols), bf16),
            shape((width // 2, mid_cols), bf16),
            shape((16, width), f32),
        ),
        scratch_shapes=[
            pltpu.VMEM((tokens, width), bf16),
            pltpu.VMEM((tokens, units), bf16),
            pltpu.VMEM((tokens, units), bf16),
            pltpu.VMEM((tokens, width), bf16),
            pltpu.VMEM((tokens, width), bf16),
        ],
        compiler_params=pltpu.CompilerParams(vmem_limit_bytes=22 * MiB),
        name="middle",
    )(
        x,
        context,
        grad_out.reshape(tokens, width),
        grad_mask,
        w_output,
        attn_biases,
        norm_gains,
        norm_shifts,
        w_inner,
        inner_bias,
        w_outer,
        outer_bias,
        order,
    )

    def back(p, d_context):
        return pl.pallas_call(
            partial(attend_back_kernel, scale=scale, p=p),
            out_shape=(
                shape((block, TILE), bf16),
                shape((window, TILE), bf16),
                shape((window, TILE), bf16),
                shape((TILE, table), bf16),
                shape((TILE, table), bf16),
            ),
            scratch_shapes=[
                pltpu.VMEM((tiles, 2 * TILE, blocks * TILE), bf16),
                pltpu.VMEM((tiles * (blocks - 1) * TILE, 2 * TILE), bf16),
                pltpu.VMEM((2 * tiles * TILE, table), bf16),
                pltpu.VMEM((tiles, blocks, TILE, 2 * TILE), bf16),
                pltpu.VMEM((2 * window, table), bf16),
                pltpu.VMEM((TILE, window), f32),
            ],
            compiler_params=pltpu.CompilerParams(vmem_limit_bytes=20 * MiB),
            cost_estimate=pl.CostEstimate(
                flops=1000, bytes_accessed=1000, transcendentals=0
            ),
            name="attend_back",
        )(q3, k3, v3, pk3, pq_rev3, d_context, context, probs)

    def tied(first, second):
        return lax.optimization_barrier((first, second))

    def halves(total):
        return total[: total.shape[0] // 2], total[total.shape[0] // 2 :]

    def row_begin(total, step):
        keep, send = halves(total)
        return keep, exchange(send, "rows", 1 << step)

    def row_step(total, step):
        keep, received = row_begin(total, step)
        return keep + received

    def seq_step(total, step):
        return total + exchange(total, "seq", 1 << step)

    def opened(total):
        cut, part = column_cut(total.shape[1])
        one = row_step(total[:, :cut], 1)
        two = total[:, cut : cut + part] + exchange(total[:, cut + part :], "seq", 1)
        return one, two

    def finished(one, two):
        for step in range(2, row_bits - 1):
            one = row_step(one, step)
        for step in range(2, row_bits - 1):
            two = row_step(two, step)
        both = row_step(jnp.concatenate([one, two], axis=1), row_bits - 1)
        for step in range(1, seq_bits):
            both = seq_step(both, step)
        return both, exchange(both, "seq", 1)

    received = exchange(mid_send, "rows", 1)
    back0 = back(0, d_context)
    mid_keep, dq0 = tied(mid_keep, back0[0])
    mid = mid_keep + received
    mid, d_context = tied(mid, d_context)
    keep, send = halves(mid)
    back1 = back(1, d_context)
    received = exchange(send, "rows", 2)
    back2 = back(2, d_context)
    dq1, dq2 = back1[0], back2[0]
    mid = keep + received
    dq = (dq0, dq1, dq2)
    dk, dv, dpk, dpq = ((back0[i], back1[i], back2[i]) for i in range(1, 5))

    rest_cols = 6 * width + table + TILE
    rest_keep, rest_send = pl.pallas_call(
        partial(weight_grad_kernel, n_seq=n_seq),
        out_shape=(
            shape((width // 2, rest_cols), bf16),
            shape((width // 2, rest_cols), bf16),
        ),
        compiler_params=pltpu.CompilerParams(vmem_limit_bytes=20 * MiB),
        cost_estimate=pl.CostEstimate(flops=1000, bytes_accessed=1000, transcendentals=0),
        name="weight_grad",
    )(x_t, rel_t, w_pk_t, w_pq_t, order, rows, context, d_first, *outside, *dq, *dk, *dv, *dpk, *dpq)

    rest_send, d_first = tied(rest_send, d_first)
    edge = shape((span, width), bf16)
    loaded = (d_first, w_query, w_key, w_value)
    own, *edges = pl.pallas_call(
        input_grad_kernel,
        out_shape=(shape((tokens, width), f32),) + (edge,) * (1 if n_seq == 2 else 2),
        compiler_params=pltpu.CompilerParams(vmem_limit_bytes=12 * MiB),
        cost_estimate=pl.CostEstimate(flops=1000, bytes_accessed=1000, transcendentals=0),
        name="input_grad",
    )(*dq, *dk, *dv, *(pltpu.with_memory_space_constraint(a, pltpu.HBM) for a in loaded))
    rest_keep, own = tied(rest_keep, own)
    rest = rest_keep + exchange(rest_send, "rows", 1)
    rest, mid = tied(rest, mid)
    rest_one, rest_two = opened(rest)
    rest_two = row_step(rest_two, 1)
    rest_two, edges = tied(rest_two, edges)
    nothing = jnp.zeros((block - span, width), f32)
    if n_seq == 2:
        arrived = exchange(edges[0], "seq", 1).astype(f32)
        own = own + jnp.where(
            me_seq == 0,
            jnp.concatenate([nothing, arrived], axis=0),
            jnp.concatenate([arrived, nothing], axis=0),
        )
    else:
        from_next = lax.ppermute(edges[0], "seq", backward).astype(f32)
        from_prev = lax.ppermute(edges[1], "seq", forward).astype(f32)
        own = (
            own
            + jnp.concatenate([nothing, from_next], axis=0)
            + jnp.concatenate([from_prev, nothing], axis=0)
        )
    grad_hidden = own.astype(bf16)

    rest = finished(rest_one, rest_two)
    for step in range(2, row_bits):
        mid = row_step(mid, step)
    for step in range(seq_bits - 1):
        mid = seq_step(mid, step)
    mid = (mid, exchange(mid, "seq", 1 << (seq_bits - 1)))

    square = shape((share, width), f32)
    grads = pl.pallas_call(
        partial(final_kernel, width=width, units=units, count=table),
        out_shape=(
            square,
            square,
            square,
            square,
            shape((share, table), f32),
            square,
            square,
            shape((4, share), f32),
            shape((2, share), f32),
            shape((2, share), f32),
            shape((share, units), f32),
            shape((share, units), f32),
            shape((1, share), f32),
            shape((units // TILE, TILE), f32),
        ),
        compiler_params=pltpu.CompilerParams(vmem_limit_bytes=12 * MiB),
        name="final",
    )(*mid, *rest)
    return (
        result.reshape(count, block, width),
        grad_hidden.reshape(count, block, width),
        *grads[:4],
        grads[4].T,
        *grads[5:11],
        grads[13].reshape(units),
        grads[11].T,
        grads[12].reshape(share),
    )


def solution(mesh):
    in_specs = (
        P("rows", "seq", None),
        P("rows", "seq", None),
        P("rows", "seq"),
    ) + (P(),) * 14
    out_specs = (
        P("rows", "seq", None),
        P("rows", "seq", None),
        P("rows", None),
        P("rows", None),
        P("rows", None),
        P("rows", None),
        P(None, "rows"),
        P("rows", None),
        P("rows", None),
        P(None, "rows"),
        P(None, "rows"),
        P(None, "rows"),
        P("rows", None),
        P(),
        P(None, "rows"),
        P("rows"),
    )
    return jax.shard_map(local, mesh=mesh, in_specs=in_specs, out_specs=out_specs, check_vma=False)
```

```python
from functools import partial
import math

import jax
import jax.numpy as jnp
import numpy as np
from jax import lax
from jax.experimental import pallas as pl
from jax.experimental.pallas import tpu as pltpu
from jax.sharding import PartitionSpec as P

HEADS = 6
PAIRS = HEADS // 2
TILE = 128
norm_eps = 1e-07
masked_score = -1e30
f32 = jnp.float32
bf16 = jnp.bfloat16
MiB = 1 << 20


def nn(left, right):
    return lax.dot_general(left, right, (((1,), (0,)), ((), ())), preferred_element_type=f32)


def nt(left, right):
    return lax.dot_general(left, right, (((1,), (1,)), ((), ())), preferred_element_type=f32)


def iota(shape, axis):
    return lax.broadcasted_iota(jnp.int32, shape, axis)


def where_bf16(mask, value):
    return jnp.where(mask, value.astype(f32), 0.0).astype(bf16)


def skew(block, first):
    return pltpu.roll(block, first, 1, stride=1, stride_axis=0)


def column_cut(columns):
    cut = columns // (4 * TILE) * (2 * TILE) + columns % (2 * TILE)
    return cut, (columns - cut) // 2


def store_halves(keep, send, first, value):
    value = value.astype(bf16)
    half = value.shape[0] // 2
    keep[:, first : first + value.shape[1]] = value[:half]
    send[:, first : first + value.shape[1]] = value[half:]


def store_parts(keep, send, first, value):
    cut, part = column_cut(keep.shape[1])
    bit = lax.axis_index("seq") % 2
    value = value.astype(bf16)
    half = value.shape[0] // 2
    ahead = min(max(cut - first, 0), value.shape[1])
    if ahead:
        keep[:, first : first + ahead] = value[:half, :ahead]
        send[:, first : first + ahead] = value[half:, :ahead]
    for c in range(ahead, value.shape[1], TILE):
        which, offset = divmod(first + c - cut, part)
        place = cut + jnp.bitwise_xor(which, bit) * part + offset
        cols = pl.ds(pl.multiple_of(place, TILE), TILE)
        keep[:, cols] = value[:half, c : c + TILE]
        send[:, cols] = value[half:, c : c + TILE]


def exchange(value, axis, bit):
    count = lax.axis_size(axis)
    return lax.ppermute(value, axis, [(i, i ^ bit) for i in range(count)])


def project_kernel(*refs):
    sources, outs, held, arrived = refs[:9], refs[9:20], refs[20:29], refs[29]
    q_out, k_out, v_out, pk_out, pk_rev_out, pq_rev_out, order_out = outs[:7]
    x_turned, rel_turned, w_pk_ordered, w_pq_ordered = outs[7:]
    places, x, w_query, w_key, w_value, rel, w_pos_key, w_pos_query, biases = held
    copies = [
        pltpu.make_async_copy(source, target, arrived.at[i])
        for i, (source, target) in enumerate(zip(sources, held))
    ]
    for copy in copies:
        copy.start()

    def split(out, value):
        for p in range(PAIRS):
            out[p] = value[:, p * TILE : (p + 1) * TILE].astype(bf16)

    width = order_out.shape[0]
    copies[0].wait()
    shard = jnp.bitwise_xor(places[:, 0:1], lax.axis_index("rows"))
    target = shard * places[0, 2] + places[:, 1:2]
    order_out[...] = jnp.where(iota((width, width), 1) == target, 1.0, 0.0).astype(bf16)
    for copy in copies[1:]:
        copy.wait()
    bias = biases[...].astype(f32)
    split(q_out, nn(x[...], w_query[...]) + bias[0:1])
    split(k_out, nn(x[...], w_key[...]))
    split(v_out, nn(x[...], w_value[...]) + bias[1:2])
    count = rel.shape[0]
    pos_keys = nn(rel[...], w_pos_key[...]).astype(bf16)
    pos_queries = (nn(rel[...], w_pos_query[...]) + bias[2:3]).astype(bf16)
    row, col = iota((count, count), 0), iota((count, count), 1)
    flip = jnp.where(col == count - 1 - row, 1.0, 0.0).astype(bf16)
    pick = jnp.where(col == jnp.minimum(count - row, count - 1), 1.0, 0.0).astype(bf16)
    split(pk_out, pos_keys)
    split(pk_rev_out, nn(flip, pos_keys))
    split(pq_rev_out, nn(pick, pos_queries))
    x_turned[...] = nt(order_out[...], x[...]).astype(bf16)
    rel_turned[...] = nt(order_out[...], rel[...]).astype(bf16)
    w_pk_ordered[...] = nn(order_out[...], w_pos_key[...]).astype(bf16)
    w_pq_ordered[...] = nn(order_out[...], w_pos_query[...]).astype(bf16)


def key_block_range(wb, blocks, tiles):
    low, high = max(0, blocks - 1 - wb), min(blocks - 1, tiles + blocks - 2 - wb)
    return low, high, max(low - 1, 0), min(high, blocks - 2)


def attend_kernel(q, k_own, v_own, pk_rev, pq_rev, w_key, w_value, biases, *refs, scale, n_seq):
    edges, refs = refs[:-6], refs[-6:]

    def one_pair(p, carry):
        attend_pair(
            p, q, k_own, v_own, pk_rev, pq_rev, w_key, w_value, biases, edges, *refs, scale, n_seq
        )
        return carry

    lax.fori_loop(0, PAIRS, one_pair, 0)


def attend_pair(
    p,
    q,
    k_own,
    v_own,
    pk_rev,
    pq_rev,
    w_key,
    w_value,
    biases,
    edges,
    context,
    probs,
    k,
    v,
    from_scr,
    score_scr,
    scale,
    n_seq,
):
    me_seq = lax.axis_index("seq")
    cols = pl.ds(pl.multiple_of(p * TILE, TILE), TILE)
    span, block = edges[0].shape[0], k_own.shape[1]
    k[p, span : span + block, :] = k_own[p]
    v[p, span : span + block, :] = v_own[p]
    bias = biases[1:2, cols].astype(f32)
    both = jnp.concatenate([w_key[:, cols], w_value[:, cols]], axis=1)
    sides = ((0, span + block),) if len(edges) == 1 else ((0,), (span + block,))
    for firsts, source in zip(sides, edges):
        product = nn(source[...], both)
        for first in firsts:
            k[p, first : first + span, :] = product[:, :TILE].astype(bf16)
            v[p, first : first + span, :] = (product[:, TILE:] + bias).astype(bf16)
    row, lane = iota((TILE, TILE), 0), iota((TILE, TILE), 1)
    eye = jnp.where(row == lane, 1.0, 0.0).astype(bf16)
    halves = (lane < TILE // 2, lane >= TILE // 2)
    tiles = q.shape[1] // TILE
    blocks = pk_rev.shape[1] // TILE + 1
    side = blocks // 2
    tables = []
    for h in range(2):
        table = pq_rev[p].astype(f32)
        half = iota((table.shape[0], TILE), 1) // (TILE // 2) == h
        tables.append(jnp.where(half, table, 0.0).astype(bf16))
    for wb in range(tiles + blocks - 1):
        low, high, first, last = key_block_range(wb, blocks, tiles)
        kb = k[p, wb * TILE : (wb + 1) * TILE, :]
        span = slice(first * TILE, (last + 1) * TILE)
        product = nt(kb, jnp.concatenate([tables[0][span], tables[1][span]], axis=0))
        for h in range(2):
            turned = {}
            for a in range(first, last + 1):
                at = (h * (last + 1 - first) + a - first) * TILE
                turned[a] = skew(product[:, at : at + TILE], 0)
            for e in range(low, high + 1):
                if e == 0:
                    term = turned[0]
                elif e == blocks - 1:
                    term = turned[blocks - 2]
                else:
                    term = jnp.where(lane >= row, turned[e], turned[e - 1])
                it, b = wb - (blocks - 1) + e, blocks - 1 - e
                from_scr[h, it, b * TILE : (b + 1) * TILE, :] = term.astype(bf16)
    before = jnp.where(me_seq == 0, masked_score, 0.0)
    after = jnp.where(me_seq == n_seq - 1, masked_score, 0.0)
    rate = scale * math.log2(math.e)
    chains = [(it, h) for it in range(tiles) for h in range(2)]
    stacked = jnp.concatenate(
        [where_bf16(halves[h], q[p, it * TILE : (it + 1) * TILE, :]) for it, h in chains], axis=0
    )
    product = nt(stacked, pk_rev[p])
    tops = []
    for n, (it, h) in enumerate(chains):
        rows = slice(n * TILE, (n + 1) * TILE)
        turned = [
            skew(product[rows, b * TILE : (b + 1) * TILE], 1) for b in range(blocks - 1)
        ]
        left = jnp.concatenate([stacked[rows], eye], axis=1)
        right = jnp.concatenate(
            [k[p, it * TILE : (it + blocks) * TILE, :], from_scr[h, it]], axis=1
        )
        content = nt(left, right)
        largest = None
        for b in range(blocks):
            score = content[:, b * TILE : (b + 1) * TILE]
            if b == 0:
                score = jnp.where(lane > row, score + turned[0], masked_score)
            elif b == blocks - 1:
                score = jnp.where(lane <= row, score + turned[b - 1], masked_score)
            else:
                score = score + jnp.where(lane > row, turned[b], turned[b - 1])
            if it + b < side:
                score = score + before
            if it + b >= side + tiles:
                score = score + after
            score_scr[n, :, b * TILE : (b + 1) * TILE] = score
            largest = score if largest is None else jnp.maximum(largest, score)
        tops.append(largest)
    tops = [jnp.max(top, axis=1, keepdims=True) for top in tops]
    totals = []
    for n in range(len(chains)):
        weight = jnp.exp2((score_scr[n] - tops[n]) * rate)
        score_scr[n] = weight
        total = weight[:, :TILE]
        for b in range(1, blocks):
            total = total + weight[:, b * TILE : (b + 1) * TILE]
        totals.append(total)
    inverses = [1.0 / jnp.sum(total, axis=1, keepdims=True) for total in totals]
    for n, (it, h) in enumerate(chains):
        probs[p, h, it] = (score_scr[n] * inverses[n]).astype(bf16)
    for it in range(tiles):
        both = jnp.concatenate([probs[p, 0, it], probs[p, 1, it]], axis=0)
        part = nn(both, v[p, it * TILE : (it + blocks) * TILE, :])
        context[it * TILE : (it + 1) * TILE, cols] = jnp.where(
            halves[0], part[:TILE], part[TILE:]
        ).astype(bf16)


def attend_back_kernel(
    q,
    k,
    v,
    pk,
    pq_rev,
    d_context,
    context,
    probs,
    dq_out,
    dk_out,
    dv_out,
    dpk_out,
    dpq_out,
    ds_scr,
    merged_scr,
    band_scr,
    turn_scr,
    shifted_scr,
    dv_scr,
    dk_scr,
    *,
    scale,
    p,
):
    row, lane = iota((TILE, TILE), 0), iota((TILE, TILE), 1)
    flip = jnp.where(row + lane == TILE - 1, 1.0, 0.0).astype(bf16)
    row2, lane2 = iota((2 * TILE, 2 * TILE), 0), iota((2 * TILE, 2 * TILE), 1)
    same = (row2 // TILE) == (lane2 // TILE)
    flip2 = jnp.where(
        same & (row2 % TILE + lane2 % TILE == TILE - 1), 1.0, 0.0
    ).astype(bf16)
    halves = (lane < TILE // 2, lane >= TILE // 2)
    row_halves = (row < TILE // 2, row >= TILE // 2)
    cols = slice(p * TILE, (p + 1) * TILE)
    tiles = q.shape[1] // TILE
    blocks = pk.shape[1] // TILE + 1
    keys = tiles + blocks - 1
    pairs = (blocks - 1) // 2

    def part(index):
        return slice(index * TILE, (index + 1) * TILE)

    def window(it):
        return slice(it * TILE, (it + blocks) * TILE)

    def split_rows(value):
        return jnp.concatenate([where_bf16(halves[h], value) for h in range(2)], axis=0)

    def split_turned(value):
        flat = value.astype(f32).T
        return [jnp.where(row_halves[h], flat, 0.0).astype(bf16) for h in range(2)]

    for it in range(tiles):
        dct = d_context[part(it), cols]
        overlap = dct.astype(f32) * context[part(it), cols].astype(f32)
        delta = jnp.concatenate(
            [
                jnp.sum(jnp.where(halves[h], overlap, 0.0), axis=1, keepdims=True)
                for h in range(2)
            ],
            axis=0,
        )
        d_probs = nt(split_rows(dct), v[p, window(it), :])
        weights = jnp.concatenate([probs[p, 0, it], probs[p, 1, it]], axis=0)
        ds = weights.astype(f32) * (d_probs - delta) * scale
        ds_scr[it] = ds.astype(bf16)
        for h in range(2):
            for b in range(blocks - 1):
                merged = jnp.where(lane > row, ds[part(h), part(b)], ds[part(h), part(b + 1)])
                at = (it * 2 + h) * pairs + b // 2
                merged_scr[part(at), part(b % 2)] = merged.astype(bf16)
    flipped = nn(merged_scr[...], flip2)
    for it in range(tiles):
        for h in range(2):
            for b in range(blocks - 1):
                at = (it * 2 + h) * pairs + b // 2
                band_scr[part(it * 2 + h), part(blocks - 2 - b)] = skew(
                    flipped[part(at), part(b % 2)], 1
                ).astype(bf16)
    for it in range(tiles):
        for b in range(blocks):
            turn_scr[it, b] = nt(flip, ds_scr[it, :, part(b)]).astype(bf16)
    reverse = nn(flip, jnp.concatenate([k[p, part(wb), :] for wb in range(keys)], axis=1))
    reverse_t = [reverse[:, part(wb)].T for wb in range(keys)]
    for it in range(tiles):
        left = jnp.concatenate([reverse_t[it + b].astype(bf16) for b in range(blocks)], axis=1)
        direct = nn(left, jnp.concatenate([turn_scr[it, b] for b in range(blocks)], axis=0))
        direct = jnp.where(row_halves[0], direct[:, :TILE], direct[:, TILE:]).T
        total = nn(band_scr[2 * it * TILE : 2 * (it + 1) * TILE, :], pk[p])
        total = jnp.where(halves[0], total[:TILE], total[TILE:])
        dq_out[part(it), :] = (direct + total).astype(bf16)
    turned = [split_turned(q[p, part(it), :]) for it in range(tiles)]
    dpk_out[...] = nn(jnp.concatenate(sum(turned, []), axis=1), band_scr[...]).astype(bf16)
    dv_scr[...] = jnp.zeros_like(dv_scr)
    dk_scr[...] = jnp.zeros_like(dk_scr)
    for it in range(tiles):
        dk_scr[:, window(it)] += nn(jnp.concatenate(turned[it], axis=1), ds_scr[it])
        dv_scr[:, window(it)] += nn(
            jnp.concatenate(split_turned(d_context[part(it), cols]), axis=1),
            jnp.concatenate([probs[p, 0, it], probs[p, 1, it]], axis=0),
        )

    tables = []
    for h in range(2):
        table = pq_rev[p].astype(f32)
        half = iota((table.shape[0], TILE), 1) // (TILE // 2) == h
        tables.append(jnp.where(half, table, 0.0).astype(bf16))
    for wb in range(keys):
        low, high, first, last = key_block_range(wb, blocks, tiles)

        def source(e, h):
            if e < low or e > high:
                return jnp.zeros((TILE, TILE), f32)
            it, b = wb - (blocks - 1) + e, blocks - 1 - e
            return turn_scr[it, b, :, part(h)].astype(f32)

        for h in range(2):
            for a in range(blocks - 1):
                if first <= a <= last:
                    merged = jnp.where(lane + row >= TILE - 1, source(a, h), source(a + 1, h))
                    shifted_scr[part(2 * wb + h), part(a)] = skew(merged, 1).astype(bf16)
                else:
                    shifted_scr[part(2 * wb + h), part(a)] = jnp.zeros((TILE, TILE), bf16)
    lows = []
    for wb in range(keys):
        low, high, first, last = key_block_range(wb, blocks, tiles)
        left, right = [], []
        span = slice(first * TILE, (last + 1) * TILE)
        for h in range(2):
            left.append(shifted_scr[part(2 * wb + h), span])
            right.append(tables[h][span])
        total = nn(jnp.concatenate(left, axis=1), jnp.concatenate(right, axis=0))
        lows.append(total.astype(bf16))
    natural = nn(flip, jnp.concatenate(lows, axis=1))
    for wb in range(keys):
        direct = dk_scr[:, part(wb)].T
        dk_out[part(wb), :] = (natural[:, part(wb)] + direct).astype(bf16)
    turned = [
        jnp.where(row_halves[h], reverse_t[wb], 0.0).astype(bf16)
        for wb in range(keys)
        for h in range(2)
    ]
    dpq_out[...] = nn(jnp.concatenate(turned, axis=1), shifted_scr[...]).astype(bf16)
    for wb in range(keys):
        dv_out[part(wb), :] = dv_scr[:, part(wb)].T.astype(bf16)


def norm_parts(value):
    centre = value - jnp.mean(value, axis=1, keepdims=True)
    rate = lax.rsqrt(jnp.mean(centre * centre, axis=1, keepdims=True) + norm_eps)
    return centre * rate, rate


def norm_back(cotangent, normal, rate):
    return rate * (
        cotangent
        - jnp.mean(cotangent, axis=1, keepdims=True)
        - normal * jnp.mean(cotangent * normal, axis=1, keepdims=True)
    )


def middle_kernel(
    x,
    context,
    grad_out,
    mask,
    w_output,
    biases,
    gains,
    shifts,
    w_inner,
    inner_bias,
    w_outer,
    outer_bias,
    order,
    result,
    d_first_out,
    d_context,
    keep,
    send,
    inner_out,
    rows_out,
    low_scr,
    active_scr,
    d_inner_scr,
    d_outer_scr,
    d_att_scr,
    *,
    step,
):
    tokens, width = x.shape
    units = w_inner.shape[1]
    bias = biases[3:4, :].astype(f32)
    gain_one, gain_two = gains[0:1, :].astype(f32), gains[1:2, :].astype(f32)
    shift_one, shift_two = shifts[0:1, :].astype(f32), shifts[1:2, :].astype(f32)
    in_bias = inner_bias[...].astype(f32).reshape(1, units)
    out_bias = outer_bias[...].astype(f32).reshape(1, width)
    diagonal = iota((TILE, TILE), 0) == iota((TILE, TILE), 1)
    sums = [jnp.zeros((1, width), f32) for _ in range(6)]

    def add(index, value):
        sums[index] = sums[index] + jnp.sum(value, axis=0, keepdims=True)

    parts = [slice(first, first + step) for first in range(0, tokens, step)]
    first_norm, slopes, second = [], [], []
    for rows in parts:
        attended = nn(context[rows, :], w_output[...]) + bias
        n_one, r_one = norm_parts(x[rows, :].astype(f32) + attended)
        normed = n_one * gain_one + shift_one
        low_scr[rows, :] = normed.astype(bf16)
        first_norm.append((n_one, r_one, normed))
    for rows in parts:
        inner = nn(low_scr[rows, :], w_inner[...]) + in_bias
        cumulative = 0.5 + 0.5 * lax.erf(inner * math.sqrt(0.5))
        active_scr[rows, :] = (inner * cumulative).astype(bf16)
        slopes.append(
            cumulative + inner * jnp.exp(-0.5 * inner * inner) * (1.0 / math.sqrt(2 * math.pi))
        )
    for rows, (_, _, normed) in zip(parts, first_norm):
        outer = nn(active_scr[rows, :], w_outer[...]) + out_bias
        n_two, r_two = norm_parts(normed + outer)
        result[rows, :] = (n_two * gain_two + shift_two).astype(bf16)
        columns = []
        for part in range(rows.start, rows.stop, TILE):
            line = mask[0:1, part : part + TILE].astype(f32)
            columns.append(jnp.sum(jnp.where(diagonal, line, 0.0), axis=1, keepdims=True))
        cotangent = grad_out[rows, :].astype(f32) * jnp.concatenate(columns, axis=0)
        add(0, cotangent * n_two)
        add(1, cotangent)
        d_second = norm_back(cotangent * gain_two, n_two, r_two)
        d_outer = d_second.astype(bf16)
        d_outer_scr[rows, :] = d_outer
        add(2, d_outer.astype(f32))
        second.append(d_second)
    for rows, slope in zip(parts, slopes):
        d_inner_scr[rows, :] = (nt(d_outer_scr[rows, :], w_outer[...]) * slope).astype(bf16)
    for rows, d_second, (n_one, r_one, _) in zip(parts, second, first_norm):
        d_normed = d_second + nt(d_inner_scr[rows, :], w_inner[...])
        add(3, d_normed * n_one)
        add(4, d_normed)
        d_first = norm_back(d_normed * gain_one, n_one, r_one)
        d_first_out[rows, :] = d_first
        d_att = d_first.astype(bf16)
        d_att_scr[rows, :] = d_att
        add(5, d_att.astype(f32))
    for rows in parts:
        d_context[rows, :] = nt(d_att_scr[rows, :], w_output[...]).astype(bf16)

    def put(first, left, right):
        turned = nt(order[...], left).astype(bf16)
        for c in range(0, right.shape[1], width):
            store_halves(keep, send, first + c, nn(turned, right[:, c : c + width]))

    put(0, low_scr[...], d_inner_scr)
    put(units, d_outer_scr[...], active_scr)
    inner_out[...] = nn(jnp.ones((8, tokens), bf16), d_inner_scr[...])
    zero = jnp.zeros((1, width), f32)
    table = [zero, zero, zero, sums[5], sums[3], sums[0], sums[4], sums[1], sums[2]]
    rows_out[...] = jnp.concatenate(table + [zero] * (16 - len(table)), axis=0)


def weight_grad_kernel(
    x_t, rel_t, w_pk_t, w_pq_t, order, rows, context, d_first, inner, *refs, n_seq, share
):
    edges = refs[: 1 if n_seq == 2 else 2]
    backs, (keep, send) = refs[len(edges) : -2], refs[-2:]
    width, block = x_t.shape
    count = rel_t.shape[1]
    span = count // 2
    put = partial(store_parts, keep, send)

    def joined(index, rows=slice(None), axis=1):
        some = backs[PAIRS * index : PAIRS * (index + 1)]
        return jnp.concatenate([ref[rows, :] for ref in some], axis=axis)

    ord_ = order[...]
    dq = joined(0)
    put(0, nn(x_t[...], dq))
    turned = [nt(ord_, edge[...]).astype(bf16) for edge in edges] + [x_t[...]]
    if n_seq == 2:
        first = pl.multiple_of((1 - lax.axis_index("seq")) * (span + block), TILE)
        places = [pl.ds(first, span)]
    else:
        places = [slice(0, span), slice(span + block, 2 * span + block)]
    places.append(slice(span, span + block))
    left = jnp.concatenate(turned, axis=1)
    dk, dv = (jnp.concatenate([joined(i, r) for r in places], axis=0) for i in (1, 2))
    put(width, nn(left, dk))
    put(2 * width, nn(left, dv))
    context_t = nt(ord_, context[...]).astype(bf16)
    put(5 * width, nn(context_t, d_first[...].astype(bf16)))
    dpk, dpq = joined(3, axis=0), joined(4, axis=0)
    put(3 * width, nt(rel_t[...], dpk))
    row, col = iota((count, count), 0), iota((count, count), 1)
    pick = jnp.where(col == jnp.minimum(count - row, count - 1), 1.0, 0.0).astype(bf16)
    dpq_nat = nn(dpq, pick).astype(bf16)
    put(4 * width, nt(rel_t[...], dpq_nat))
    rel_grad = nn(w_pk_t[...], dpk)
    rel_grad = rel_grad + nn(w_pq_t[...], dpq_nat)
    put(6 * width, rel_grad)
    known = rows[...]
    sum_q = nn(jnp.ones((8, block), bf16), dq)[0:1]
    sum_v = nn(jnp.ones((8, dv.shape[0]), bf16), dv)[0:1]
    sum_p = nt(jnp.ones((8, count), bf16), dpq_nat)[0:1]
    place = iota(known.shape, 0)
    known = jnp.where(place == 0, sum_q, known)
    known = jnp.where(place == 1, sum_v, known)
    known = jnp.where(place == 2, sum_p, known)
    padded = jnp.concatenate([known, jnp.zeros((TILE - known.shape[0], width), f32)], axis=0)
    block = nt(ord_, padded.astype(bf16))
    lines = [inner[0:1, c : c + TILE] for c in range(0, inner.shape[1], TILE)]
    some = len(lines)
    lines = jnp.concatenate(lines + [jnp.zeros((-some % 8, TILE), f32)] * (some % 8 > 0), axis=0)
    if compact_bias(share, inner.shape[1]):
        turned = pltpu.roll(lines, TILE // 2, 1)
        picked = [t[j : j + 1] for j in range(some) for t in (turned, lines)]
        picked += [jnp.zeros((share - 2 * some, TILE), f32)] * (share > 2 * some)
        lines = jnp.concatenate(picked, axis=0)
        lines = jnp.where(iota(lines.shape, 1) >= TILE // 2, lines, 0.0)
        put(6 * width + count, block + jnp.concatenate([lines] * (width // share), axis=0))
    else:
        put(6 * width + count, block)
        lines = [lines[:some]] + [jnp.zeros((share - some, TILE), f32)] * (share > some)
        put(6 * width + count + TILE, jnp.concatenate(lines * (width // share), axis=0))


def input_grad_kernel(
    dq0, dq1, dq2, dk0, dk1, dk2, dv0, dv1, dv2, d_first, w_query, w_key, w_value, own, *outs
):
    span = outs[0].shape[0]
    block = own.shape[0]

    def joined(refs, rows):
        return jnp.concatenate([ref[rows, :] for ref in refs], axis=1)

    def halo(rows):
        return nt(joined((dk0, dk1, dk2), rows), w_key[...]) + nt(
            joined((dv0, dv1, dv2), rows), w_value[...]
        )

    if len(outs) == 1:
        first = pl.multiple_of((1 - lax.axis_index("seq")) * (span + block), TILE)
        outs[0][...] = halo(pl.ds(first, span)).astype(bf16)
    else:
        outs[0][...] = halo(slice(0, span)).astype(bf16)
        outs[1][...] = halo(slice(span + block, 2 * span + block)).astype(bf16)
    dq = jnp.concatenate([dq0[...], dq1[...], dq2[...]], axis=1)
    own[...] = halo(slice(span, span + block)) + d_first[...] + nt(dq, w_query[...])


def compact_bias(share, units):
    return 2 * units // TILE <= share


def final_kernel(*refs, width, units, count):
    (g_q, g_k, g_v, g_o, g_rel, g_pk, g_pq, g_bias, g_gain, g_shift, g_in, g_out, g_ob, g_ib) = (
        refs[4:]
    )
    low = lax.axis_index("seq") % 2 == 0
    share = refs[0].shape[0]
    mid = refs[0][...].astype(f32) + refs[1][...].astype(f32)
    cut, _ = column_cut(6 * width + count + (1 if compact_bias(share, units) else 2) * TILE)
    mine, other = refs[2][...].astype(f32), refs[3][...].astype(f32)
    rest = jnp.concatenate(
        [
            mine[:, :cut] + other[:, :cut],
            jnp.where(low, mine[:, cut:], other[:, cut:]),
            jnp.where(low, other[:, cut:], mine[:, cut:]),
        ],
        axis=1,
    )
    g_in[...] = mid[:, :units]
    g_out[...] = mid[:, units : 2 * units]
    for i, out in enumerate((g_q, g_k, g_v, g_pk, g_pq, g_o)):
        out[...] = rest[:, i * width : (i + 1) * width]
    g_rel[...] = rest[:, 6 * width : 6 * width + count]
    block = rest[:, 6 * width + count : 6 * width + count + TILE]
    if compact_bias(share, units):
        turned = pltpu.roll(block, TILE // 2, 1)
        left = iota((1, TILE), 1) < TILE // 2
        g_ib[...] = jnp.concatenate(
            [
                jnp.where(left, turned[2 * j : 2 * j + 1], block[2 * j + 1 : 2 * j + 2])
                for j in range(units // TILE)
            ],
            axis=0,
        )
    else:
        g_ib[...] = rest[: units // TILE, 6 * width + count + TILE :]
    lines = block.T
    g_bias[...] = lines[0:4]
    g_gain[...] = lines[4:6]
    g_shift[...] = lines[6:8]
    g_ob[...] = lines[8:9]


def bit_reversed(value, bits):
    out = 0
    for _ in range(bits):
        out = out * 2 + value % 2
        value //= 2
    return out


def local(
    hidden,
    grad_out,
    grad_mask,
    w_query,
    w_key,
    w_value,
    w_output,
    rel_table,
    w_pos_key,
    w_pos_query,
    attn_biases,
    norm_gains,
    norm_shifts,
    w_inner,
    inner_bias,
    w_outer,
    outer_bias,
):
    count, block, width = hidden.shape
    tokens = count * block
    table = rel_table.shape[0]
    span = table // 2
    window = block + 2 * span
    units = w_inner.shape[1]
    head = width // HEADS
    scale = 1.0 / math.sqrt(3.0 * head)
    n_rows, n_seq = lax.axis_size("rows"), lax.axis_size("seq")
    row_bits, seq_bits = n_rows.bit_length() - 1, n_seq.bit_length() - 1
    share = width // n_rows
    tiles, blocks = block // TILE, table // TILE + 1
    me_seq = lax.axis_index("seq")
    x = hidden.reshape(tokens, width)
    shape = jax.ShapeDtypeStruct

    forward = [(i, i + 1) for i in range(n_seq - 1)]
    backward = [(i + 1, i) for i in range(n_seq - 1)]
    if n_seq == 2:
        start = (1 - me_seq) * (block - span)
        x_low = exchange(lax.dynamic_slice_in_dim(x, start, span, axis=0), "seq", 1)
        x_high = x_low
    else:
        x_low = lax.ppermute(x[block - span :], "seq", forward)
        x_high = lax.ppermute(x[:span], "seq", backward)

    outside = (x_low,) if n_seq == 2 else (x_low, x_high)
    places = np.zeros((width, 4), np.int32)
    for i in range(width):
        places[i] = (bit_reversed(i // share, row_bits), i % share, share, 0)

    loaded = (
        jnp.asarray(places),
        x,
        w_query,
        w_key,
        w_value,
        rel_table,
        w_pos_key,
        w_pos_query,
        attn_biases,
    )
    q3, k3, v3, pk3, pk_rev3, pq_rev3, order, x_t, rel_t, w_pk_t, w_pq_t = pl.pallas_call(
        project_kernel,
        out_shape=(
            shape((PAIRS, block, TILE), bf16),
            shape((PAIRS, block, TILE), bf16),
            shape((PAIRS, block, TILE), bf16),
            shape((PAIRS, table, TILE), bf16),
            shape((PAIRS, table, TILE), bf16),
            shape((PAIRS, table, TILE), bf16),
            shape((width, width), bf16),
            shape((width, tokens), bf16),
            shape((width, table), bf16),
            shape((width, width), bf16),
            shape((width, width), bf16),
        ),
        in_specs=[pl.BlockSpec(memory_space=pltpu.HBM)] * len(loaded),
        scratch_shapes=[pltpu.VMEM(a.shape, a.dtype) for a in loaded]
        + [pltpu.SemaphoreType.DMA((len(loaded),))],
        compiler_params=pltpu.CompilerParams(vmem_limit_bytes=12 * MiB),
        name="project",
    )(*(pltpu.with_memory_space_constraint(a, pltpu.HBM) for a in loaded))
    probs_shape = (PAIRS, 2, tiles, TILE, blocks * TILE)
    context, probs, k3, v3 = pl.pallas_call(
        partial(attend_kernel, scale=scale, n_seq=n_seq),
        out_shape=(
            shape((tokens, width), bf16),
            shape(probs_shape, bf16),
            shape((PAIRS, window, TILE), bf16),
            shape((PAIRS, window, TILE), bf16),
        ),
        scratch_shapes=[
            pltpu.VMEM((2, tiles, blocks * TILE, TILE), bf16),
            pltpu.VMEM((2 * tiles, TILE, blocks * TILE), f32),
        ],
        compiler_params=pltpu.CompilerParams(vmem_limit_bytes=20 * MiB),
        name="attend",
    )(q3, k3, v3, pk_rev3, pq_rev3, w_key, w_value, attn_biases, *outside)

    mid_cols = 2 * units
    result, d_first, d_context, mid_keep, mid_send, inner_sum, rows = pl.pallas_call(
        partial(middle_kernel, step=512),
        out_shape=(
            shape((tokens, width), bf16),
            shape((tokens, width), f32),
            shape((tokens, width), bf16),
            shape((width // 2, mid_cols), bf16),
            shape((width // 2, mid_cols), bf16),
            shape((8, units), f32),
            shape((16, width), f32),
        ),
        scratch_shapes=[
            pltpu.VMEM((tokens, width), bf16),
            pltpu.VMEM((tokens, units), bf16),
            pltpu.VMEM((tokens, units), bf16),
            pltpu.VMEM((tokens, width), bf16),
            pltpu.VMEM((tokens, width), bf16),
        ],
        compiler_params=pltpu.CompilerParams(vmem_limit_bytes=22 * MiB),
        name="middle",
    )(
        x,
        context,
        grad_out.reshape(tokens, width),
        grad_mask,
        w_output,
        attn_biases,
        norm_gains,
        norm_shifts,
        w_inner,
        inner_bias,
        w_outer,
        outer_bias,
        order,
    )

    def back(p, d_context):
        return pl.pallas_call(
            partial(attend_back_kernel, scale=scale, p=p),
            out_shape=(
                shape((block, TILE), bf16),
                shape((window, TILE), bf16),
                shape((window, TILE), bf16),
                shape((TILE, table), bf16),
                shape((TILE, table), bf16),
            ),
            scratch_shapes=[
                pltpu.VMEM((tiles, 2 * TILE, blocks * TILE), bf16),
                pltpu.VMEM((tiles * (blocks - 1) * TILE, 2 * TILE), bf16),
                pltpu.VMEM((2 * tiles * TILE, table), bf16),
                pltpu.VMEM((tiles, blocks, TILE, 2 * TILE), bf16),
                pltpu.VMEM((2 * window, table), bf16),
                pltpu.VMEM((TILE, window), f32),
                pltpu.VMEM((TILE, window), f32),
            ],
            compiler_params=pltpu.CompilerParams(vmem_limit_bytes=20 * MiB),
            cost_estimate=pl.CostEstimate(
                flops=1000, bytes_accessed=1000, transcendentals=0
            ),
            name="attend_back",
        )(q3, k3, v3, pk3, pq_rev3, d_context, context, probs)

    def tied(first, second):
        return lax.optimization_barrier((first, second))

    def halves(total):
        return total[: total.shape[0] // 2], total[total.shape[0] // 2 :]

    def row_begin(total, step):
        keep, send = halves(total)
        return keep, exchange(send, "rows", 1 << step)

    def row_step(total, step):
        keep, received = row_begin(total, step)
        return keep + received

    def seq_step(total, step):
        return total + exchange(total, "seq", 1 << step)

    def opened(total):
        cut, part = column_cut(total.shape[1])
        one = row_step(total[:, :cut], 1)
        two = total[:, cut : cut + part] + exchange(total[:, cut + part :], "seq", 1)
        return one, two

    def finished(one, two):
        for step in range(2, row_bits - 1):
            one = row_step(one, step)
        for step in range(2, row_bits - 1):
            two = row_step(two, step)
        both = row_step(jnp.concatenate([one, two], axis=1), row_bits - 1)
        for step in range(1, seq_bits):
            both = seq_step(both, step)
        return both, exchange(both, "seq", 1)

    received = exchange(mid_send, "rows", 1)
    back0 = back(0, d_context)
    mid_keep, dq0 = tied(mid_keep, back0[0])
    mid = mid_keep + received
    mid, d_context = tied(mid, d_context)
    keep, send = halves(mid)
    back1 = back(1, d_context)
    received = exchange(send, "rows", 2)
    back2 = back(2, d_context)
    dq1, dq2 = back1[0], back2[0]
    mid = keep + received
    dq = (dq0, dq1, dq2)
    dk, dv, dpk, dpq = ((back0[i], back1[i], back2[i]) for i in range(1, 5))

    rest_cols = 6 * width + table + (1 if compact_bias(share, units) else 2) * TILE
    rest_keep, rest_send = pl.pallas_call(
        partial(weight_grad_kernel, n_seq=n_seq, share=share),
        out_shape=(
            shape((width // 2, rest_cols), bf16),
            shape((width // 2, rest_cols), bf16),
        ),
        compiler_params=pltpu.CompilerParams(vmem_limit_bytes=20 * MiB),
        cost_estimate=pl.CostEstimate(flops=1000, bytes_accessed=1000, transcendentals=0),
        name="weight_grad",
    )(x_t, rel_t, w_pk_t, w_pq_t, order, rows, context, d_first, inner_sum, *outside, *dq, *dk, *dv, *dpk, *dpq)

    rest_send, d_first = tied(rest_send, d_first)
    edge = shape((span, width), bf16)
    loaded = (d_first, w_query, w_key, w_value)
    own, *edges = pl.pallas_call(
        input_grad_kernel,
        out_shape=(shape((tokens, width), f32),) + (edge,) * (1 if n_seq == 2 else 2),
        compiler_params=pltpu.CompilerParams(vmem_limit_bytes=12 * MiB),
        cost_estimate=pl.CostEstimate(flops=1000, bytes_accessed=1000, transcendentals=0),
        name="input_grad",
    )(*dq, *dk, *dv, *(pltpu.with_memory_space_constraint(a, pltpu.HBM) for a in loaded))
    rest_keep, own = tied(rest_keep, own)
    rest = rest_keep + exchange(rest_send, "rows", 1)
    rest, mid = tied(rest, mid)
    rest_one, rest_two = opened(rest)
    rest_two = row_step(rest_two, 1)
    rest_two, edges = tied(rest_two, edges)
    nothing = jnp.zeros((block - span, width), f32)
    if n_seq == 2:
        arrived = exchange(edges[0], "seq", 1).astype(f32)
        own = own + jnp.where(
            me_seq == 0,
            jnp.concatenate([nothing, arrived], axis=0),
            jnp.concatenate([arrived, nothing], axis=0),
        )
    else:
        from_next = lax.ppermute(edges[0], "seq", backward).astype(f32)
        from_prev = lax.ppermute(edges[1], "seq", forward).astype(f32)
        own = (
            own
            + jnp.concatenate([nothing, from_next], axis=0)
            + jnp.concatenate([from_prev, nothing], axis=0)
        )
    grad_hidden = own.astype(bf16)

    rest = finished(rest_one, rest_two)
    for step in range(2, row_bits):
        mid = row_step(mid, step)
    for step in range(seq_bits - 1):
        mid = seq_step(mid, step)
    mid = (mid, exchange(mid, "seq", 1 << (seq_bits - 1)))

    square = shape((share, width), f32)
    grads = pl.pallas_call(
        partial(final_kernel, width=width, units=units, count=table),
        out_shape=(
            square,
            square,
            square,
            square,
            shape((share, table), f32),
            square,
            square,
            shape((4, share), f32),
            shape((2, share), f32),
            shape((2, share), f32),
            shape((share, units), f32),
            shape((share, units), f32),
            shape((1, share), f32),
            shape((units // TILE, TILE), f32),
        ),
        compiler_params=pltpu.CompilerParams(vmem_limit_bytes=12 * MiB),
        name="final",
    )(*mid, *rest)
    return (
        result.reshape(count, block, width),
        grad_hidden.reshape(count, block, width),
        *grads[:4],
        grads[4].T,
        *grads[5:11],
        grads[13].reshape(units),
        grads[11].T,
        grads[12].reshape(share),
    )


def solution(mesh):
    in_specs = (
        P("rows", "seq", None),
        P("rows", "seq", None),
        P("rows", "seq"),
    ) + (P(),) * 14
    out_specs = (
        P("rows", "seq", None),
        P("rows", "seq", None),
        P("rows", None),
        P("rows", None),
        P("rows", None),
        P("rows", None),
        P(None, "rows"),
        P("rows", None),
        P("rows", None),
        P(None, "rows"),
        P(None, "rows"),
        P(None, "rows"),
        P("rows", None),
        P(),
        P(None, "rows"),
        P("rows"),
    )
    return jax.shard_map(local, mesh=mesh, in_specs=in_specs, out_specs=out_specs, check_vma=False)
```

```python
from functools import partial
import math

import jax
import jax.numpy as jnp
import numpy as np
from jax import lax
from jax.experimental import pallas as pl
from jax.experimental.pallas import tpu as pltpu
from jax.sharding import PartitionSpec as P

HEADS = 6
PAIRS = HEADS // 2
TILE = 128
norm_eps = 1e-07
masked_score = -1e30
f32 = jnp.float32
bf16 = jnp.bfloat16
MiB = 1 << 20


def nn(left, right):
    return lax.dot_general(left, right, (((1,), (0,)), ((), ())), preferred_element_type=f32)


def nt(left, right):
    return lax.dot_general(left, right, (((1,), (1,)), ((), ())), preferred_element_type=f32)


def iota(shape, axis):
    return lax.broadcasted_iota(jnp.int32, shape, axis)


def where_bf16(mask, value):
    return jnp.where(mask, value.astype(f32), 0.0).astype(bf16)


def skew(block, first):
    return pltpu.roll(block, first, 1, stride=1, stride_axis=0)


def column_cut(columns):
    cut = columns // (4 * TILE) * (2 * TILE) + columns % (2 * TILE)
    return cut, (columns - cut) // 2


def store_halves(keep, send, first, value):
    value = value.astype(bf16)
    half = value.shape[0] // 2
    keep[:, first : first + value.shape[1]] = value[:half]
    send[:, first : first + value.shape[1]] = value[half:]


def store_parts(keep, send, first, value):
    cut, part = column_cut(keep.shape[1])
    bit = lax.axis_index("seq") % 2
    value = value.astype(bf16)
    half = value.shape[0] // 2
    ahead = min(max(cut - first, 0), value.shape[1])
    if ahead:
        keep[:, first : first + ahead] = value[:half, :ahead]
        send[:, first : first + ahead] = value[half:, :ahead]
    for c in range(ahead, value.shape[1], TILE):
        which, offset = divmod(first + c - cut, part)
        place = cut + jnp.bitwise_xor(which, bit) * part + offset
        cols = pl.ds(pl.multiple_of(place, TILE), TILE)
        keep[:, cols] = value[:half, c : c + TILE]
        send[:, cols] = value[half:, c : c + TILE]


def exchange(value, axis, bit):
    count = lax.axis_size(axis)
    return lax.ppermute(value, axis, [(i, i ^ bit) for i in range(count)])


def project_kernel(*refs):
    sources, outs, held, arrived = refs[:9], refs[9:20], refs[20:29], refs[29]
    q_out, k_out, v_out, pk_out, pk_rev_out, pq_rev_out, order_out = outs[:7]
    x_turned, rel_turned, w_pk_ordered, w_pq_ordered = outs[7:]
    places, x, w_query, w_key, w_value, rel, w_pos_key, w_pos_query, biases = held
    copies = [
        pltpu.make_async_copy(source, target, arrived.at[i])
        for i, (source, target) in enumerate(zip(sources, held))
    ]
    for copy in copies:
        copy.start()

    def split(out, value):
        for p in range(PAIRS):
            out[p] = value[:, p * TILE : (p + 1) * TILE].astype(bf16)

    width = order_out.shape[0]
    copies[0].wait()
    shard = jnp.bitwise_xor(places[:, 0:1], lax.axis_index("rows"))
    target = shard * places[0, 2] + places[:, 1:2]
    order_out[...] = jnp.where(iota((width, width), 1) == target, 1.0, 0.0).astype(bf16)
    for copy in copies[1:]:
        copy.wait()
    bias = biases[...].astype(f32)
    split(q_out, nn(x[...], w_query[...]) + bias[0:1])
    split(k_out, nn(x[...], w_key[...]))
    split(v_out, nn(x[...], w_value[...]) + bias[1:2])
    count = rel.shape[0]
    pos_keys = nn(rel[...], w_pos_key[...]).astype(bf16)
    pos_queries = (nn(rel[...], w_pos_query[...]) + bias[2:3]).astype(bf16)
    row, col = iota((count, count), 0), iota((count, count), 1)
    flip = jnp.where(col == count - 1 - row, 1.0, 0.0).astype(bf16)
    pick = jnp.where(col == jnp.minimum(count - row, count - 1), 1.0, 0.0).astype(bf16)
    split(pk_out, pos_keys)
    split(pk_rev_out, nn(flip, pos_keys))
    split(pq_rev_out, nn(pick, pos_queries))
    x_turned[...] = nt(order_out[...], x[...]).astype(bf16)
    rel_turned[...] = nt(order_out[...], rel[...]).astype(bf16)
    w_pk_ordered[...] = nn(order_out[...], w_pos_key[...]).astype(bf16)
    w_pq_ordered[...] = nn(order_out[...], w_pos_query[...]).astype(bf16)


def key_block_range(wb, blocks, tiles):
    low, high = max(0, blocks - 1 - wb), min(blocks - 1, tiles + blocks - 2 - wb)
    return low, high, max(low - 1, 0), min(high, blocks - 2)


def attend_kernel(q, k_own, v_own, pk_rev, pq_rev, w_key, w_value, biases, *refs, scale, n_seq):
    edges, (context, probs, k, v, from_scr, score_scr) = refs[:-6], refs[-6:]
    me_seq = lax.axis_index("seq")
    span, block = edges[0].shape[0], k_own.shape[1]
    row, lane = iota((TILE, TILE), 0), iota((TILE, TILE), 1)
    eye = jnp.where(row == lane, 1.0, 0.0).astype(bf16)
    halves = (lane < TILE // 2, lane >= TILE // 2)
    tiles = q.shape[1] // TILE
    blocks = pk_rev.shape[1] // TILE + 1
    side = blocks // 2
    bias = biases[1:2, :].astype(f32)
    sides = ((0, span + block),) if len(edges) == 1 else ((0,), (span + block,))
    for firsts, source in zip(sides, edges):
        new_keys = nn(source[...], w_key[...]).astype(bf16)
        new_values = (nn(source[...], w_value[...]) + bias).astype(bf16)
        for p in range(PAIRS):
            for first in firsts:
                k[p, first : first + span, :] = new_keys[:, p * TILE : (p + 1) * TILE]
                v[p, first : first + span, :] = new_values[:, p * TILE : (p + 1) * TILE]
    for p in range(PAIRS):
        k[p, span : span + block, :] = k_own[p]
        v[p, span : span + block, :] = v_own[p]

    def masked_tables(p):
        table = pq_rev[p].astype(f32)
        half = iota((table.shape[0], TILE), 1) // (TILE // 2)
        return [jnp.where(half == h, table, 0.0).astype(bf16) for h in range(2)]

    def from_terms(p, slot, tables, wb):
        low, high, first, last = key_block_range(wb, blocks, tiles)
        kb = k[p, wb * TILE : (wb + 1) * TILE, :]
        rows = slice(first * TILE, (last + 1) * TILE)
        product = nt(kb, jnp.concatenate([tables[0][rows], tables[1][rows]], axis=0))
        for h in range(2):
            turned = {}
            for a in range(first, last + 1):
                at = (h * (last + 1 - first) + a - first) * TILE
                turned[a] = skew(product[:, at : at + TILE], 0)
            for e in range(low, high + 1):
                if e == 0:
                    term = turned[0]
                elif e == blocks - 1:
                    term = turned[blocks - 2]
                else:
                    term = jnp.where(lane >= row, turned[e], turned[e - 1])
                it, b = wb - (blocks - 1) + e, blocks - 1 - e
                from_scr[slot, h, it, b * TILE : (b + 1) * TILE, :] = term.astype(bf16)

    before = jnp.where(me_seq == 0, masked_score, 0.0)
    after = jnp.where(me_seq == n_seq - 1, masked_score, 0.0)
    rate = scale * math.log2(math.e)
    keys = tiles + blocks - 1
    tables = masked_tables(0)
    for wb in range(keys):
        from_terms(0, 0, tables, wb)

    def one_pair(p, carry):
        attend_pair(p, p % 2)
        return carry

    def attend_pair(p, slot):
        cols = pl.ds(pl.multiple_of(p * TILE, TILE), TILE)
        following = jnp.minimum(p + 1, PAIRS - 1)
        tables = masked_tables(following)
        chains = [(it, h) for it in range(tiles) for h in range(2)]
        stacked = jnp.concatenate(
            [where_bf16(halves[h], q[p, it * TILE : (it + 1) * TILE, :]) for it, h in chains], axis=0
        )
        product = nt(stacked, pk_rev[p])
        tops = []
        for n, (it, h) in enumerate(chains):
            rows = slice(n * TILE, (n + 1) * TILE)
            turned = [
                skew(product[rows, b * TILE : (b + 1) * TILE], 1) for b in range(blocks - 1)
            ]
            left = jnp.concatenate([stacked[rows], eye], axis=1)
            right = jnp.concatenate(
                [k[p, it * TILE : (it + blocks) * TILE, :], from_scr[slot, h, it]], axis=1
            )
            content = nt(left, right)
            largest = None
            for b in range(blocks):
                score = content[:, b * TILE : (b + 1) * TILE]
                if b == 0:
                    score = jnp.where(lane > row, score + turned[0], masked_score)
                elif b == blocks - 1:
                    score = jnp.where(lane <= row, score + turned[b - 1], masked_score)
                else:
                    score = score + jnp.where(lane > row, turned[b], turned[b - 1])
                if it + b < side:
                    score = score + before
                if it + b >= side + tiles:
                    score = score + after
                score_scr[n, :, b * TILE : (b + 1) * TILE] = score
                largest = score if largest is None else jnp.maximum(largest, score)
            tops.append(largest)
        tops = [jnp.max(top, axis=1, keepdims=True) for top in tops]
        totals = []
        for n in range(len(chains)):
            weight = jnp.exp2((score_scr[n] - tops[n]) * rate)
            score_scr[n] = weight
            total = weight[:, :TILE]
            for b in range(1, blocks):
                total = total + weight[:, b * TILE : (b + 1) * TILE]
            totals.append(total)
            for wb in range(n * keys // len(chains), (n + 1) * keys // len(chains)):
                from_terms(following, 1 - slot, tables, wb)
        inverses = [1.0 / jnp.sum(total, axis=1, keepdims=True) for total in totals]
        for n, (it, h) in enumerate(chains):
            probs[p, h, it] = (score_scr[n] * inverses[n]).astype(bf16)
        for it in range(tiles):
            both = jnp.concatenate([probs[p, 0, it], probs[p, 1, it]], axis=0)
            part = nn(both, v[p, it * TILE : (it + blocks) * TILE, :])
            context[it * TILE : (it + 1) * TILE, cols] = jnp.where(
                halves[0], part[:TILE], part[TILE:]
            ).astype(bf16)

    lax.fori_loop(0, PAIRS, one_pair, 0)


def attend_back_kernel(
    q,
    k,
    v,
    pk,
    pq_rev,
    d_context,
    context,
    probs,
    dq_out,
    dk_out,
    dv_out,
    dpk_out,
    dpq_out,
    ds_scr,
    merged_scr,
    band_scr,
    turn_scr,
    shifted_scr,
    dv_scr,
    dk_scr,
    *,
    scale,
    p,
):
    row, lane = iota((TILE, TILE), 0), iota((TILE, TILE), 1)
    flip = jnp.where(row + lane == TILE - 1, 1.0, 0.0).astype(bf16)
    row2, lane2 = iota((2 * TILE, 2 * TILE), 0), iota((2 * TILE, 2 * TILE), 1)
    same = (row2 // TILE) == (lane2 // TILE)
    flip2 = jnp.where(
        same & (row2 % TILE + lane2 % TILE == TILE - 1), 1.0, 0.0
    ).astype(bf16)
    halves = (lane < TILE // 2, lane >= TILE // 2)
    row_halves = (row < TILE // 2, row >= TILE // 2)
    cols = slice(p * TILE, (p + 1) * TILE)
    tiles = q.shape[1] // TILE
    blocks = pk.shape[1] // TILE + 1
    keys = tiles + blocks - 1
    pairs = (blocks - 1) // 2

    def part(index):
        return slice(index * TILE, (index + 1) * TILE)

    def window(it):
        return slice(it * TILE, (it + blocks) * TILE)

    def split_rows(value):
        return jnp.concatenate([where_bf16(halves[h], value) for h in range(2)], axis=0)

    def split_turned(value):
        flat = value.astype(f32).T
        return [jnp.where(row_halves[h], flat, 0.0).astype(bf16) for h in range(2)]

    for it in range(tiles):
        dct = d_context[part(it), cols]
        overlap = dct.astype(f32) * context[part(it), cols].astype(f32)
        delta = jnp.concatenate(
            [
                jnp.sum(jnp.where(halves[h], overlap, 0.0), axis=1, keepdims=True)
                for h in range(2)
            ],
            axis=0,
        )
        d_probs = nt(split_rows(dct), v[p, window(it), :])
        weights = jnp.concatenate([probs[p, 0, it], probs[p, 1, it]], axis=0)
        ds = weights.astype(f32) * (d_probs - delta) * scale
        ds_scr[it] = ds.astype(bf16)
        for h in range(2):
            for b in range(blocks - 1):
                merged = jnp.where(lane > row, ds[part(h), part(b)], ds[part(h), part(b + 1)])
                at = (it * 2 + h) * pairs + b // 2
                merged_scr[part(at), part(b % 2)] = merged.astype(bf16)
    flipped = nn(merged_scr[...], flip2)
    for it in range(tiles):
        for h in range(2):
            for b in range(blocks - 1):
                at = (it * 2 + h) * pairs + b // 2
                band_scr[part(it * 2 + h), part(blocks - 2 - b)] = skew(
                    flipped[part(at), part(b % 2)], 1
                ).astype(bf16)
    for it in range(tiles):
        for b in range(blocks):
            turn_scr[it, b] = nt(flip, ds_scr[it, :, part(b)]).astype(bf16)
    reverse = nn(flip, jnp.concatenate([k[p, part(wb), :] for wb in range(keys)], axis=1))
    reverse_t = [reverse[:, part(wb)].T for wb in range(keys)]
    for it in range(tiles):
        left = jnp.concatenate([reverse_t[it + b].astype(bf16) for b in range(blocks)], axis=1)
        direct = nn(left, jnp.concatenate([turn_scr[it, b] for b in range(blocks)], axis=0))
        direct = jnp.where(row_halves[0], direct[:, :TILE], direct[:, TILE:]).T
        total = nn(band_scr[2 * it * TILE : 2 * (it + 1) * TILE, :], pk[p])
        total = jnp.where(halves[0], total[:TILE], total[TILE:])
        dq_out[part(it), :] = (direct + total).astype(bf16)
    turned = [split_turned(q[p, part(it), :]) for it in range(tiles)]
    dpk_out[...] = nn(jnp.concatenate(sum(turned, []), axis=1), band_scr[...]).astype(bf16)
    dv_scr[...] = jnp.zeros_like(dv_scr)
    dk_scr[...] = jnp.zeros_like(dk_scr)
    for it in range(tiles):
        dk_scr[:, window(it)] += nn(jnp.concatenate(turned[it], axis=1), ds_scr[it])
        dv_scr[:, window(it)] += nn(
            jnp.concatenate(split_turned(d_context[part(it), cols]), axis=1),
            jnp.concatenate([probs[p, 0, it], probs[p, 1, it]], axis=0),
        )

    tables = []
    for h in range(2):
        table = pq_rev[p].astype(f32)
        half = iota((table.shape[0], TILE), 1) // (TILE // 2) == h
        tables.append(jnp.where(half, table, 0.0).astype(bf16))
    for wb in range(keys):
        low, high, first, last = key_block_range(wb, blocks, tiles)

        def source(e, h):
            if e < low or e > high:
                return jnp.zeros((TILE, TILE), f32)
            it, b = wb - (blocks - 1) + e, blocks - 1 - e
            return turn_scr[it, b, :, part(h)].astype(f32)

        for h in range(2):
            for a in range(blocks - 1):
                if first <= a <= last:
                    merged = jnp.where(lane + row >= TILE - 1, source(a, h), source(a + 1, h))
                    shifted_scr[part(2 * wb + h), part(a)] = skew(merged, 1).astype(bf16)
                else:
                    shifted_scr[part(2 * wb + h), part(a)] = jnp.zeros((TILE, TILE), bf16)
    lows = []
    for wb in range(keys):
        low, high, first, last = key_block_range(wb, blocks, tiles)
        left, right = [], []
        span = slice(first * TILE, (last + 1) * TILE)
        for h in range(2):
            left.append(shifted_scr[part(2 * wb + h), span])
            right.append(tables[h][span])
        total = nn(jnp.concatenate(left, axis=1), jnp.concatenate(right, axis=0))
        lows.append(total.astype(bf16))
    natural = nn(flip, jnp.concatenate(lows, axis=1))
    for wb in range(keys):
        direct = dk_scr[:, part(wb)].T
        dk_out[part(wb), :] = (natural[:, part(wb)] + direct).astype(bf16)
    turned = [
        jnp.where(row_halves[h], reverse_t[wb], 0.0).astype(bf16)
        for wb in range(keys)
        for h in range(2)
    ]
    dpq_out[...] = nn(jnp.concatenate(turned, axis=1), shifted_scr[...]).astype(bf16)
    for wb in range(keys):
        dv_out[part(wb), :] = dv_scr[:, part(wb)].T.astype(bf16)


def norm_parts(value):
    centre = value - jnp.mean(value, axis=1, keepdims=True)
    rate = lax.rsqrt(jnp.mean(centre * centre, axis=1, keepdims=True) + norm_eps)
    return centre * rate, rate


def norm_back(cotangent, normal, rate):
    return rate * (
        cotangent
        - jnp.mean(cotangent, axis=1, keepdims=True)
        - normal * jnp.mean(cotangent * normal, axis=1, keepdims=True)
    )


def middle_kernel(
    x,
    context,
    grad_out,
    mask,
    w_output,
    biases,
    gains,
    shifts,
    w_inner,
    inner_bias,
    w_outer,
    outer_bias,
    order,
    result,
    d_first_out,
    d_context,
    keep,
    send,
    inner_out,
    rows_out,
    low_scr,
    active_scr,
    d_inner_scr,
    d_outer_scr,
    d_att_scr,
    *,
    step,
):
    tokens, width = x.shape
    units = w_inner.shape[1]
    bias = biases[3:4, :].astype(f32)
    gain_one, gain_two = gains[0:1, :].astype(f32), gains[1:2, :].astype(f32)
    shift_one, shift_two = shifts[0:1, :].astype(f32), shifts[1:2, :].astype(f32)
    in_bias = inner_bias[...].astype(f32).reshape(1, units)
    out_bias = outer_bias[...].astype(f32).reshape(1, width)
    diagonal = iota((TILE, TILE), 0) == iota((TILE, TILE), 1)
    sums = [jnp.zeros((1, width), f32) for _ in range(6)]

    def add(index, value):
        sums[index] = sums[index] + jnp.sum(value, axis=0, keepdims=True)

    parts = [slice(first, first + step) for first in range(0, tokens, step)]
    first_norm, slopes, second = [], [], []
    for rows in parts:
        attended = nn(context[rows, :], w_output[...]) + bias
        n_one, r_one = norm_parts(x[rows, :].astype(f32) + attended)
        normed = n_one * gain_one + shift_one
        low_scr[rows, :] = normed.astype(bf16)
        first_norm.append((n_one, r_one, normed))
    for rows in parts:
        inner = nn(low_scr[rows, :], w_inner[...]) + in_bias
        cumulative = 0.5 + 0.5 * lax.erf(inner * math.sqrt(0.5))
        active_scr[rows, :] = (inner * cumulative).astype(bf16)
        slopes.append(
            cumulative + inner * jnp.exp(-0.5 * inner * inner) * (1.0 / math.sqrt(2 * math.pi))
        )
    for rows, (_, _, normed) in zip(parts, first_norm):
        outer = nn(active_scr[rows, :], w_outer[...]) + out_bias
        n_two, r_two = norm_parts(normed + outer)
        result[rows, :] = (n_two * gain_two + shift_two).astype(bf16)
        columns = []
        for part in range(rows.start, rows.stop, TILE):
            line = mask[0:1, part : part + TILE].astype(f32)
            columns.append(jnp.sum(jnp.where(diagonal, line, 0.0), axis=1, keepdims=True))
        cotangent = grad_out[rows, :].astype(f32) * jnp.concatenate(columns, axis=0)
        add(0, cotangent * n_two)
        add(1, cotangent)
        d_second = norm_back(cotangent * gain_two, n_two, r_two)
        d_outer = d_second.astype(bf16)
        d_outer_scr[rows, :] = d_outer
        add(2, d_outer.astype(f32))
        second.append(d_second)
    for rows, slope in zip(parts, slopes):
        d_inner_scr[rows, :] = (nt(d_outer_scr[rows, :], w_outer[...]) * slope).astype(bf16)
    for rows, d_second, (n_one, r_one, _) in zip(parts, second, first_norm):
        d_normed = d_second + nt(d_inner_scr[rows, :], w_inner[...])
        add(3, d_normed * n_one)
        add(4, d_normed)
        d_first = norm_back(d_normed * gain_one, n_one, r_one)
        d_first_out[rows, :] = d_first
        d_att = d_first.astype(bf16)
        d_att_scr[rows, :] = d_att
        add(5, d_att.astype(f32))
    for rows in parts:
        d_context[rows, :] = nt(d_att_scr[rows, :], w_output[...]).astype(bf16)

    def put(first, left, right):
        turned = nt(order[...], left).astype(bf16)
        for c in range(0, right.shape[1], width):
            store_halves(keep, send, first + c, nn(turned, right[:, c : c + width]))

    put(0, low_scr[...], d_inner_scr)
    put(units, d_outer_scr[...], active_scr)
    inner_out[...] = nn(jnp.ones((8, tokens), bf16), d_inner_scr[...])
    zero = jnp.zeros((1, width), f32)
    table = [zero, zero, zero, sums[5], sums[3], sums[0], sums[4], sums[1], sums[2]]
    rows_out[...] = jnp.concatenate(table + [zero] * (16 - len(table)), axis=0)


def weight_grad_kernel(
    x_t, rel_t, w_pk_t, w_pq_t, order, rows, context, d_first, inner, *refs, n_seq, share
):
    edges = refs[: 1 if n_seq == 2 else 2]
    backs, (keep, send) = refs[len(edges) : -2], refs[-2:]
    width, block = x_t.shape
    count = rel_t.shape[1]
    span = count // 2
    put = partial(store_parts, keep, send)

    def joined(index, rows=slice(None), axis=1):
        some = backs[PAIRS * index : PAIRS * (index + 1)]
        return jnp.concatenate([ref[rows, :] for ref in some], axis=axis)

    ord_ = order[...]
    dq = joined(0)
    put(0, nn(x_t[...], dq))
    turned = [nt(ord_, edge[...]).astype(bf16) for edge in edges] + [x_t[...]]
    if n_seq == 2:
        first = pl.multiple_of((1 - lax.axis_index("seq")) * (span + block), TILE)
        places = [pl.ds(first, span)]
    else:
        places = [slice(0, span), slice(span + block, 2 * span + block)]
    places.append(slice(span, span + block))
    left = jnp.concatenate(turned, axis=1)
    dk, dv = (jnp.concatenate([joined(i, r) for r in places], axis=0) for i in (1, 2))
    put(width, nn(left, dk))
    put(2 * width, nn(left, dv))
    context_t = nt(ord_, context[...]).astype(bf16)
    put(5 * width, nn(context_t, d_first[...].astype(bf16)))
    dpk, dpq = joined(3, axis=0), joined(4, axis=0)
    put(3 * width, nt(rel_t[...], dpk))
    row, col = iota((count, count), 0), iota((count, count), 1)
    pick = jnp.where(col == jnp.minimum(count - row, count - 1), 1.0, 0.0).astype(bf16)
    dpq_nat = nn(dpq, pick).astype(bf16)
    put(4 * width, nt(rel_t[...], dpq_nat))
    rel_grad = nn(w_pk_t[...], dpk)
    rel_grad = rel_grad + nn(w_pq_t[...], dpq_nat)
    put(6 * width, rel_grad)
    known = rows[...]
    sum_q = nn(jnp.ones((8, block), bf16), dq)[0:1]
    sum_v = nn(jnp.ones((8, dv.shape[0]), bf16), dv)[0:1]
    sum_p = nt(jnp.ones((8, count), bf16), dpq_nat)[0:1]
    place = iota(known.shape, 0)
    known = jnp.where(place == 0, sum_q, known)
    known = jnp.where(place == 1, sum_v, known)
    known = jnp.where(place == 2, sum_p, known)
    padded = jnp.concatenate([known, jnp.zeros((TILE - known.shape[0], width), f32)], axis=0)
    block = nt(ord_, padded.astype(bf16))
    lines = [inner[0:1, c : c + TILE] for c in range(0, inner.shape[1], TILE)]
    some = len(lines)
    lines = jnp.concatenate(lines + [jnp.zeros((-some % 8, TILE), f32)] * (some % 8 > 0), axis=0)
    if compact_bias(share, inner.shape[1]):
        turned = pltpu.roll(lines, TILE // 2, 1)
        picked = [t[j : j + 1] for j in range(some) for t in (turned, lines)]
        picked += [jnp.zeros((share - 2 * some, TILE), f32)] * (share > 2 * some)
        lines = jnp.concatenate(picked, axis=0)
        lines = jnp.where(iota(lines.shape, 1) >= TILE // 2, lines, 0.0)
        put(6 * width + count, block + jnp.concatenate([lines] * (width // share), axis=0))
    else:
        put(6 * width + count, block)
        lines = [lines[:some]] + [jnp.zeros((share - some, TILE), f32)] * (share > some)
        put(6 * width + count + TILE, jnp.concatenate(lines * (width // share), axis=0))


def input_grad_kernel(
    dq0, dq1, dq2, dk0, dk1, dk2, dv0, dv1, dv2, d_first, w_query, w_key, w_value, own, *outs
):
    span = outs[0].shape[0]
    block = own.shape[0]

    def joined(refs, rows):
        return jnp.concatenate([ref[rows, :] for ref in refs], axis=1)

    def halo(rows):
        return nt(joined((dk0, dk1, dk2), rows), w_key[...]) + nt(
            joined((dv0, dv1, dv2), rows), w_value[...]
        )

    if len(outs) == 1:
        first = pl.multiple_of((1 - lax.axis_index("seq")) * (span + block), TILE)
        outs[0][...] = halo(pl.ds(first, span)).astype(bf16)
    else:
        outs[0][...] = halo(slice(0, span)).astype(bf16)
        outs[1][...] = halo(slice(span + block, 2 * span + block)).astype(bf16)
    dq = jnp.concatenate([dq0[...], dq1[...], dq2[...]], axis=1)
    own[...] = halo(slice(span, span + block)) + d_first[...] + nt(dq, w_query[...])


def compact_bias(share, units):
    return 2 * units // TILE <= share


def final_kernel(*refs, width, units, count):
    (g_q, g_k, g_v, g_o, g_rel, g_pk, g_pq, g_bias, g_gain, g_shift, g_in, g_out, g_ob, g_ib) = (
        refs[4:]
    )
    low = lax.axis_index("seq") % 2 == 0
    share = refs[0].shape[0]
    mid = refs[0][...].astype(f32) + refs[1][...].astype(f32)
    cut, _ = column_cut(6 * width + count + (1 if compact_bias(share, units) else 2) * TILE)
    mine, other = refs[2][...].astype(f32), refs[3][...].astype(f32)
    rest = jnp.concatenate(
        [
            mine[:, :cut] + other[:, :cut],
            jnp.where(low, mine[:, cut:], other[:, cut:]),
            jnp.where(low, other[:, cut:], mine[:, cut:]),
        ],
        axis=1,
    )
    g_in[...] = mid[:, :units]
    g_out[...] = mid[:, units : 2 * units]
    for i, out in enumerate((g_q, g_k, g_v, g_pk, g_pq, g_o)):
        out[...] = rest[:, i * width : (i + 1) * width]
    g_rel[...] = rest[:, 6 * width : 6 * width + count]
    block = rest[:, 6 * width + count : 6 * width + count + TILE]
    if compact_bias(share, units):
        turned = pltpu.roll(block, TILE // 2, 1)
        left = iota((1, TILE), 1) < TILE // 2
        g_ib[...] = jnp.concatenate(
            [
                jnp.where(left, turned[2 * j : 2 * j + 1], block[2 * j + 1 : 2 * j + 2])
                for j in range(units // TILE)
            ],
            axis=0,
        )
    else:
        g_ib[...] = rest[: units // TILE, 6 * width + count + TILE :]
    lines = block.T
    g_bias[...] = lines[0:4]
    g_gain[...] = lines[4:6]
    g_shift[...] = lines[6:8]
    g_ob[...] = lines[8:9]


def bit_reversed(value, bits):
    out = 0
    for _ in range(bits):
        out = out * 2 + value % 2
        value //= 2
    return out


def local(
    hidden,
    grad_out,
    grad_mask,
    w_query,
    w_key,
    w_value,
    w_output,
    rel_table,
    w_pos_key,
    w_pos_query,
    attn_biases,
    norm_gains,
    norm_shifts,
    w_inner,
    inner_bias,
    w_outer,
    outer_bias,
):
    count, block, width = hidden.shape
    tokens = count * block
    table = rel_table.shape[0]
    span = table // 2
    window = block + 2 * span
    units = w_inner.shape[1]
    head = width // HEADS
    scale = 1.0 / math.sqrt(3.0 * head)
    n_rows, n_seq = lax.axis_size("rows"), lax.axis_size("seq")
    row_bits, seq_bits = n_rows.bit_length() - 1, n_seq.bit_length() - 1
    share = width // n_rows
    tiles, blocks = block // TILE, table // TILE + 1
    me_seq = lax.axis_index("seq")
    x = hidden.reshape(tokens, width)
    shape = jax.ShapeDtypeStruct

    forward = [(i, i + 1) for i in range(n_seq - 1)]
    backward = [(i + 1, i) for i in range(n_seq - 1)]
    if n_seq == 2:
        start = (1 - me_seq) * (block - span)
        x_low = exchange(lax.dynamic_slice_in_dim(x, start, span, axis=0), "seq", 1)
        x_high = x_low
    else:
        x_low = lax.ppermute(x[block - span :], "seq", forward)
        x_high = lax.ppermute(x[:span], "seq", backward)

    outside = (x_low,) if n_seq == 2 else (x_low, x_high)
    places = np.zeros((width, 4), np.int32)
    for i in range(width):
        places[i] = (bit_reversed(i // share, row_bits), i % share, share, 0)

    loaded = (
        jnp.asarray(places),
        x,
        w_query,
        w_key,
        w_value,
        rel_table,
        w_pos_key,
        w_pos_query,
        attn_biases,
    )
    q3, k3, v3, pk3, pk_rev3, pq_rev3, order, x_t, rel_t, w_pk_t, w_pq_t = pl.pallas_call(
        project_kernel,
        out_shape=(
            shape((PAIRS, block, TILE), bf16),
            shape((PAIRS, block, TILE), bf16),
            shape((PAIRS, block, TILE), bf16),
            shape((PAIRS, table, TILE), bf16),
            shape((PAIRS, table, TILE), bf16),
            shape((PAIRS, table, TILE), bf16),
            shape((width, width), bf16),
            shape((width, tokens), bf16),
            shape((width, table), bf16),
            shape((width, width), bf16),
            shape((width, width), bf16),
        ),
        in_specs=[pl.BlockSpec(memory_space=pltpu.HBM)] * len(loaded),
        scratch_shapes=[pltpu.VMEM(a.shape, a.dtype) for a in loaded]
        + [pltpu.SemaphoreType.DMA((len(loaded),))],
        compiler_params=pltpu.CompilerParams(vmem_limit_bytes=12 * MiB),
        name="project",
    )(*(pltpu.with_memory_space_constraint(a, pltpu.HBM) for a in loaded))
    probs_shape = (PAIRS, 2, tiles, TILE, blocks * TILE)
    context, probs, k3, v3 = pl.pallas_call(
        partial(attend_kernel, scale=scale, n_seq=n_seq),
        out_shape=(
            shape((tokens, width), bf16),
            shape(probs_shape, bf16),
            shape((PAIRS, window, TILE), bf16),
            shape((PAIRS, window, TILE), bf16),
        ),
        scratch_shapes=[
            pltpu.VMEM((2, 2, tiles, blocks * TILE, TILE), bf16),
            pltpu.VMEM((2 * tiles, TILE, blocks * TILE), f32),
        ],
        compiler_params=pltpu.CompilerParams(vmem_limit_bytes=20 * MiB),
        name="attend",
    )(q3, k3, v3, pk_rev3, pq_rev3, w_key, w_value, attn_biases, *outside)

    mid_cols = 2 * units
    result, d_first, d_context, mid_keep, mid_send, inner_sum, rows = pl.pallas_call(
        partial(middle_kernel, step=512),
        out_shape=(
            shape((tokens, width), bf16),
            shape((tokens, width), f32),
            shape((tokens, width), bf16),
            shape((width // 2, mid_cols), bf16),
            shape((width // 2, mid_cols), bf16),
            shape((8, units), f32),
            shape((16, width), f32),
        ),
        scratch_shapes=[
            pltpu.VMEM((tokens, width), bf16),
            pltpu.VMEM((tokens, units), bf16),
            pltpu.VMEM((tokens, units), bf16),
            pltpu.VMEM((tokens, width), bf16),
            pltpu.VMEM((tokens, width), bf16),
        ],
        compiler_params=pltpu.CompilerParams(vmem_limit_bytes=22 * MiB),
        name="middle",
    )(
        x,
        context,
        grad_out.reshape(tokens, width),
        grad_mask,
        w_output,
        attn_biases,
        norm_gains,
        norm_shifts,
        w_inner,
        inner_bias,
        w_outer,
        outer_bias,
        order,
    )

    def back(p, d_context):
        return pl.pallas_call(
            partial(attend_back_kernel, scale=scale, p=p),
            out_shape=(
                shape((block, TILE), bf16),
                shape((window, TILE), bf16),
                shape((window, TILE), bf16),
                shape((TILE, table), bf16),
                shape((TILE, table), bf16),
            ),
            scratch_shapes=[
                pltpu.VMEM((tiles, 2 * TILE, blocks * TILE), bf16),
                pltpu.VMEM((tiles * (blocks - 1) * TILE, 2 * TILE), bf16),
                pltpu.VMEM((2 * tiles * TILE, table), bf16),
                pltpu.VMEM((tiles, blocks, TILE, 2 * TILE), bf16),
                pltpu.VMEM((2 * window, table), bf16),
                pltpu.VMEM((TILE, window), f32),
                pltpu.VMEM((TILE, window), f32),
            ],
            compiler_params=pltpu.CompilerParams(vmem_limit_bytes=20 * MiB),
            cost_estimate=pl.CostEstimate(
                flops=1000, bytes_accessed=1000, transcendentals=0
            ),
            name="attend_back",
        )(q3, k3, v3, pk3, pq_rev3, d_context, context, probs)

    def tied(first, second):
        return lax.optimization_barrier((first, second))

    def halves(total):
        return total[: total.shape[0] // 2], total[total.shape[0] // 2 :]

    def row_begin(total, step):
        keep, send = halves(total)
        return keep, exchange(send, "rows", 1 << step)

    def row_step(total, step):
        keep, received = row_begin(total, step)
        return keep + received

    def seq_step(total, step):
        return total + exchange(total, "seq", 1 << step)

    def opened(total):
        cut, part = column_cut(total.shape[1])
        one = row_step(total[:, :cut], 1)
        two = total[:, cut : cut + part] + exchange(total[:, cut + part :], "seq", 1)
        return one, two

    def finished(one, two):
        for step in range(2, row_bits - 1):
            one = row_step(one, step)
        for step in range(2, row_bits - 1):
            two = row_step(two, step)
        both = row_step(jnp.concatenate([one, two], axis=1), row_bits - 1)
        for step in range(1, seq_bits):
            both = seq_step(both, step)
        return both, exchange(both, "seq", 1)

    received = exchange(mid_send, "rows", 1)
    back0 = back(0, d_context)
    mid_keep, dq0 = tied(mid_keep, back0[0])
    mid = mid_keep + received
    mid, d_context = tied(mid, d_context)
    keep, send = halves(mid)
    back1 = back(1, d_context)
    received = exchange(send, "rows", 2)
    back2 = back(2, d_context)
    dq1, dq2 = back1[0], back2[0]
    mid = keep + received
    dq = (dq0, dq1, dq2)
    dk, dv, dpk, dpq = ((back0[i], back1[i], back2[i]) for i in range(1, 5))

    rest_cols = 6 * width + table + (1 if compact_bias(share, units) else 2) * TILE
    rest_keep, rest_send = pl.pallas_call(
        partial(weight_grad_kernel, n_seq=n_seq, share=share),
        out_shape=(
            shape((width // 2, rest_cols), bf16),
            shape((width // 2, rest_cols), bf16),
        ),
        compiler_params=pltpu.CompilerParams(vmem_limit_bytes=20 * MiB),
        cost_estimate=pl.CostEstimate(flops=1000, bytes_accessed=1000, transcendentals=0),
        name="weight_grad",
    )(x_t, rel_t, w_pk_t, w_pq_t, order, rows, context, d_first, inner_sum, *outside, *dq, *dk, *dv, *dpk, *dpq)

    rest_send, d_first = tied(rest_send, d_first)
    edge = shape((span, width), bf16)
    loaded = (d_first, w_query, w_key, w_value)
    own, *edges = pl.pallas_call(
        input_grad_kernel,
        out_shape=(shape((tokens, width), f32),) + (edge,) * (1 if n_seq == 2 else 2),
        compiler_params=pltpu.CompilerParams(vmem_limit_bytes=12 * MiB),
        cost_estimate=pl.CostEstimate(flops=1000, bytes_accessed=1000, transcendentals=0),
        name="input_grad",
    )(*dq, *dk, *dv, *(pltpu.with_memory_space_constraint(a, pltpu.HBM) for a in loaded))
    rest_keep, own = tied(rest_keep, own)
    rest = rest_keep + exchange(rest_send, "rows", 1)
    rest, mid = tied(rest, mid)
    rest_one, rest_two = opened(rest)
    rest_two = row_step(rest_two, 1)
    rest_two, edges = tied(rest_two, edges)
    nothing = jnp.zeros((block - span, width), f32)
    if n_seq == 2:
        arrived = exchange(edges[0], "seq", 1).astype(f32)
        own = own + jnp.where(
            me_seq == 0,
            jnp.concatenate([nothing, arrived], axis=0),
            jnp.concatenate([arrived, nothing], axis=0),
        )
    else:
        from_next = lax.ppermute(edges[0], "seq", backward).astype(f32)
        from_prev = lax.ppermute(edges[1], "seq", forward).astype(f32)
        own = (
            own
            + jnp.concatenate([nothing, from_next], axis=0)
            + jnp.concatenate([from_prev, nothing], axis=0)
        )
    grad_hidden = own.astype(bf16)

    rest = finished(rest_one, rest_two)
    for step in range(2, row_bits):
        mid = row_step(mid, step)
    for step in range(seq_bits - 1):
        mid = seq_step(mid, step)
    mid = (mid, exchange(mid, "seq", 1 << (seq_bits - 1)))

    square = shape((share, width), f32)
    grads = pl.pallas_call(
        partial(final_kernel, width=width, units=units, count=table),
        out_shape=(
            square,
            square,
            square,
            square,
            shape((share, table), f32),
            square,
            square,
            shape((4, share), f32),
            shape((2, share), f32),
            shape((2, share), f32),
            shape((share, units), f32),
            shape((share, units), f32),
            shape((1, share), f32),
            shape((units // TILE, TILE), f32),
        ),
        compiler_params=pltpu.CompilerParams(vmem_limit_bytes=12 * MiB),
        name="final",
    )(*mid, *rest)
    return (
        result.reshape(count, block, width),
        grad_hidden.reshape(count, block, width),
        *grads[:4],
        grads[4].T,
        *grads[5:11],
        grads[13].reshape(units),
        grads[11].T,
        grads[12].reshape(share),
    )


def solution(mesh):
    in_specs = (
        P("rows", "seq", None),
        P("rows", "seq", None),
        P("rows", "seq"),
    ) + (P(),) * 14
    out_specs = (
        P("rows", "seq", None),
        P("rows", "seq", None),
        P("rows", None),
        P("rows", None),
        P("rows", None),
        P("rows", None),
        P(None, "rows"),
        P("rows", None),
        P("rows", None),
        P(None, "rows"),
        P(None, "rows"),
        P(None, "rows"),
        P("rows", None),
        P(),
        P(None, "rows"),
        P("rows"),
    )
    return jax.shard_map(local, mesh=mesh, in_specs=in_specs, out_specs=out_specs, check_vma=False)
```
